128 devices in a mesh: gx: 8 (over z_hi, y), gy: 4 (over z_lo, core), dev: 4 (over x).
Axes of the slice: x: 4, y: 4, z: 4 (z_hi: 2, z_lo: 2; z = z_hi * 2 + z_lo), core: 2. Of those that a mesh axis runs over, the one named last changes fastest.
Arguments:
- design: bfloat16 [512, 256, 1024], P('gx', ('gy', 'dev')), may hold values from 0 to 1
- tap_offsets: int32 [16, 3], replicated, may hold values from 0 to 1
- tap_weights: float32 [16], replicated, may hold values from 0.2 to 2
- input_load: float32 [256, 128, 512], P('gx', 'gy', 'dev'), may hold values from -6 to 6
- input_mask: int32 [256, 128, 512], P('gx', 'gy', 'dev'), may hold values 0 or 1
- output_mask: int32 [256, 128, 512], P('gx', 'gy', 'dev'), may hold values 0 or 1
- fixed_mask: int32 [256, 128, 512], P('gx', 'gy', 'dev'), may hold values 0 or 1
Outputs:
- grad_design: float32 [512, 256, 1024], P('gx', ('gy', 'dev'))
The draws below stay inside these ranges and needn't reach their ends.
All inputs are finite; a program needn't handle non-finite values. No bound on the sum of `input_mask` or of `output_mask` or of `fixed_mask` on one device may be relied on, other than what follows from the above.
Results may differ from the reference program's by a relative error of at most 0.0044.
Values may be sent and summed in bfloat16 or wider, within the bound.
A program may use at most 64 MiB of HBM per device.

```python
import math
import jax
import jax.numpy as jnp

ITERS = 2
TAPS = 16
NX = 256
NY = 128
NZ = 512


def touch_ends(drawn, stream_key, least, high):
    dims = drawn.shape
    place = [jax.random.randint(jax.random.fold_in(stream_key, axis), (), 0, dims[axis]) for axis in range(len(dims))]
    drawn = drawn.at[tuple(place)].set(least)
    longest = dims.index(max(dims))
    place[longest] = (place[longest] + 1) % dims[longest]
    return drawn.at[tuple(place)].set(high)


def block_scale(own_key, extent, shards, least, largest):
    level, own = 1.0, jax.random.fold_in(own_key, 6)
    for axis_at, blocks in shards:
        draws = jnp.exp(jax.random.uniform(jax.random.fold_in(own, axis_at), (blocks,), jnp.float32, least / len(shards), largest / len(shards)))
        level = level * jnp.repeat(draws, extent[axis_at] // blocks).reshape([-1 if axis == axis_at else 1 for axis in range(len(extent))])
    return level


def gaussian(stream_key, extent, scale, most, split=(), kind=jnp.bfloat16):
    level = block_scale(stream_key, extent, split, -0.22, 0.18) if split else 1.0
    values = jax.random.normal(stream_key, extent, jnp.float32) * scale * level
    return jnp.minimum(jnp.maximum(values, -most), most).astype(kind)


def setup_inputs(seed: int = 0) -> dict:
    key_list = jax.random.split(jax.random.key(seed), 8)
    design = jnp.clip(1.0 * jax.random.uniform(key_list[0], (2 * NX, 2 * NY, 2 * NZ), jnp.float32) ** block_scale(key_list[0], (2 * NX, 2 * NY, 2 * NZ), ((0, 8), (1, 16)), -0.2, 0.2), 0.0, 1.0).astype(jnp.bfloat16)
    tap_offsets = touch_ends(jax.random.randint(key_list[1], (TAPS, 3), 0, 2), jax.random.fold_in(key_list[1], 1), 0, 1).astype(jnp.int32)
    tap_weights = jnp.clip(jnp.exp(jax.random.uniform(key_list[2], (TAPS,), jnp.float32, math.log(0.2), math.log(2.0))), 0.2, 2.0)
    input_load = gaussian(key_list[3], (NX, NY, NZ), 1.0, 6.0, ((0, 8), (1, 4), (2, 4)), jnp.float32)
    input_mask = touch_ends((jax.random.randint(key_list[4], (NX, NY, NZ), 0, 4) < 1).astype(jnp.int32), jax.random.fold_in(key_list[4], 1), 0, 1)
    output_mask = touch_ends((jax.random.randint(key_list[5], (NX, NY, NZ), 0, 8) < 1).astype(jnp.int32), jax.random.fold_in(key_list[5], 1), 0, 1)
    fixed_mask = touch_ends((jax.random.randint(key_list[6], (NX, NY, NZ), 0, 16) < 1).astype(jnp.int32), jax.random.fold_in(key_list[6], 1), 0, 1)
    return dict(design=design, tap_offsets=tap_offsets, tap_weights=tap_weights, input_load=input_load, input_mask=input_mask, output_mask=output_mask, fixed_mask=fixed_mask)


floor_stiffness = 0.01
ground_spring = 0.1
port_spring = 0.5
gain_factor = 64.0
tiny_term = 1e-6


def child_weights(tap_offsets, tap_weights):
    codes = tap_offsets[:, 0] * 4 + tap_offsets[:, 1] * 2 + tap_offsets[:, 2]
    onehot = (codes[:, None] == jnp.arange(8, dtype=jnp.int32)[None, :]).astype(jnp.float32)
    shares = tap_weights / jnp.sum(tap_weights)
    return jnp.sum(onehot * shares[:, None], axis=0).astype(jnp.bfloat16).reshape(2, 2, 2)


def neighbours(padded):
    center = padded[:, 1:-1, 1:-1, 1:-1]
    beside = [padded[:, 2:, 1:-1, 1:-1], padded[:, :-2, 1:-1, 1:-1],
              padded[:, 1:-1, 2:, 1:-1], padded[:, 1:-1, :-2, 1:-1],
              padded[:, 1:-1, 1:-1, 2:], padded[:, 1:-1, 1:-1, :-2]]
    return center, beside


def extend(stack):
    return jnp.pad(stack, ((0, 0), (1, 1), (1, 1), (1, 1)))


def operate(field_stack, conductance, diagonal):
    center, beside = neighbours(extend(field_stack))
    result = diagonal * center
    for face_cond, other_side in zip(conductance, beside):
        result = result + face_cond * (center - other_side)
    return result


def inner_sums(left, right):
    return jnp.sum(left * right, axis=(1, 2, 3))


def reference(design, tap_offsets, tap_weights, input_load, input_mask, output_mask, fixed_mask):
    child_table = child_weights(tap_offsets, tap_weights).astype(jnp.float32)
    density = jnp.zeros((NX, NY, NZ), jnp.float32)
    for x_bit in range(2):
        for y_bit in range(2):
            for z_bit in range(2):
                density = density + child_table[x_bit, y_bit, z_bit] * design[x_bit::2, y_bit::2, z_bit::2].astype(jnp.float32)
    stiffness = floor_stiffness + (1.0 - floor_stiffness) * density * density * density
    stiff_center, stiff_beside = neighbours(extend(stiffness[None]))
    conductance = [2.0 * stiff_center * other_side / (stiff_center + other_side) for other_side in stiff_beside]
    diagonal = ground_spring + fixed_mask.astype(jnp.float32) + port_spring * (input_mask + output_mask).astype(jnp.float32)
    loads = jnp.stack([input_mask.astype(jnp.float32) * input_load, output_mask.astype(jnp.float32)])
    solution = jnp.zeros_like(loads)
    residual = loads
    direction = loads
    norm_now = inner_sums(residual, residual)
    for step in range(ITERS):
        applied = operate(direction, conductance, diagonal)
        step_size = norm_now / (inner_sums(direction, applied) + tiny_term)
        solution = solution + step_size[:, None, None, None] * direction
        residual = residual - step_size[:, None, None, None] * applied
        if step + 1 < ITERS:
            norm_next = inner_sums(residual, residual)
            direction = residual + (norm_next / (norm_now + tiny_term))[:, None, None, None] * direction
            norm_now = norm_next
    center, beside = neighbours(extend(solution))
    sensitivity = jnp.zeros((NX, NY, NZ), jnp.float32)
    for stiff_other, other_side in zip(stiff_beside, beside):
        face_total = stiff_center[0] + stiff_other[0]
        weight = 2.0 * stiff_other[0] * stiff_other[0] / (face_total * face_total)
        sensitivity = sensitivity + weight * (center[0] - other_side[0]) * (center[1] - other_side[1])
    slope = -3.0 * (1.0 - floor_stiffness) * density * density * sensitivity
    scaled = gain_factor * slope
    layers = []
    for x_bit in range(2):
        rows_y = []
        for y_bit in range(2):
            pieces = [child_table[x_bit, y_bit, z_bit] * scaled for z_bit in range(2)]
            rows_y.append(jnp.stack(pieces, axis=3).reshape(NX, NY, 2 * NZ))
        layers.append(jnp.stack(rows_y, axis=2).reshape(NX, 2 * NY, 2 * NZ))
    return jnp.stack(layers, axis=1).reshape(2 * NX, 2 * NY, 2 * NZ)
```

```python
import functools

import jax
import jax.numpy as jnp
from jax import lax
from jax.experimental import pallas as pl
from jax.experimental.pallas import tpu as pltpu
from jax.sharding import PartitionSpec as P

MESH = pl.DeviceIdType.MESH

FLOOR = 0.01
GROUND = 0.1
PORT = 0.5
GAIN = 64.0
TINY = 1e-06
MAX_STEP = 10.0

CHUNKS = 4
STEPS = 4
F32 = jnp.float32
BF16 = jnp.bfloat16

ST, RH, QH = 0, 1, 2


def child_scalars(offs, wts):
    taps = wts.shape[0]
    total = wts[0]
    for t in range(1, taps):
        total = total + wts[t]
    sums = [jnp.float32(0.0)] * 8
    for t in range(taps):
        code = offs[t, 0] * 4 + offs[t, 1] * 2 + offs[t, 2]
        for c in range(8):
            sums[c] = sums[c] + jnp.where(code == c, wts[t], jnp.float32(0.0))
    return sums, total


def child_rows(offs, wts, lanes):
    sums, total = child_scalars(offs, wts)
    below = jnp.full((1, lanes), total, F32)
    return [jnp.full((1, lanes), s, F32) / below for s in sums]


def step_kernel(
    n_gx, n_gy, n_dev,
    design, load, imask, omask, fmask, offs, wts,
    out,
    dbuf, lbuf, ibuf, obuf, fbuf,
    wmat, pbuf, dsend, dens, st, fld, diag,
    cx, cy, cz, sarr, gprev,
    xr_st, xr_r, xr_q,
    ys_st, ys_r, ys_q, yr_st, yr_r, yr_q,
    zs_st, zs_r, zs_q, zr_st, zr_r, zr_q,
    yflux, zflux, zcon, ycon, xcon,
    ysb, zsb,
    ar1, ar2, coef, bsend,
    in_sem, a_send, a_recv, h_send, h_recv, s_send, s_recv, t_send, t_recv, b_send, b_recv, o_sem,
):
    gx = lax.axis_index("gx")
    gy = lax.axis_index("gy")
    me = lax.axis_index("dev")
    nx, ny, nz = lbuf.shape
    per = nx // CHUNKS
    core = lax.rem(gy, 2)
    half = gy // 2

    ins = []
    for ch in range(CHUNKS):
        c = pltpu.make_async_copy(
            design.at[pl.ds(ch * per, per)], dbuf.at[pl.ds(ch * per, per)], in_sem.at[ch]
        )
        c.start()
        ins.append(c)
    fields_in = []
    for k, (a, b) in enumerate(((load, lbuf), (imask, ibuf), (omask, obuf), (fmask, fbuf))):
        c = pltpu.make_async_copy(a, b, in_sem.at[CHUNKS + k])
        c.start()
        fields_in.append(c)

    for ref in (xr_st, xr_r, xr_q, yr_st, yr_r, yr_q, zr_st, zr_r, zr_q):
        ref[...] = jnp.zeros_like(ref)

    id1 = me * 2 + core
    id2 = gx * 2 + half

    def peer1(k):
        other = lax.rem(id1 + k, 8)
        return {"gx": gx, "gy": half * 2 + lax.rem(other, 2), "dev": other // 2}

    def peer2(k):
        other = lax.rem(id2 + k, 16)
        return {"gx": other // 2, "gy": lax.rem(other, 2) * 2 + core, "dev": me}

    barrier = pltpu.get_barrier_semaphore()
    for k in range(1, 8):
        pl.semaphore_signal(barrier, inc=1, device_id=peer1(k), device_id_type=MESH)
    for k in range(1, 16):
        pl.semaphore_signal(barrier, inc=1, device_id=peer2(k), device_id_type=MESH)
    pl.semaphore_signal(
        barrier, inc=1, device_id={"gx": gx, "gy": n_gy - 1 - gy, "dev": me}, device_id_type=MESH
    )

    kid = child_rows(offs, wts, 256)
    row_i = lax.broadcasted_iota(jnp.int32, (256, 256), 0)
    col_i = lax.broadcasted_iota(jnp.int32, (256, 256), 1)
    paired = row_i // 2 == lax.rem(col_i, 128)
    even = lax.rem(row_i, 2) == 0
    left = col_i < 128
    for a in range(2):
        e = jnp.where(
            even,
            jnp.where(left, kid[4 * a], kid[4 * a + 2]),
            jnp.where(left, kid[4 * a + 1], kid[4 * a + 3]),
        )
        wmat[a] = jnp.where(paired, e, 0.0).astype(BF16)

    def a2a(ch, k):
        dst = lax.rem(me + k, n_dev)
        return pltpu.make_async_remote_copy(
            src_ref=dsend.at[dst, pl.ds(ch * per, per)],
            dst_ref=dens.at[pl.ds(ch * per, per), pl.ds(pl.multiple_of(me * 8, 8), 8)],
            send_sem=a_send.at[ch, k - 1],
            recv_sem=a_recv.at[ch, k - 1],
            device_id={"gx": gx, "gy": gy, "dev": dst},
            device_id_type=MESH,
        )

    def a2a_in(ch, k):
        src = lax.rem(me + n_dev - k, n_dev)
        return pltpu.make_async_remote_copy(
            src_ref=dsend.at[src, pl.ds(ch * per, per)],
            dst_ref=dens.at[pl.ds(ch * per, per), pl.ds(pl.multiple_of(src * 8, 8), 8)],
            send_sem=a_send.at[ch, k - 1],
            recv_sem=a_recv.at[ch, k - 1],
            device_id={"gx": gx, "gy": gy, "dev": src},
            device_id_type=MESH,
        )

    for ch in range(CHUNKS):
        ins[ch].wait()
        for c in range(n_dev):
            total = None
            for a in range(2):
                lhs = dbuf[pl.ds(ch * per, per), a, :, pl.ds(256 * c, 256)].reshape(per * 16, 256)
                part = jnp.dot(lhs, wmat[a], preferred_element_type=F32)
                total = part if total is None else total + part
            pbuf[c, 0] = total[:, :128]
            pbuf[c, 1] = total[:, 128:]
            d = pbuf[c, 0, pl.ds(0, per * 8, stride=2), :] + pbuf[c, 1, pl.ds(1, per * 8, stride=2), :]
            dsend[c, pl.ds(ch * per, per)] = d.reshape(per, 8, 128)
        if ch == 0:
            pl.semaphore_wait(barrier, 23)
        for k in (2, 1, 3):
            a2a(ch, k).start()
        dens[pl.ds(ch * per, per), pl.ds(pl.multiple_of(me * 8, 8), 8)] = dsend[me, pl.ds(ch * per, per)]

    xsend = {
        ST: (lambda side: st.at[0 if side == 0 else nx - 1]),
        RH: (lambda side: fld.at[pl.ds(0, 2), 0 if side == 0 else nx - 1]),
        QH: (lambda side: fld.at[pl.ds(2, 2), 0 if side == 0 else nx - 1]),
    }
    xrecv = {ST: xr_st, RH: xr_r, QH: xr_q}
    ysend = {ST: ys_st, RH: ys_r, QH: ys_q}
    yrecv = {ST: yr_st, RH: yr_r, QH: yr_q}
    zsend = {ST: zs_st, RH: zs_r, QH: zs_q}
    zrecv = {ST: zr_st, RH: zr_r, QH: zr_q}
    spot = {"gx": (gx, n_gx), "gy": (gy, n_gy), "dev": (me, n_dev)}

    def face(e, axis, side):
        k = {"gx": 0, "gy": 2, "dev": 4}[axis] + side
        src = {
            "gx": lambda: xsend[e](side),
            "gy": lambda: ysend[e].at[side],
            "dev": lambda: zsend[e].at[side],
        }[axis]()
        dst = {"gx": xrecv, "gy": yrecv, "dev": zrecv}[axis][e].at[1 - side]
        pos, size = spot[axis]
        other = pos - 1 if side == 0 else pos + 1
        other = jnp.clip(other, 0, size - 1)
        target = {"gx": gx, "gy": gy, "dev": me}
        target[axis] = other
        copy = pltpu.make_async_remote_copy(
            src_ref=src, dst_ref=dst, send_sem=h_send.at[e, k], recv_sem=h_recv.at[e, k],
            device_id=target, device_id_type=MESH,
        )
        sends = pos > 0 if side == 0 else pos < size - 1
        gets = pos < size - 1 if side == 0 else pos > 0
        return copy, sends, gets

    def start_face(e, axis, side):
        copy, sends, _ = face(e, axis, side)

        @pl.when(sends)
        def _():
            copy.start()

    def wait_face(e, axis, side):
        copy, _, gets = face(e, axis, side)

        @pl.when(gets)
        def _():
            copy.wait_recv()

    iy = lax.broadcasted_iota(jnp.int32, (ny, nz), 0)
    iz = lax.broadcasted_iota(jnp.int32, (ny, nz), 1)
    last_y, last_z = iy == ny - 1, iz == nz - 1
    first_y, first_z = iy == 0, iz == 0
    zero = jnp.zeros((ny, nz), F32)

    def fold(v):
        return jnp.sum(v.reshape(ny // 8, 8, nz), axis=0)

    def lane_to(v, lane, at):
        return pltpu.roll(v, lax.rem(at - lane + 2 * nz, nz), 1)

    for c in fields_in:
        c.wait()
    for f in range(4):
        fld[f, nx] = zero
    st[nx] = zero

    def load_plane(i, carry):
        zlo, zhi, m0r, m0s = carry
        im, om = ibuf[i].astype(F32), obuf[i].astype(F32)
        r, s = im * lbuf[i], om
        diag[i] = GROUND + fbuf[i].astype(F32) + PORT * (im + om)
        fld[0, i] = r
        fld[1, i] = s
        for f, v in enumerate((r, s)):
            ys_r[0, f, pl.ds(i, 1), :] = v[0:1]
            ys_r[1, f, pl.ds(i, 1), :] = v[ny - 1 : ny]
            spot_z = iz == i + nx * f
            zlo = jnp.where(spot_z, lane_to(v, 0, i + nx * f), zlo)
            zhi = jnp.where(spot_z, lane_to(v, nz - 1, i + nx * f), zhi)
        return zlo, zhi, m0r + fold(r * r), m0s + fold(s * s)

    none = jnp.zeros((8, nz), F32)
    zlo, zhi, m0r, m0s = lax.fori_loop(0, nx, load_plane, (zero, zero, none, none))
    zs_r[0] = zlo
    zs_r[1] = zhi
    for axis in ("gx", "gy", "dev"):
        for side in range(2):
            start_face(RH, axis, side)

    zlo, zhi = zero, zero
    for ch in range(CHUNKS):
        for k in (2, 1, 3):
            a2a_in(ch, k).wait_recv()

        def stiff_plane(i, carry):
            zlo, zhi = carry
            d = dens[i]
            s = FLOOR + (1.0 - FLOOR) * d * d * d
            st[i] = s
            ys_st[0, pl.ds(i, 1), :] = s[0:1]
            ys_st[1, pl.ds(i, 1), :] = s[ny - 1 : ny]
            zlo = jnp.where(iz == i, lane_to(s, 0, i), zlo)
            zhi = jnp.where(iz == i, lane_to(s, nz - 1, i), zhi)
            return zlo, zhi

        zlo, zhi = lax.fori_loop(ch * per, (ch + 1) * per, stiff_plane, (zlo, zhi))
        if ch == 0:
            start_face(ST, "gx", 0)
    zs_st[0] = zlo
    zs_st[1] = zhi
    start_face(ST, "gx", 1)
    for axis in ("gy", "dev"):
        for side in range(2):
            start_face(ST, axis, side)

    def between(a, b):
        return 2.0 * a * b / (a + b)

    def inner_plane(i, carry):
        before_r, before_s = carry
        s = st[i]
        kx = between(s, st[i + 1])
        ky = between(s, jnp.where(last_y, 0.0, pltpu.roll(s, ny - 1, 0)))
        kz = between(s, jnp.where(last_z, 0.0, pltpu.roll(s, nz - 1, 1)))
        cx[i] = kx
        cy[i] = ky
        cz[i] = kz
        dg = diag[i]
        new = []
        for f, before in ((0, before_r), (1, before_s)):
            v = fld[f, i]
            fx = kx * (v - fld[f, i + 1])
            fy = ky * (v - pltpu.roll(v, ny - 1, 0))
            fz = kz * (v - pltpu.roll(v, nz - 1, 1))
            q = dg * v + (fx - before) + (fy - pltpu.roll(fy, 1, 0)) + (fz - pltpu.roll(fz, 1, 1))
            fld[2 + f, i] = q
            new.append(fx)
        return tuple(new)

    lax.fori_loop(0, nx, inner_plane, (zero, zero))

    for e in (RH, ST):
        for axis in ("gx", "gy", "dev"):
            for side in range(2):
                wait_face(e, axis, side)

    one_lane, two_lane = iz < nx, iz < 2 * nx
    for side in range(2):
        edge = 0 if side == 0 else nx - 1
        xcon[side] = between(st[edge], xr_st[side])
        ycon[side] = between(ys_st[side], yr_st[side])
        kz = between(zs_st[side] + jnp.where(one_lane, 0.0, 1.0), zr_st[side])
        zcon[side] = jnp.where(one_lane, kz, jnp.where(two_lane, pltpu.roll(kz, nx, 1), 0.0))
        for f in range(2):
            fld[2 + f, edge] += xcon[side] * (fld[f, edge] - xr_r[side, f])
            yflux[side, f] = ycon[side] * (ys_r[side, f] - yr_r[side, f])
        zflux[side] = zcon[side] * (zs_r[side] - zr_r[side])

    def edge_plane(i, carry):
        zlo, zhi, sums = carry
        sums = list(sums)
        for f in range(2):
            q = fld[2 + f, i]
            q += jnp.where(first_y, yflux[0, f, pl.ds(i, 1), :], 0.0)
            q += jnp.where(last_y, yflux[1, f, pl.ds(i, 1), :], 0.0)
            at = i + nx * f
            q += jnp.where(first_z, lane_to(zflux[0], at, 0), 0.0)
            q += jnp.where(last_z, lane_to(zflux[1], at, nz - 1), 0.0)
            fld[2 + f, i] = q
            ys_q[0, f, pl.ds(i, 1), :] = q[0:1]
            ys_q[1, f, pl.ds(i, 1), :] = q[ny - 1 : ny]
            zlo = jnp.where(iz == at, lane_to(q, 0, at), zlo)
            zhi = jnp.where(iz == at, lane_to(q, nz - 1, at), zhi)
            sums[f] += fold(fld[f, i] * q)
            sums[2 + f] += fold(q * q)
        return zlo, zhi, tuple(sums)

    zlo, zhi, sums12 = lax.fori_loop(0, nx, edge_plane, (zero, zero, (none,) * 4))
    zs_q[0] = zlo
    zs_q[1] = zhi
    for axis in ("gx", "gy", "dev"):
        for side in range(2):
            start_face(QH, axis, side)

    gprev[...] = jnp.zeros_like(gprev)

    def product_plane(i, carry):
        e_r, e_s = carry
        v = [fld[f, i] for f in range(4)]
        dg = diag[i]
        e_r += fold(dg * v[2] * v[2])
        e_s += fold(dg * v[3] * v[3])
        held = [None] * 4
        for axis in range(3):
            k = (cx, cy, cz)[axis][i]
            if axis == 0:
                d = [v[f] - fld[f, i + 1] for f in range(4)]
            elif axis == 1:
                d = [v[f] - pltpu.roll(v[f], ny - 1, 0) for f in range(4)]
            else:
                d = [v[f] - pltpu.roll(v[f], nz - 1, 1) for f in range(4)]
            kr, kq = k * d[0], k * d[2]
            ks, kp = k * d[1], k * d[3]
            e_r += fold(kq * d[2])
            e_s += fold(kp * d[3])
            for j, (a, b) in enumerate(((kr, ks), (kr, kp), (kq, ks), (kq, kp))):
                g = a * b
                if axis == 0:
                    held[j] = g + gprev[j]
                    gprev[j] = g
                elif axis == 1:
                    held[j] += g + pltpu.roll(g, 1, 0)
                else:
                    held[j] += g + pltpu.roll(g, 1, 1)
        for j in range(4):
            sarr[j, i] = held[j]
        return e_r, e_s

    e_r, e_s = lax.fori_loop(0, nx, product_plane, (none, none))

    for side in range(2):
        for axis in ("gx", "gy", "dev"):
            wait_face(QH, axis, side)

    dxs = [xcon[1] * (fld[2 + f, nx - 1] - xr_q[1, f]) * (fld[2 + f, nx - 1] - xr_q[1, f]) for f in range(2)]
    dys = [ycon[1] * (ys_q[1, f] - yr_q[1, f]) * (ys_q[1, f] - yr_q[1, f]) for f in range(2)]
    dz = zs_q[1] - zr_q[1]
    dz = zcon[1] * dz * dz
    e_r += fold(dxs[0] + dys[0] + jnp.where(one_lane, dz, 0.0))
    e_s += fold(dxs[1] + dys[1] + jnp.where(one_lane, 0.0, dz))

    for k, v in enumerate((m0r, m0s) + tuple(sums12) + (e_r, e_s)):
        ar1[id1, k : k + 1, :] = jnp.sum(v, axis=0, keepdims=True)

    def gather1(k):
        return pltpu.make_async_remote_copy(
            src_ref=ar1.at[id1], dst_ref=ar1.at[id1], send_sem=s_send.at[k], recv_sem=s_recv.at[k],
            device_id=peer1(k), device_id_type=MESH,
        )

    def gather1_in(k):
        src = lax.rem(id1 + 8 - k, 8)
        return pltpu.make_async_remote_copy(
            src_ref=ar1.at[src], dst_ref=ar1.at[src], send_sem=s_send.at[k], recv_sem=s_recv.at[k],
            device_id=peer1(8 - k), device_id_type=MESH,
        )

    def gather2(k):
        return pltpu.make_async_remote_copy(
            src_ref=ar2.at[id2], dst_ref=ar2.at[id2], send_sem=t_send.at[k], recv_sem=t_recv.at[k],
            device_id=peer2(k), device_id_type=MESH,
        )

    def gather2_in(k):
        src = lax.rem(id2 + 16 - k, 16)
        return pltpu.make_async_remote_copy(
            src_ref=ar2.at[src], dst_ref=ar2.at[src], send_sem=t_send.at[k], recv_sem=t_recv.at[k],
            device_id=peer2(16 - k), device_id_type=MESH,
        )

    for k in range(1, 8):
        gather1(k).start()

    for side in range(2):
        edge = 0 if side == 0 else nx - 1
        k = xcon[side]
        d = [k * (fld[f, edge] - (xr_r if f < 2 else xr_q)[side, f % 2]) for f in range(4)]
        for j, (a, b) in enumerate(((0, 1), (0, 3), (2, 1), (2, 3))):
            sarr[j, edge] += d[a] * d[b]
        k = ycon[side]
        d = [
            k * ((ys_r if f < 2 else ys_q)[side, f % 2] - (yr_r if f < 2 else yr_q)[side, f % 2])
            for f in range(4)
        ]
        for j, (a, b) in enumerate(((0, 1), (0, 3), (2, 1), (2, 3))):
            ysb[side, j] = d[a] * d[b]
        k = zcon[side]
        dr = k * (zs_r[side] - zr_r[side])
        dq = k * (zs_q[side] - zr_q[side])
        ds, dp = pltpu.roll(dr, nz - nx, 1), pltpu.roll(dq, nz - nx, 1)
        packed = zero
        for j, g in enumerate((dr * ds, dr * dp, dq * ds, dq * dp)):
            packed = jnp.where(iz // nx == j, g if j == 0 else pltpu.roll(g, nx * j, 1), packed)
        zsb[side] = packed

    def scale_plane(i, carry):
        d, s = dens[i], st[i]
        ratio = d / s
        scale = (-1.5 * (1.0 - FLOOR) * GAIN) * ratio * ratio
        for j in range(4):
            g = sarr[j, i]
            g += jnp.where(first_y, ysb[0, j, pl.ds(i, 1), :], 0.0)
            g += jnp.where(last_y, ysb[1, j, pl.ds(i, 1), :], 0.0)
            at = i + nx * j
            g += jnp.where(first_z, lane_to(zsb[0], at, 0), 0.0)
            g += jnp.where(last_z, lane_to(zsb[1], at, nz - 1), 0.0)
            sarr[j, i] = scale * g
        return carry

    lax.fori_loop(0, nx // 2, scale_plane, 0)

    for k in range(1, 8):
        gather1_in(k).wait_recv()
    part = ar1[0]
    for k in range(1, 8):
        part = part + ar1[k]
    ar2[id2] = part
    for k in range(1, 16):
        gather2(k).start()

    lax.fori_loop(nx // 2, nx, scale_plane, 0)

    for k in range(1, 16):
        gather2_in(k).wait_recv()
    whole = ar2[0]
    for k in range(1, 16):
        whole = whole + ar2[k]

    coef[...] = jnp.broadcast_to(jnp.sum(whole, axis=1, keepdims=True), coef.shape)
    m0, m1, m2, m3 = (coef[pl.ds(2 * k, 2), :] for k in range(4))
    step0 = m0 / (m1 + TINY)
    rr1 = jnp.maximum(m0 - 2.0 * step0 * m1 + step0 * step0 * m2, 0.0)
    beta = rr1 / (m0 + TINY)
    r_a_r = m1 - 2.0 * step0 * m2 + step0 * step0 * m3
    r_a_d = m1 - step0 * m2
    d_a_d = r_a_r + 2.0 * beta * r_a_d + beta * beta * m1
    step1 = jnp.minimum(rr1 / (jnp.maximum(d_a_d, 0.0) + TINY), MAX_STEP)
    c0 = step0 + step1 * (1.0 + beta)
    c1 = -step0 * step1
    mix = [
        c0[0:1] * c0[1:2],
        c0[0:1] * c1[1:2],
        c1[0:1] * c0[1:2],
        c1[0:1] * c1[1:2],
    ]

    rows = per * 8

    def back(ch, k):
        dst = lax.rem(me + k, n_dev)
        return pltpu.make_async_remote_copy(
            src_ref=bsend.at[dst, pl.ds(ch * rows, rows)],
            dst_ref=out.at[me, pl.ds(ch * rows, rows)],
            send_sem=b_send.at[ch, k - 1],
            recv_sem=b_recv.at[ch, k - 1],
            device_id={"gx": gx, "gy": gy, "dev": dst},
            device_id_type=MESH,
        )

    def back_in(ch, k):
        src = lax.rem(me + n_dev - k, n_dev)
        return pltpu.make_async_remote_copy(
            src_ref=bsend.at[src, pl.ds(ch * rows, rows)],
            dst_ref=out.at[src, pl.ds(ch * rows, rows)],
            send_sem=b_send.at[ch, k - 1],
            recv_sem=b_recv.at[ch, k - 1],
            device_id={"gx": gx, "gy": gy, "dev": src},
            device_id_type=MESH,
        )

    for ch in range(CHUNKS):

        def pair_planes(p, carry):
            v = None
            for j in range(4):
                part = mix[j] * sarr[j, pl.ds(2 * p, 2)]
                v = part if v is None else v + part
            for d in range(n_dev):
                two = v[:, 8 * d : 8 * d + 8, :].reshape(16, nz)
                bsend[d, pl.ds(pl.multiple_of(p * 16, 16), 16), :] = two.astype(BF16)
            return carry

        lax.fori_loop(ch * per // 2, (ch + 1) * per // 2, pair_planes, 0)
        for k in (2, 1, 3):
            back(ch, k).start()
    own = pltpu.make_async_copy(bsend.at[me], out.at[me], o_sem)
    own.start()

    for ch in range(CHUNKS):
        for k in range(1, 4):
            a2a(ch, k).wait_send()
    for e in (ST, RH, QH):
        for axis in ("gx", "gy", "dev"):
            for side in range(2):
                copy, sends, _ = face(e, axis, side)

                @pl.when(sends)
                def _():
                    copy.wait_send()

    for k in range(1, 8):
        gather1(k).wait_send()
    for k in range(1, 16):
        gather2(k).wait_send()
    own.wait()
    for ch in range(CHUNKS):
        for k in (2, 1, 3):
            back(ch, k).wait_send()
            back_in(ch, k).wait_recv()


def expand_kernel(offs, wts, s_hbm, o_hbm, sbuf, obuf, wexp, i_sem, o_sem):
    n_dev, rows, nz = sbuf.shape
    nx = rows // 8
    per = nx // STEPS

    def fetch(c):
        part = pl.ds(c * per * 8, per * 8)
        return pltpu.make_async_copy(s_hbm.at[:, part], sbuf.at[:, part], i_sem.at[c])

    def store(c, l):
        return pltpu.make_async_copy(
            obuf.at[l, pl.ds(c * 2 * per, 2 * per)],
            o_hbm.at[pl.ds(c * 2 * per, 2 * per), :, pl.ds(128 * l, 128)],
            o_sem.at[c, l],
        )

    for c in range(STEPS):
        fetch(c).start()
    kid = child_rows(offs, wts, 256)
    row_i = lax.broadcasted_iota(jnp.int32, (128, 256), 0)
    col_i = lax.broadcasted_iota(jnp.int32, (128, 256), 1)
    paired = col_i // 2 == row_i
    even = lax.rem(col_i, 2) == 0
    for ab in range(4):
        e = jnp.where(even, kid[2 * ab], kid[2 * ab + 1])
        wexp[ab] = jnp.where(paired, e, 0.0).astype(BF16)

    for c in range(STEPS):
        fetch(c).wait()
        for d in range(n_dev):
            lhs = sbuf[d, pl.ds(c * per * 8, per * 8)]
            for a in range(2):
                for b in range(2):
                    t = jnp.dot(lhs, wexp[2 * a + b], preferred_element_type=F32)
                    for i in range(per):
                        for h in range(2):
                            obuf[2 * d + h, 2 * (c * per + i) + a, pl.ds(b, 8, stride=2), :] = t[
                                8 * i : 8 * i + 8, 128 * h : 128 * h + 128
                            ]
            for h in range(2):
                store(c, 2 * d + h).start()
    for c in range(STEPS):
        for l in range(2 * n_dev):
            store(c, l).wait()


def solution(mesh):
    n_gx, n_gy, n_dev = mesh.shape["gx"], mesh.shape["gy"], mesh.shape["dev"]

    def body(design, tap_offsets, tap_weights, input_load, input_mask, output_mask, fixed_mask):
        nx, ny, nz = input_load.shape
        cell = (nx, ny, nz)
        plane = (ny, nz)
        hbm = pl.BlockSpec(memory_space=pl.ANY)
        smem = pl.BlockSpec(memory_space=pltpu.SMEM)
        vm = lambda *shape: pltpu.VMEM(shape, F32)
        dma = lambda *shape: pltpu.SemaphoreType.DMA(shape)
        scratch = [
            pltpu.VMEM((nx, 2, 16, 1024), BF16),
            vm(*cell),
            pltpu.VMEM(cell, jnp.int32),
            pltpu.VMEM(cell, jnp.int32),
            pltpu.VMEM(cell, jnp.int32),
            pltpu.VMEM((2, 256, 256), BF16),
            vm(n_dev, 2, nx // CHUNKS * 16, 128),
            vm(n_dev, nx, 8, nz),
            vm(*cell),
            vm(nx + 1, *plane),
            vm(4, nx + 1, *plane),
            vm(*cell),
            vm(*cell), vm(*cell), vm(*cell),
            vm(4, *cell),
            vm(4, *plane),
            vm(2, *plane), vm(2, 2, *plane), vm(2, 2, *plane),
            vm(2, nx, nz), vm(2, 2, nx, nz), vm(2, 2, nx, nz),
            vm(2, nx, nz), vm(2, 2, nx, nz), vm(2, 2, nx, nz),
            vm(2, *plane), vm(2, *plane), vm(2, *plane),
            vm(2, *plane), vm(2, *plane), vm(2, *plane),
            vm(2, 2, nx, nz), vm(2, *plane), vm(2, *plane), vm(2, nx, nz), vm(2, *plane),
            vm(2, 4, nx, nz), vm(2, *plane),
            vm(8, 8, 128), vm(16, 8, 128), vm(8, 128),
            pltpu.VMEM((n_dev, nx * 8, nz), BF16),
            dma(CHUNKS + 4), dma(CHUNKS, 3), dma(CHUNKS, 3), dma(3, 6), dma(3, 6),
            dma(8), dma(8), dma(16), dma(16), dma(CHUNKS, 3), dma(CHUNKS, 3), pltpu.SemaphoreType.DMA,
        ]
        returned = pl.pallas_call(
            functools.partial(step_kernel, n_gx, n_gy, n_dev),
            out_shape=jax.ShapeDtypeStruct((n_dev, nx * 8, nz), BF16),
            in_specs=[hbm] * 5 + [smem, smem],
            out_specs=hbm,
            scratch_shapes=scratch,
            compiler_params=pltpu.CompilerParams(
                collective_id=0, has_side_effects=True, vmem_limit_bytes=40 * 1024 * 1024
            ),
            name="step",
        )(
            design.reshape(nx, 2, 16, 1024), input_load, input_mask, output_mask, fixed_mask,
            tap_offsets, tap_weights,
        )
        return pl.pallas_call(
            expand_kernel,
            out_shape=jax.ShapeDtypeStruct(design.shape, F32),
            in_specs=[smem, smem, hbm],
            out_specs=hbm,
            scratch_shapes=[
                pltpu.VMEM((n_dev, nx * 8, nz), BF16),
                vm(2 * n_dev, 2 * nx, 16, 128),
                pltpu.VMEM((4, 128, 256), BF16),
                dma(STEPS),
                dma(STEPS, 2 * n_dev),
            ],
            name="expand",
        )(tap_offsets, tap_weights, returned)

    block = P("gx", "gy", "dev")
    owner = P("gx", ("gy", "dev"), None)
    return jax.shard_map(
        body, mesh=mesh,
        in_specs=(owner, P(), P(), block, block, block, block),
        out_specs=owner,
        check_vma=False,
    )
```

```python
import functools

import jax
import jax.numpy as jnp
from jax import lax
from jax.experimental import pallas as pl
from jax.experimental.pallas import tpu as pltpu
from jax.sharding import PartitionSpec as P

MESH = pl.DeviceIdType.MESH

FLOOR = 0.01
GROUND = 0.1
PORT = 0.5
GAIN = 64.0
TINY = 1e-06
MAX_STEP = 10.0

CHUNKS = 4
STEPS = 4
F32 = jnp.float32
BF16 = jnp.bfloat16

ST, RH, QH = 0, 1, 2


def child_scalars(offs, wts):
    taps = wts.shape[0]
    total = wts[0]
    for t in range(1, taps):
        total = total + wts[t]
    sums = [jnp.float32(0.0)] * 8
    for t in range(taps):
        code = offs[0, t] * 4 + offs[1, t] * 2 + offs[2, t]
        for c in range(8):
            sums[c] = sums[c] + jnp.where(code == c, wts[t], jnp.float32(0.0))
    return sums, total


def child_rows(offs, wts, lanes):
    sums, total = child_scalars(offs, wts)
    below = jnp.full((1, lanes), total, F32)
    return [jnp.full((1, lanes), s, F32) / below for s in sums]


def step_kernel(
    n_gx, n_gy, n_dev,
    design, load, imask, omask, fmask, offs_hbm, wts_hbm,
    out,
    dbuf, lbuf, ibuf, obuf, fbuf,
    wmat, pbuf, dsend, dens, st, fld, diag,
    cx, cy, cz, sarr, gprev,
    xr_st, xr_r, xr_q,
    ys_st, ys_r, ys_q, yr_st, yr_r, yr_q,
    zs_st, zs_r, zs_q, zr_st, zr_r, zr_q,
    yflux, zflux, zcon, ycon, xcon,
    ysb, zsb,
    ar1, ar2, coef, bsend,
    offs, wts, tap_sem, in_sem, a_send, a_recv, h_send, h_recv, s_send, s_recv, t_send, t_recv, b_send, b_recv, o_sem,
):
    gx = lax.axis_index("gx")
    gy = lax.axis_index("gy")
    me = lax.axis_index("dev")
    nx, ny, nz = lbuf.shape
    per = nx // CHUNKS
    core = lax.rem(gy, 2)
    half = gy // 2

    taps_in = [
        pltpu.make_async_copy(offs_hbm, offs, tap_sem.at[0]),
        pltpu.make_async_copy(wts_hbm, wts, tap_sem.at[1]),
    ]
    for c in taps_in:
        c.start()
    ins = []
    for ch in range(CHUNKS):
        c = pltpu.make_async_copy(
            design.at[pl.ds(ch * per, per)], dbuf.at[pl.ds(ch * per, per)], in_sem.at[ch]
        )
        c.start()
        ins.append(c)
    fields_in = []
    for k, (a, b) in enumerate(((load, lbuf), (imask, ibuf), (omask, obuf), (fmask, fbuf))):
        c = pltpu.make_async_copy(a, b, in_sem.at[CHUNKS + k])
        c.start()
        fields_in.append(c)

    for ref in (xr_st, xr_r, xr_q, yr_st, yr_r, yr_q, zr_st, zr_r, zr_q):
        ref[...] = jnp.zeros_like(ref)

    id1 = me * 2 + core
    id2 = gx * 2 + half

    def peer1(k):
        other = lax.rem(id1 + k, 8)
        return {"gx": gx, "gy": half * 2 + lax.rem(other, 2), "dev": other // 2}

    def peer2(k):
        other = lax.rem(id2 + k, 16)
        return {"gx": other // 2, "gy": lax.rem(other, 2) * 2 + core, "dev": me}

    barrier = pltpu.get_barrier_semaphore()
    for k in range(1, 8):
        pl.semaphore_signal(barrier, inc=1, device_id=peer1(k), device_id_type=MESH)
    for k in range(1, 16):
        pl.semaphore_signal(barrier, inc=1, device_id=peer2(k), device_id_type=MESH)
    pl.semaphore_signal(
        barrier, inc=1, device_id={"gx": gx, "gy": n_gy - 1 - gy, "dev": me}, device_id_type=MESH
    )

    for c in taps_in:
        c.wait()
    kid = child_rows(offs, wts, 256)
    row_i = lax.broadcasted_iota(jnp.int32, (256, 256), 0)
    col_i = lax.broadcasted_iota(jnp.int32, (256, 256), 1)
    paired = row_i // 2 == lax.rem(col_i, 128)
    even = lax.rem(row_i, 2) == 0
    left = col_i < 128
    for a in range(2):
        e = jnp.where(
            even,
            jnp.where(left, kid[4 * a], kid[4 * a + 2]),
            jnp.where(left, kid[4 * a + 1], kid[4 * a + 3]),
        )
        wmat[a] = jnp.where(paired, e, 0.0).astype(BF16)

    def a2a(ch, k):
        dst = lax.rem(me + k, n_dev)
        return pltpu.make_async_remote_copy(
            src_ref=dsend.at[dst, pl.ds(ch * per, per)],
            dst_ref=dens.at[pl.ds(ch * per, per), pl.ds(pl.multiple_of(me * 8, 8), 8)],
            send_sem=a_send.at[ch, k - 1],
            recv_sem=a_recv.at[ch, k - 1],
            device_id={"gx": gx, "gy": gy, "dev": dst},
            device_id_type=MESH,
        )

    def a2a_in(ch, k):
        src = lax.rem(me + n_dev - k, n_dev)
        return pltpu.make_async_remote_copy(
            src_ref=dsend.at[src, pl.ds(ch * per, per)],
            dst_ref=dens.at[pl.ds(ch * per, per), pl.ds(pl.multiple_of(src * 8, 8), 8)],
            send_sem=a_send.at[ch, k - 1],
            recv_sem=a_recv.at[ch, k - 1],
            device_id={"gx": gx, "gy": gy, "dev": src},
            device_id_type=MESH,
        )

    for ch in range(CHUNKS):
        ins[ch].wait()
        for c in range(n_dev):
            total = None
            for a in range(2):
                lhs = dbuf[pl.ds(ch * per, per), a, :, pl.ds(256 * c, 256)].reshape(per * 16, 256)
                part = jnp.dot(lhs, wmat[a], preferred_element_type=F32)
                total = part if total is None else total + part
            pbuf[c, 0] = total[:, :128]
            pbuf[c, 1] = total[:, 128:]
            d = pbuf[c, 0, pl.ds(0, per * 8, stride=2), :] + pbuf[c, 1, pl.ds(1, per * 8, stride=2), :]
            dsend[c, pl.ds(ch * per, per)] = d.reshape(per, 8, 128)
        if ch == 0:
            pl.semaphore_wait(barrier, 23)
        for k in (2, 1, 3):
            a2a(ch, k).start()
        dens[pl.ds(ch * per, per), pl.ds(pl.multiple_of(me * 8, 8), 8)] = dsend[me, pl.ds(ch * per, per)]

    xsend = {
        ST: (lambda side: st.at[0 if side == 0 else nx - 1]),
        RH: (lambda side: fld.at[pl.ds(0, 2), 0 if side == 0 else nx - 1]),
        QH: (lambda side: fld.at[pl.ds(2, 2), 0 if side == 0 else nx - 1]),
    }
    xrecv = {ST: xr_st, RH: xr_r, QH: xr_q}
    ysend = {ST: ys_st, RH: ys_r, QH: ys_q}
    yrecv = {ST: yr_st, RH: yr_r, QH: yr_q}
    zsend = {ST: zs_st, RH: zs_r, QH: zs_q}
    zrecv = {ST: zr_st, RH: zr_r, QH: zr_q}
    spot = {"gx": (gx, n_gx), "gy": (gy, n_gy), "dev": (me, n_dev)}

    def face(e, axis, side):
        k = {"gx": 0, "gy": 2, "dev": 4}[axis] + side
        src = {
            "gx": lambda: xsend[e](side),
            "gy": lambda: ysend[e].at[side],
            "dev": lambda: zsend[e].at[side],
        }[axis]()
        dst = {"gx": xrecv, "gy": yrecv, "dev": zrecv}[axis][e].at[1 - side]
        pos, size = spot[axis]
        other = pos - 1 if side == 0 else pos + 1
        other = jnp.clip(other, 0, size - 1)
        target = {"gx": gx, "gy": gy, "dev": me}
        target[axis] = other
        copy = pltpu.make_async_remote_copy(
            src_ref=src, dst_ref=dst, send_sem=h_send.at[e, k], recv_sem=h_recv.at[e, k],
            device_id=target, device_id_type=MESH,
        )
        sends = pos > 0 if side == 0 else pos < size - 1
        gets = pos < size - 1 if side == 0 else pos > 0
        return copy, sends, gets

    def start_face(e, axis, side):
        copy, sends, _ = face(e, axis, side)

        @pl.when(sends)
        def _():
            copy.start()

    def wait_face(e, axis, side):
        copy, _, gets = face(e, axis, side)

        @pl.when(gets)
        def _():
            copy.wait_recv()

    iy = lax.broadcasted_iota(jnp.int32, (ny, nz), 0)
    iz = lax.broadcasted_iota(jnp.int32, (ny, nz), 1)
    last_y, last_z = iy == ny - 1, iz == nz - 1
    first_y, first_z = iy == 0, iz == 0
    zero = jnp.zeros((ny, nz), F32)

    def fold(v):
        return jnp.sum(v.reshape(ny // 8, 8, nz), axis=0)

    def lane_to(v, lane, at):
        return pltpu.roll(v, lax.rem(at - lane + 2 * nz, nz), 1)

    for c in fields_in:
        c.wait()
    for f in range(4):
        fld[f, nx] = zero
    st[nx] = zero

    def load_plane(i, carry):
        zlo, zhi, m0r, m0s = carry
        im, om = ibuf[i].astype(F32), obuf[i].astype(F32)
        r, s = im * lbuf[i], om
        diag[i] = GROUND + fbuf[i].astype(F32) + PORT * (im + om)
        fld[0, i] = r
        fld[1, i] = s
        for f, v in enumerate((r, s)):
            ys_r[0, f, pl.ds(i, 1), :] = v[0:1]
            ys_r[1, f, pl.ds(i, 1), :] = v[ny - 1 : ny]
            spot_z = iz == i + nx * f
            zlo = jnp.where(spot_z, lane_to(v, 0, i + nx * f), zlo)
            zhi = jnp.where(spot_z, lane_to(v, nz - 1, i + nx * f), zhi)
        return zlo, zhi, m0r + fold(r * r), m0s + fold(s * s)

    none = jnp.zeros((8, nz), F32)
    zlo, zhi, m0r, m0s = lax.fori_loop(0, nx, load_plane, (zero, zero, none, none))
    zs_r[0] = zlo
    zs_r[1] = zhi
    for axis in ("gx", "gy", "dev"):
        for side in range(2):
            start_face(RH, axis, side)

    zlo, zhi = zero, zero
    for ch in range(CHUNKS):
        for k in (2, 1, 3):
            a2a_in(ch, k).wait_recv()

        def stiff_plane(i, carry):
            zlo, zhi = carry
            d = dens[i]
            s = FLOOR + (1.0 - FLOOR) * d * d * d
            st[i] = s
            ys_st[0, pl.ds(i, 1), :] = s[0:1]
            ys_st[1, pl.ds(i, 1), :] = s[ny - 1 : ny]
            zlo = jnp.where(iz == i, lane_to(s, 0, i), zlo)
            zhi = jnp.where(iz == i, lane_to(s, nz - 1, i), zhi)
            return zlo, zhi

        zlo, zhi = lax.fori_loop(ch * per, (ch + 1) * per, stiff_plane, (zlo, zhi))
        if ch == 0:
            start_face(ST, "gx", 0)
    zs_st[0] = zlo
    zs_st[1] = zhi
    start_face(ST, "gx", 1)
    for axis in ("gy", "dev"):
        for side in range(2):
            start_face(ST, axis, side)

    def between(a, b):
        return 2.0 * a * b / (a + b)

    def inner_plane(i, carry):
        before_r, before_s = carry
        s = st[i]
        kx = between(s, st[i + 1])
        ky = between(s, jnp.where(last_y, 0.0, pltpu.roll(s, ny - 1, 0)))
        kz = between(s, jnp.where(last_z, 0.0, pltpu.roll(s, nz - 1, 1)))
        cx[i] = kx
        cy[i] = ky
        cz[i] = kz
        dg = diag[i]
        new = []
        for f, before in ((0, before_r), (1, before_s)):
            v = fld[f, i]
            fx = kx * (v - fld[f, i + 1])
            fy = ky * (v - pltpu.roll(v, ny - 1, 0))
            fz = kz * (v - pltpu.roll(v, nz - 1, 1))
            q = dg * v + (fx - before) + (fy - pltpu.roll(fy, 1, 0)) + (fz - pltpu.roll(fz, 1, 1))
            fld[2 + f, i] = q
            new.append(fx)
        return tuple(new)

    lax.fori_loop(0, nx, inner_plane, (zero, zero))

    for e in (RH, ST):
        for axis in ("gx", "gy", "dev"):
            for side in range(2):
                wait_face(e, axis, side)

    one_lane, two_lane = iz < nx, iz < 2 * nx
    for side in range(2):
        edge = 0 if side == 0 else nx - 1
        xcon[side] = between(st[edge], xr_st[side])
        ycon[side] = between(ys_st[side], yr_st[side])
        kz = between(zs_st[side] + jnp.where(one_lane, 0.0, 1.0), zr_st[side])
        zcon[side] = jnp.where(one_lane, kz, jnp.where(two_lane, pltpu.roll(kz, nx, 1), 0.0))
        for f in range(2):
            fld[2 + f, edge] += xcon[side] * (fld[f, edge] - xr_r[side, f])
            yflux[side, f] = ycon[side] * (ys_r[side, f] - yr_r[side, f])
        zflux[side] = zcon[side] * (zs_r[side] - zr_r[side])

    def edge_plane(i, carry):
        zlo, zhi, sums = carry
        sums = list(sums)
        for f in range(2):
            q = fld[2 + f, i]
            q += jnp.where(first_y, yflux[0, f, pl.ds(i, 1), :], 0.0)
            q += jnp.where(last_y, yflux[1, f, pl.ds(i, 1), :], 0.0)
            at = i + nx * f
            q += jnp.where(first_z, lane_to(zflux[0], at, 0), 0.0)
            q += jnp.where(last_z, lane_to(zflux[1], at, nz - 1), 0.0)
            fld[2 + f, i] = q
            ys_q[0, f, pl.ds(i, 1), :] = q[0:1]
            ys_q[1, f, pl.ds(i, 1), :] = q[ny - 1 : ny]
            zlo = jnp.where(iz == at, lane_to(q, 0, at), zlo)
            zhi = jnp.where(iz == at, lane_to(q, nz - 1, at), zhi)
            sums[f] += fold(fld[f, i] * q)
            sums[2 + f] += fold(q * q)
        return zlo, zhi, tuple(sums)

    zlo, zhi, sums12 = lax.fori_loop(0, nx, edge_plane, (zero, zero, (none,) * 4))
    zs_q[0] = zlo
    zs_q[1] = zhi
    for axis in ("gx", "gy", "dev"):
        for side in range(2):
            start_face(QH, axis, side)

    gprev[...] = jnp.zeros_like(gprev)

    def product_plane(i, carry):
        e_r, e_s = carry
        v = [fld[f, i] for f in range(4)]
        dg = diag[i]
        e_r += fold(dg * v[2] * v[2])
        e_s += fold(dg * v[3] * v[3])
        held = [None] * 4
        for axis in range(3):
            k = (cx, cy, cz)[axis][i]
            if axis == 0:
                d = [v[f] - fld[f, i + 1] for f in range(4)]
            elif axis == 1:
                d = [v[f] - pltpu.roll(v[f], ny - 1, 0) for f in range(4)]
            else:
                d = [v[f] - pltpu.roll(v[f], nz - 1, 1) for f in range(4)]
            kr, kq = k * d[0], k * d[2]
            ks, kp = k * d[1], k * d[3]
            e_r += fold(kq * d[2])
            e_s += fold(kp * d[3])
            for j, (a, b) in enumerate(((kr, ks), (kr, kp), (kq, ks), (kq, kp))):
                g = a * b
                if axis == 0:
                    held[j] = g + gprev[j]
                    gprev[j] = g
                elif axis == 1:
                    held[j] += g + pltpu.roll(g, 1, 0)
                else:
                    held[j] += g + pltpu.roll(g, 1, 1)
        for j in range(4):
            sarr[j, i] = held[j]
        return e_r, e_s

    e_r, e_s = lax.fori_loop(0, nx, product_plane, (none, none))

    for side in range(2):
        for axis in ("gx", "gy", "dev"):
            wait_face(QH, axis, side)

    dxs = [xcon[1] * (fld[2 + f, nx - 1] - xr_q[1, f]) * (fld[2 + f, nx - 1] - xr_q[1, f]) for f in range(2)]
    dys = [ycon[1] * (ys_q[1, f] - yr_q[1, f]) * (ys_q[1, f] - yr_q[1, f]) for f in range(2)]
    dz = zs_q[1] - zr_q[1]
    dz = zcon[1] * dz * dz
    e_r += fold(dxs[0] + dys[0] + jnp.where(one_lane, dz, 0.0))
    e_s += fold(dxs[1] + dys[1] + jnp.where(one_lane, 0.0, dz))

    for k, v in enumerate((m0r, m0s) + tuple(sums12) + (e_r, e_s)):
        ar1[id1, k : k + 1, :] = jnp.sum(v, axis=0, keepdims=True)

    def gather1(k):
        return pltpu.make_async_remote_copy(
            src_ref=ar1.at[id1], dst_ref=ar1.at[id1], send_sem=s_send.at[k], recv_sem=s_recv.at[k],
            device_id=peer1(k), device_id_type=MESH,
        )

    def gather1_in(k):
        src = lax.rem(id1 + 8 - k, 8)
        return pltpu.make_async_remote_copy(
            src_ref=ar1.at[src], dst_ref=ar1.at[src], send_sem=s_send.at[k], recv_sem=s_recv.at[k],
            device_id=peer1(8 - k), device_id_type=MESH,
        )

    def gather2(k):
        return pltpu.make_async_remote_copy(
            src_ref=ar2.at[id2], dst_ref=ar2.at[id2], send_sem=t_send.at[k], recv_sem=t_recv.at[k],
            device_id=peer2(k), device_id_type=MESH,
        )

    def gather2_in(k):
        src = lax.rem(id2 + 16 - k, 16)
        return pltpu.make_async_remote_copy(
            src_ref=ar2.at[src], dst_ref=ar2.at[src], send_sem=t_send.at[k], recv_sem=t_recv.at[k],
            device_id=peer2(16 - k), device_id_type=MESH,
        )

    for k in range(1, 8):
        gather1(k).start()

    for side in range(2):
        edge = 0 if side == 0 else nx - 1
        k = xcon[side]
        d = [k * (fld[f, edge] - (xr_r if f < 2 else xr_q)[side, f % 2]) for f in range(4)]
        for j, (a, b) in enumerate(((0, 1), (0, 3), (2, 1), (2, 3))):
            sarr[j, edge] += d[a] * d[b]
        k = ycon[side]
        d = [
            k * ((ys_r if f < 2 else ys_q)[side, f % 2] - (yr_r if f < 2 else yr_q)[side, f % 2])
            for f in range(4)
        ]
        for j, (a, b) in enumerate(((0, 1), (0, 3), (2, 1), (2, 3))):
            ysb[side, j] = d[a] * d[b]
        k = zcon[side]
        dr = k * (zs_r[side] - zr_r[side])
        dq = k * (zs_q[side] - zr_q[side])
        ds, dp = pltpu.roll(dr, nz - nx, 1), pltpu.roll(dq, nz - nx, 1)
        packed = zero
        for j, g in enumerate((dr * ds, dr * dp, dq * ds, dq * dp)):
            packed = jnp.where(iz // nx == j, g if j == 0 else pltpu.roll(g, nx * j, 1), packed)
        zsb[side] = packed

    def scale_plane(i, carry):
        d, s = dens[i], st[i]
        ratio = d / s
        scale = (-1.5 * (1.0 - FLOOR) * GAIN) * ratio * ratio
        for j in range(4):
            g = sarr[j, i]
            g += jnp.where(first_y, ysb[0, j, pl.ds(i, 1), :], 0.0)
            g += jnp.where(last_y, ysb[1, j, pl.ds(i, 1), :], 0.0)
            at = i + nx * j
            g += jnp.where(first_z, lane_to(zsb[0], at, 0), 0.0)
            g += jnp.where(last_z, lane_to(zsb[1], at, nz - 1), 0.0)
            sarr[j, i] = scale * g
        return carry

    lax.fori_loop(0, nx // 2, scale_plane, 0)

    for k in range(1, 8):
        gather1_in(k).wait_recv()
    part = ar1[0]
    for k in range(1, 8):
        part = part + ar1[k]
    ar2[id2] = part
    for k in range(1, 16):
        gather2(k).start()

    lax.fori_loop(nx // 2, nx, scale_plane, 0)

    for k in range(1, 16):
        gather2_in(k).wait_recv()
    whole = ar2[0]
    for k in range(1, 16):
        whole = whole + ar2[k]

    coef[...] = jnp.broadcast_to(jnp.sum(whole, axis=1, keepdims=True), coef.shape)
    m0, m1, m2, m3 = (coef[pl.ds(2 * k, 2), :] for k in range(4))
    step0 = m0 / (m1 + TINY)
    rr1 = jnp.maximum(m0 - 2.0 * step0 * m1 + step0 * step0 * m2, 0.0)
    beta = rr1 / (m0 + TINY)
    r_a_r = m1 - 2.0 * step0 * m2 + step0 * step0 * m3
    r_a_d = m1 - step0 * m2
    d_a_d = r_a_r + 2.0 * beta * r_a_d + beta * beta * m1
    step1 = jnp.minimum(rr1 / (jnp.maximum(d_a_d, 0.0) + TINY), MAX_STEP)
    c0 = step0 + step1 * (1.0 + beta)
    c1 = -step0 * step1
    mix = [
        c0[0:1] * c0[1:2],
        c0[0:1] * c1[1:2],
        c1[0:1] * c0[1:2],
        c1[0:1] * c1[1:2],
    ]

    rows = per * 8

    def back(ch, k):
        dst = lax.rem(me + k, n_dev)
        return pltpu.make_async_remote_copy(
            src_ref=bsend.at[dst, pl.ds(ch * rows, rows)],
            dst_ref=out.at[me, pl.ds(ch * rows, rows)],
            send_sem=b_send.at[ch, k - 1],
            recv_sem=b_recv.at[ch, k - 1],
            device_id={"gx": gx, "gy": gy, "dev": dst},
            device_id_type=MESH,
        )

    def back_in(ch, k):
        src = lax.rem(me + n_dev - k, n_dev)
        return pltpu.make_async_remote_copy(
            src_ref=bsend.at[src, pl.ds(ch * rows, rows)],
            dst_ref=out.at[src, pl.ds(ch * rows, rows)],
            send_sem=b_send.at[ch, k - 1],
            recv_sem=b_recv.at[ch, k - 1],
            device_id={"gx": gx, "gy": gy, "dev": src},
            device_id_type=MESH,
        )

    for ch in range(CHUNKS):

        def pair_planes(p, carry):
            v = None
            for j in range(4):
                part = mix[j] * sarr[j, pl.ds(2 * p, 2)]
                v = part if v is None else v + part
            for d in range(n_dev):
                two = v[:, 8 * d : 8 * d + 8, :].reshape(16, nz)
                bsend[d, pl.ds(pl.multiple_of(p * 16, 16), 16), :] = two.astype(BF16)
            return carry

        lax.fori_loop(ch * per // 2, (ch + 1) * per // 2, pair_planes, 0)
        for k in (2, 1, 3):
            back(ch, k).start()
    own = pltpu.make_async_copy(bsend.at[me], out.at[me], o_sem)
    own.start()

    for ch in range(CHUNKS):
        for k in range(1, 4):
            a2a(ch, k).wait_send()
    for e in (ST, RH, QH):
        for axis in ("gx", "gy", "dev"):
            for side in range(2):
                copy, sends, _ = face(e, axis, side)

                @pl.when(sends)
                def _():
                    copy.wait_send()

    for k in range(1, 8):
        gather1(k).wait_send()
    for k in range(1, 16):
        gather2(k).wait_send()
    own.wait()
    for ch in range(CHUNKS):
        for k in (2, 1, 3):
            back(ch, k).wait_send()
            back_in(ch, k).wait_recv()


def expand_kernel(offs_hbm, wts_hbm, s_hbm, o_hbm, offs, wts, sbuf, obuf, wexp, tap_sem, i_sem, o_sem):
    n_dev, rows, nz = sbuf.shape
    nx = rows // 8
    per = nx // STEPS

    def fetch(c):
        part = pl.ds(c * per * 8, per * 8)
        return pltpu.make_async_copy(s_hbm.at[:, part], sbuf.at[:, part], i_sem.at[c])

    def store(c, l):
        return pltpu.make_async_copy(
            obuf.at[l, pl.ds(c * 2 * per, 2 * per)],
            o_hbm.at[pl.ds(c * 2 * per, 2 * per), :, pl.ds(128 * l, 128)],
            o_sem.at[c, l],
        )

    taps_in = [
        pltpu.make_async_copy(offs_hbm, offs, tap_sem.at[0]),
        pltpu.make_async_copy(wts_hbm, wts, tap_sem.at[1]),
    ]
    for c in taps_in:
        c.start()
    for c in range(STEPS):
        fetch(c).start()
    for c in taps_in:
        c.wait()
    kid = child_rows(offs, wts, 256)
    row_i = lax.broadcasted_iota(jnp.int32, (128, 256), 0)
    col_i = lax.broadcasted_iota(jnp.int32, (128, 256), 1)
    paired = col_i // 2 == row_i
    even = lax.rem(col_i, 2) == 0
    for ab in range(4):
        e = jnp.where(even, kid[2 * ab], kid[2 * ab + 1])
        wexp[ab] = jnp.where(paired, e, 0.0).astype(BF16)

    for c in range(STEPS):
        fetch(c).wait()
        for d in range(n_dev):
            lhs = sbuf[d, pl.ds(c * per * 8, per * 8)]
            for a in range(2):
                for b in range(2):
                    t = jnp.dot(lhs, wexp[2 * a + b], preferred_element_type=F32)
                    for i in range(per):
                        for h in range(2):
                            obuf[2 * d + h, 2 * (c * per + i) + a, pl.ds(b, 8, stride=2), :] = t[
                                8 * i : 8 * i + 8, 128 * h : 128 * h + 128
                            ]
            for h in range(2):
                store(c, 2 * d + h).start()
    for c in range(STEPS):
        for l in range(2 * n_dev):
            store(c, l).wait()


def solution(mesh):
    n_gx, n_gy, n_dev = mesh.shape["gx"], mesh.shape["gy"], mesh.shape["dev"]

    def body(design, tap_offsets, tap_weights, input_load, input_mask, output_mask, fixed_mask):
        nx, ny, nz = input_load.shape
        cell = (nx, ny, nz)
        plane = (ny, nz)
        hbm = pl.BlockSpec(memory_space=pl.ANY)
        vm = lambda *shape: pltpu.VMEM(shape, F32)
        dma = lambda *shape: pltpu.SemaphoreType.DMA(shape)
        scratch = [
            pltpu.VMEM((nx, 2, 16, 1024), BF16),
            vm(*cell),
            pltpu.VMEM(cell, jnp.int32),
            pltpu.VMEM(cell, jnp.int32),
            pltpu.VMEM(cell, jnp.int32),
            pltpu.VMEM((2, 256, 256), BF16),
            vm(n_dev, 2, nx // CHUNKS * 16, 128),
            vm(n_dev, nx, 8, nz),
            vm(*cell),
            vm(nx + 1, *plane),
            vm(4, nx + 1, *plane),
            vm(*cell),
            vm(*cell), vm(*cell), vm(*cell),
            vm(4, *cell),
            vm(4, *plane),
            vm(2, *plane), vm(2, 2, *plane), vm(2, 2, *plane),
            vm(2, nx, nz), vm(2, 2, nx, nz), vm(2, 2, nx, nz),
            vm(2, nx, nz), vm(2, 2, nx, nz), vm(2, 2, nx, nz),
            vm(2, *plane), vm(2, *plane), vm(2, *plane),
            vm(2, *plane), vm(2, *plane), vm(2, *plane),
            vm(2, 2, nx, nz), vm(2, *plane), vm(2, *plane), vm(2, nx, nz), vm(2, *plane),
            vm(2, 4, nx, nz), vm(2, *plane),
            vm(8, 8, 128), vm(16, 8, 128), vm(8, 128),
            pltpu.VMEM((n_dev, nx * 8, nz), BF16),
            pltpu.SMEM((3, 16), jnp.int32), pltpu.SMEM((16,), F32), dma(2),
            dma(CHUNKS + 4), dma(CHUNKS, 3), dma(CHUNKS, 3), dma(3, 6), dma(3, 6),
            dma(8), dma(8), dma(16), dma(16), dma(CHUNKS, 3), dma(CHUNKS, 3), pltpu.SemaphoreType.DMA,
        ]
        returned = pl.pallas_call(
            functools.partial(step_kernel, n_gx, n_gy, n_dev),
            out_shape=jax.ShapeDtypeStruct((n_dev, nx * 8, nz), BF16),
            in_specs=[hbm] * 7,
            out_specs=hbm,
            scratch_shapes=scratch,
            compiler_params=pltpu.CompilerParams(
                collective_id=0, has_side_effects=True
            ),
            name="step",
        )(
            design.reshape(nx, 2, 16, 1024), input_load, input_mask, output_mask, fixed_mask,
            tap_offsets.T, tap_weights,
        )
        return pl.pallas_call(
            expand_kernel,
            out_shape=jax.ShapeDtypeStruct(design.shape, F32),
            in_specs=[hbm, hbm, hbm],
            out_specs=hbm,
            scratch_shapes=[
                pltpu.SMEM((3, 16), jnp.int32), pltpu.SMEM((16,), F32),
                pltpu.VMEM((n_dev, nx * 8, nz), BF16),
                vm(2 * n_dev, 2 * nx, 16, 128),
                pltpu.VMEM((4, 128, 256), BF16),
                dma(2),
                dma(STEPS),
                dma(STEPS, 2 * n_dev),
            ],
            name="expand",
        )(tap_offsets.T, tap_weights, returned)

    block = P("gx", "gy", "dev")
    owner = P("gx", ("gy", "dev"), None)
    return jax.shard_map(
        body, mesh=mesh,
        in_specs=(owner, P(), P(), block, block, block, block),
        out_specs=owner,
        check_vma=False,
    )
```

```python
import functools

import jax
import jax.numpy as jnp
from jax import lax
from jax.experimental import pallas as pl
from jax.experimental.pallas import tpu as pltpu
from jax.sharding import PartitionSpec as P

MESH = pl.DeviceIdType.MESH

FLOOR = 0.01
GROUND = 0.1
PORT = 0.5
GAIN = 64.0
TINY = 1e-06
MAX_STEP = 10.0

CODE = 32000.0
ORDER = (0, 3, 1, 2)
CHUNKS = len(ORDER)
STEPS = 4
F32 = jnp.float32
BF16 = jnp.bfloat16
I16 = jnp.int16
I32 = jnp.int32

ST, RH, QH = 0, 1, 2


def child_rows(offs, wts, lanes):
    taps = wts.shape[0]
    total = wts[0]
    for t in range(1, taps):
        total = total + wts[t]
    sums = [jnp.float32(0.0)] * 8
    for t in range(taps):
        code = offs[0, t] * 4 + offs[1, t] * 2 + offs[2, t]
        for c in range(8):
            sums[c] = sums[c] + jnp.where(code == c, wts[t], jnp.float32(0.0))
    below = jnp.full((1, lanes), total, F32)
    return [jnp.full((1, lanes), s, F32) / below for s in sums]


def between(a, b):
    return 2.0 * a * b / (a + b)


def step_kernel(
    n_gx, n_gy, n_dev,
    design, load, imask, omask, fmask, offs_hbm, wts_hbm,
    out, dloc,
    dbuf, lbuf, ibuf, obuf, fbuf,
    wmat, pbuf, dsend, isend, irecv, st, rs, qq, diag, dzu, dzl,
    cx, cy, czu, czl, sarr, gprev,
    xr_st, xr_r, xr_q,
    ys_st, ys_r, ys_q, yr_st, yr_r, yr_q,
    zs_st, zs_r, zs_q, zr_st, zr_r, zr_q,
    yflux, zflux, zcon, ycon, xcon, zhal,
    ysb, zsb,
    ar1, ar2, coef, bsend,
    offs, wts, tap_sem, in_sem, a_send, a_recv, h_send, h_recv, s_send, s_recv, t_send, t_recv,
    b_send, b_recv, o_sem, ready,
):
    gx = lax.axis_index("gx")
    gy = lax.axis_index("gy")
    me = lax.axis_index("dev")
    nx, ny, nz = lbuf.shape
    per = nx // CHUNKS
    rows = per * 8
    core = lax.rem(gy, 2)
    half = gy // 2
    ypos = lax.rem(gx, 4)
    zpos = gx // 4 * 2 + half

    taps_in = [
        pltpu.make_async_copy(offs_hbm, offs, tap_sem.at[0]),
        pltpu.make_async_copy(wts_hbm, wts, tap_sem.at[1]),
    ]
    for c in taps_in:
        c.start()
    ins = {}
    for ch in ORDER:
        c = pltpu.make_async_copy(
            design.at[pl.ds(ch * per, per)], dbuf.at[pl.ds(ch * per, per)], in_sem.at[ch]
        )
        c.start()
        ins[ch] = c
    fields_in = []
    for k, (a, b) in enumerate(((load, lbuf), (imask, ibuf), (omask, obuf), (fmask, fbuf))):
        c = pltpu.make_async_copy(a, b, in_sem.at[CHUNKS + k])
        c.start()
        fields_in.append(c)

    for ref in (xr_st, xr_r, xr_q, yr_st, yr_r, yr_q, zr_st, zr_r, zr_q):
        ref[...] = jnp.zeros_like(ref)

    id1 = me * 2 + core
    id2 = gx * 2 + half

    def peer1(k):
        other = lax.rem(id1 + k, 8)
        return {"gx": gx, "gy": half * 2 + lax.rem(other, 2), "dev": other // 2}

    def peer2(k):
        other = lax.rem(id2 + k, 16)
        return {"gx": other // 2, "gy": lax.rem(other, 2) * 2 + core, "dev": me}

    def peer_y(k):
        return {"gx": gx // 4 * 4 + lax.rem(ypos + k, 4), "gy": gy, "dev": me}

    def peer_z(k):
        z = lax.rem(zpos + k, 4)
        return {"gx": z // 2 * 4 + ypos, "gy": lax.rem(z, 2) * 2 + core, "dev": me}

    barrier = pltpu.get_barrier_semaphore()
    near = [peer1(k) for k in range(1, 8)] + [peer_y(k) for k in range(1, 4)]
    near += [peer_z(k) for k in range(1, 4)] + [{"gx": gx, "gy": n_gy - 1 - gy, "dev": me}]
    for peer in near:
        pl.semaphore_signal(barrier, inc=1, device_id=peer, device_id_type=MESH)

    for c in taps_in:
        c.wait()
    kid = child_rows(offs, wts, 256)
    row_i = lax.broadcasted_iota(I32, (256, 256), 0)
    col_i = lax.broadcasted_iota(I32, (256, 256), 1)
    paired = row_i // 2 == lax.rem(col_i, 128)
    even = lax.rem(row_i, 2) == 0
    left = col_i < 128
    for a in range(2):
        e = jnp.where(
            even,
            jnp.where(left, kid[4 * a], kid[4 * a + 2]),
            jnp.where(left, kid[4 * a + 1], kid[4 * a + 3]),
        )
        wmat[a] = jnp.where(paired, e, 0.0).astype(BF16)

    def a2a(ch, k):
        dst = lax.rem(me + k, n_dev)
        part = pl.ds(ch * rows, rows)
        return pltpu.make_async_remote_copy(
            src_ref=isend.at[dst, part],
            dst_ref=irecv.at[me, part],
            send_sem=a_send.at[ch, k - 1],
            recv_sem=a_recv.at[ch, k - 1],
            device_id={"gx": gx, "gy": gy, "dev": dst},
            device_id_type=MESH,
        )

    def a2a_in(ch, k):
        src = lax.rem(me + n_dev - k, n_dev)
        part = pl.ds(ch * rows, rows)
        return pltpu.make_async_remote_copy(
            src_ref=isend.at[src, part],
            dst_ref=irecv.at[src, part],
            send_sem=a_send.at[ch, k - 1],
            recv_sem=a_recv.at[ch, k - 1],
            device_id={"gx": gx, "gy": gy, "dev": src},
            device_id_type=MESH,
        )

    for ch in ORDER:
        ins[ch].wait()
        part = pl.ds(ch * rows, rows)
        for c in range(n_dev):
            total = None
            for a in range(2):
                lhs = dbuf[pl.ds(ch * per, per), a, :, pl.ds(256 * c, 256)].reshape(per * 16, 256)
                add = jnp.dot(lhs, wmat[a], preferred_element_type=F32)
                total = add if total is None else total + add
            pbuf[c, 0] = total[:, :128]
            pbuf[c, 1] = total[:, 128:]
            d = pbuf[c, 0, pl.ds(0, rows, stride=2), :] + pbuf[c, 1, pl.ds(1, rows, stride=2), :]
            dsend[c, part] = d
            isend[c, part] = (d * CODE + 0.5).astype(I32).astype(I16)
        if ch == ORDER[0]:
            pl.semaphore_wait(barrier, len(near))
        for k in (2, 1, 3):
            a2a(ch, k).start()
        irecv[me, part] = isend[me, part]
    keep = pltpu.make_async_copy(dsend, dloc, o_sem.at[1])
    keep.start()
    for k in range(1, 4):
        pl.semaphore_signal(ready, inc=1, device_id=peer_y(k), device_id_type=MESH)

    def plane_of(i):
        return pl.ds(pl.multiple_of((i + 1) * ny, ny), ny)

    def xsend(e, side):
        where = plane_of(0 if side == 0 else nx - 1)
        if e == ST:
            return st.at[where]
        return (rs if e == RH else qq).at[:, where]

    xrecv = {ST: xr_st, RH: xr_r, QH: xr_q}
    ysend = {ST: ys_st, RH: ys_r, QH: ys_q}
    yrecv = {ST: yr_st, RH: yr_r, QH: yr_q}
    zsend = {ST: zs_st, RH: zs_r, QH: zs_q}
    zrecv = {ST: zr_st, RH: zr_r, QH: zr_q}
    spot = {"gx": (gx, n_gx), "gy": (gy, n_gy), "dev": (me, n_dev)}

    def face(e, axis, side):
        k = {"gx": 0, "gy": 2, "dev": 4}[axis] + side
        if axis == "gx":
            src, dst = xsend(e, side), xrecv[e].at[1 - side]
        elif axis == "gy":
            src, dst = ysend[e].at[side], yrecv[e].at[1 - side]
        else:
            src, dst = zsend[e], zrecv[e].at[1 - side]
        pos, size = spot[axis]
        target = {"gx": gx, "gy": gy, "dev": me}
        target[axis] = jnp.clip(pos - 1 if side == 0 else pos + 1, 0, size - 1)
        copy = pltpu.make_async_remote_copy(
            src_ref=src, dst_ref=dst, send_sem=h_send.at[e, k], recv_sem=h_recv.at[e, k],
            device_id=target, device_id_type=MESH,
        )
        sends = pos > 0 if side == 0 else pos < size - 1
        gets = pos < size - 1 if side == 0 else pos > 0
        return copy, sends, gets

    def start_face(e, axis, side):
        copy, sends, _ = face(e, axis, side)

        @pl.when(sends)
        def _():
            copy.start()

    def wait_face(e, axis, side):
        copy, _, gets = face(e, axis, side)

        @pl.when(gets)
        def _():
            copy.wait_recv()

    def end_face(e, axis, side):
        copy, sends, _ = face(e, axis, side)

        @pl.when(sends)
        def _():
            copy.wait_send()

    faces = [(axis, side) for axis in ("gx", "gy", "dev") for side in range(2)]

    iy = lax.broadcasted_iota(I32, (ny, nz), 0)
    iz = lax.broadcasted_iota(I32, (ny, nz), 1)
    first_y, last_y = iy == 0, iy == ny - 1
    first_z, last_z = iz == 0, iz == nz - 1
    ends_z = jnp.logical_or(first_z, last_z)
    key = ((iz + 1) // 2) % 64
    low_lane = lax.rem(iz, 2) == 0
    field0 = key < 32
    top8 = lax.broadcasted_iota(I32, (8, nz), 0) == 0
    end8 = lax.broadcasted_iota(I32, (8, nz), 0) == 7
    zero = jnp.zeros((ny, nz), F32)
    none = jnp.zeros((8, nz), F32)

    def fold(v):
        return jnp.sum(v.reshape(ny // 8, 8, nz), axis=0)

    def pack(into, v, f, i):
        return jnp.where(key == 32 * f + i, pltpu.roll(v, 64 * f + 2 * i, 1), into)

    def unpack(packed, f, i):
        by = 2 * nz - 64 * f - 2 * i
        by = by % nz if isinstance(i, int) else lax.rem(by, nz)
        return jnp.where(ends_z, pltpu.roll(packed, by, 1), 0.0)

    def add_rows(v, low, high):
        return jnp.concatenate(
            [v[:8] + jnp.where(top8, low, 0.0), v[8:-8], v[-8:] + jnp.where(end8, high, 0.0)], axis=0
        )

    def z_halo(ref):
        return jnp.where(low_lane, pltpu.roll(ref[0], 1, 1), pltpu.roll(ref[1], nz - 1, 1))

    for c in fields_in:
        c.wait()
    for ends in (pl.ds(0, ny), pl.ds((nx + 1) * ny, ny)):
        st[ends] = zero
        cy[ends] = zero
        for f in range(2):
            rs[f, ends] = zero
            qq[f, ends] = zero

    def load_plane(i, carry):
        zpack, m0r, m0s = carry
        im, om = ibuf[i].astype(F32), obuf[i].astype(F32)
        r, s = im * lbuf[i], om
        diag[i] = GROUND + fbuf[i].astype(F32) + PORT * (im + om)
        for f, v in enumerate((r, s)):
            rs[f, plane_of(i)] = v
            dzu[f, i] = v - pltpu.roll(v, nz - 1, 1)
            dzl[f, i] = v - pltpu.roll(v, 1, 1)
            ys_r[0, f, pl.ds(i, 1), :] = v[0:1]
            ys_r[1, f, pl.ds(i, 1), :] = v[ny - 1 : ny]
            zpack = pack(zpack, v, f, i)
        return zpack, m0r + fold(r * r), m0s + fold(s * s)

    zpack, m0r, m0s = lax.fori_loop(0, nx, load_plane, (zero, none, none), unroll=2)
    zs_r[...] = zpack
    pl.semaphore_wait(ready, 3)
    for axis, side in faces:
        start_face(RH, axis, side)

    def stiff_pair(p, zpack):
        d = [
            irecv[src, pl.ds(pl.multiple_of(16 * p, 16), 16)].astype(I32).astype(F32) * (1.0 / CODE)
            for src in range(n_dev)
        ]
        s = [FLOOR + (1.0 - FLOOR) * v * v * v for v in d]
        for h in range(2):
            i = 2 * p + h
            v = jnp.concatenate([t[8 * h : 8 * h + 8] for t in s], axis=0)
            st[plane_of(i)] = v
            ys_st[0, pl.ds(i, 1), :] = v[0:1]
            ys_st[1, pl.ds(i, 1), :] = v[ny - 1 : ny]
            zpack = pack(zpack, v, 0, i)
        return zpack

    zpack = zero
    for ch in ORDER:
        for k in (1, 3, 2):
            a2a_in(ch, k).wait_recv()
        zpack = lax.fori_loop(ch * per // 2, (ch + 1) * per // 2, stiff_pair, zpack, unroll=2)
        if ch == 0:
            start_face(ST, "gx", 0)
        if ch == CHUNKS - 1:
            start_face(ST, "gx", 1)
    zs_st[...] = jnp.where(field0, zpack, pltpu.roll(zpack, nz // 2, 1))
    for axis, side in faces[2:]:
        start_face(ST, axis, side)

    def inner_plane(i, carry):
        at = pl.multiple_of((i + 1) * ny, ny)
        here, after, up, down = pl.ds(at, ny), pl.ds(at + ny, ny), pl.ds(at + 1, ny), pl.ds(at - 1, ny)
        s = st[here]
        kx = between(s, st[after])
        kyu = between(s, jnp.where(last_y, 0.0, st[up]))
        kyl = between(s, jnp.where(first_y, 0.0, st[down]))
        kzu = between(s, jnp.where(last_z, 0.0, pltpu.roll(s, nz - 1, 1)))
        kzl = between(s, jnp.where(first_z, 0.0, pltpu.roll(s, 1, 1)))
        cx[i] = kx
        cy[here] = kyu
        czu[i] = kzu
        czl[i] = kzl
        dg = diag[i]
        new = []
        for f in range(2):
            v = rs[f, here]
            fx = kx * (v - rs[f, after])
            q = dg * v + (fx - carry[f])
            q += kyu * (v - rs[f, up]) + kyl * (v - rs[f, down])
            q += kzu * dzu[f, i] + kzl * dzl[f, i]
            qq[f, here] = q
            new.append(fx)
        return tuple(new)

    lax.fori_loop(0, nx, inner_plane, (zero, zero), unroll=2)

    for e in (RH, ST):
        for axis, side in faces:
            wait_face(e, axis, side)

    kz = between(zs_st[...], z_halo(zr_st))
    zcon[...] = kz
    zhal[0] = zs_r[...] - z_halo(zr_r)
    zflux[...] = kz * zhal[0]
    for side in range(2):
        edge = plane_of(0 if side == 0 else nx - 1)
        xcon[side] = between(st[edge], xr_st[side])
        ycon[side] = between(ys_st[side], yr_st[side])
        for f in range(2):
            qq[f, edge] += xcon[side] * (rs[f, edge] - xr_r[side, f])
            yflux[side, f] = ycon[side] * (ys_r[side, f] - yr_r[side, f])

    def edge_plane(i, carry):
        zpack, sums = carry
        sums = list(sums)
        here = plane_of(i)
        for f in range(2):
            q = qq[f, here] + unpack(zflux[...], f, i)
            q = add_rows(q, yflux[0, f, pl.ds(i, 1), :], yflux[1, f, pl.ds(i, 1), :])
            qq[f, here] = q
            ys_q[0, f, pl.ds(i, 1), :] = q[0:1]
            ys_q[1, f, pl.ds(i, 1), :] = q[ny - 1 : ny]
            zpack = pack(zpack, q, f, i)
            sums[f] += fold(rs[f, here] * q)
            sums[2 + f] += fold(q * q)
        return zpack, tuple(sums)

    carry = (zero, (none,) * 4)
    carry = edge_plane(0, carry)
    start_face(QH, "gx", 0)
    carry = edge_plane(nx - 1, carry)
    start_face(QH, "gx", 1)
    zpack, sums12 = lax.fori_loop(1, nx - 1, edge_plane, carry, unroll=2)
    zs_q[...] = zpack
    for axis, side in faces[2:]:
        start_face(QH, axis, side)

    gprev[...] = jnp.zeros_like(gprev)
    forms = ((0, 1), (0, 3), (2, 1), (2, 3))

    def product_plane(i, carry):
        e_r, e_s = carry
        at = pl.multiple_of((i + 1) * ny, ny)
        here, after, up, down = pl.ds(at, ny), pl.ds(at + ny, ny), pl.ds(at + 1, ny), pl.ds(at - 1, ny)

        def get(where):
            return [rs[0, where], rs[1, where], qq[0, where], qq[1, where]]

        v = get(here)
        dg = diag[i]
        e_r += fold(dg * v[2] * v[2])
        e_s += fold(dg * v[3] * v[3])
        q_up = [pltpu.roll(v[f], nz - 1, 1) for f in (2, 3)]
        q_down = [pltpu.roll(v[f], 1, 1) for f in (2, 3)]

        def diffs(o):
            return [a - b for a, b in zip(v, o)]

        d = diffs(get(after))
        k = cx[i]
        t = [k * a for a in d]
        e_r += fold(t[2] * d[2])
        e_s += fold(t[3] * d[3])
        held = []
        for j, (a, b) in enumerate(forms):
            g = t[a] * t[b]
            held.append(g + gprev[j])
            gprev[j] = g
        sides = (
            (True, cy[here], lambda: diffs(get(up))),
            (False, cy[down], lambda: diffs(get(down))),
            (True, czu[i], lambda: [dzu[0, i], dzu[1, i], v[2] - q_up[0], v[3] - q_up[1]]),
            (False, czl[i], lambda: [dzl[0, i], dzl[1, i], v[2] - q_down[0], v[3] - q_down[1]]),
        )
        for own, k, make in sides:
            d = make()
            t = [k * a for a in d]
            if own:
                e_r += fold(t[2] * d[2])
                e_s += fold(t[3] * d[3])
            for j, (a, b) in enumerate(forms):
                held[j] += t[a] * t[b]
        for j in range(4):
            sarr[j, i] = held[j]
        return e_r, e_s

    e_r, e_s = lax.fori_loop(0, nx, product_plane, (none, none))

    for axis, side in faces:
        wait_face(QH, axis, side)

    zhal[1] = zs_q[...] - z_halo(zr_q)
    dz = zcon[...] * zhal[1] * zhal[1]
    parts = []
    for f in range(2):
        dx = qq[f, plane_of(nx - 1)] - xr_q[1, f]
        dy = ys_q[1, f] - yr_q[1, f]
        own = jnp.logical_and(jnp.logical_not(low_lane), field0 if f == 0 else jnp.logical_not(field0))
        parts.append(fold(xcon[1] * dx * dx + ycon[1] * dy * dy + jnp.where(own, dz, 0.0)))
    e_r += parts[0]
    e_s += parts[1]

    for k, v in enumerate((m0r, m0s) + tuple(sums12) + (e_r, e_s)):
        ar1[id1, k : k + 1, :] = jnp.sum(v, axis=0, keepdims=True)

    def gather1(k):
        return pltpu.make_async_remote_copy(
            src_ref=ar1.at[id1], dst_ref=ar1.at[id1], send_sem=s_send.at[k], recv_sem=s_recv.at[k],
            device_id=peer1(k), device_id_type=MESH,
        )

    def gather1_in(k):
        src = lax.rem(id1 + 8 - k, 8)
        return pltpu.make_async_remote_copy(
            src_ref=ar1.at[src], dst_ref=ar1.at[src], send_sem=s_send.at[k], recv_sem=s_recv.at[k],
            device_id=peer1(8 - k), device_id_type=MESH,
        )

    def gather2(k):
        return pltpu.make_async_remote_copy(
            src_ref=ar2.at[id2], dst_ref=ar2.at[id2], send_sem=t_send.at[k], recv_sem=t_recv.at[k],
            device_id=peer2(k), device_id_type=MESH,
        )

    def gather2_in(k):
        src = lax.rem(id2 + 16 - k, 16)
        return pltpu.make_async_remote_copy(
            src_ref=ar2.at[src], dst_ref=ar2.at[src], send_sem=t_send.at[k], recv_sem=t_recv.at[k],
            device_id=peer2(16 - k), device_id_type=MESH,
        )

    for k in range(1, 8):
        gather1(k).start()

    for side in range(2):
        edge = plane_of(0 if side == 0 else nx - 1)
        k = xcon[side]
        d = [k * (rs[f, edge] - xr_r[side, f]) for f in range(2)]
        d += [k * (qq[f, edge] - xr_q[side, f]) for f in range(2)]
        for j, (a, b) in enumerate(forms):
            sarr[j, 0 if side == 0 else nx - 1] += d[a] * d[b]
        k = ycon[side]
        d = [k * (ys_r[side, f] - yr_r[side, f]) for f in range(2)]
        d += [k * (ys_q[side, f] - yr_q[side, f]) for f in range(2)]
        for j, (a, b) in enumerate(forms):
            ysb[side, j] = d[a] * d[b]
    dr, dq = zcon[...] * zhal[0], zcon[...] * zhal[1]
    dr2, dq2 = pltpu.roll(dr, nz // 2, 1), pltpu.roll(dq, nz // 2, 1)
    zsb[0] = jnp.where(field0, dr * dr2, dq * dq2)
    zsb[1] = dr * dq2
    packed_at = ((0, 0), (1, 0), (1, 1), (0, 1))

    def scale_plane(i, carry):
        s = st[plane_of(i)]
        scale = 1.0 / (s * s)
        for j in range(4):
            buf, f = packed_at[j]
            g = sarr[j, i] + unpack(zsb[buf], f, i)
            g = add_rows(g, ysb[0, j, pl.ds(i, 1), :], ysb[1, j, pl.ds(i, 1), :])
            sarr[j, i] = scale * g
        return carry

    lax.fori_loop(0, nx // 2, scale_plane, 0, unroll=2)

    for k in range(1, 8):
        gather1_in(k).wait_recv()
    part = ar1[0]
    for k in range(1, 8):
        part = part + ar1[k]
    ar2[id2] = part
    for k in range(1, 16):
        gather2(k).start()

    lax.fori_loop(nx // 2, nx, scale_plane, 0, unroll=2)

    keep.wait()
    for ch in range(CHUNKS):
        for k in range(1, 4):
            a2a(ch, k).wait_send()
    for e in (ST, RH, QH):
        for axis, side in faces:
            end_face(e, axis, side)
    for k in range(1, 8):
        gather1(k).wait_send()

    for k in range(1, 16):
        gather2_in(k).wait_recv()
    whole = ar2[0]
    for k in range(1, 16):
        whole = whole + ar2[k]

    coef[...] = jnp.broadcast_to(jnp.sum(whole, axis=1, keepdims=True), coef.shape)
    m0, m1, m2, m3 = (coef[pl.ds(2 * k, 2), :] for k in range(4))
    step0 = m0 / (m1 + TINY)
    rr1 = jnp.maximum(m0 - 2.0 * step0 * m1 + step0 * step0 * m2, 0.0)
    beta = rr1 / (m0 + TINY)
    r_a_r = m1 - 2.0 * step0 * m2 + step0 * step0 * m3
    r_a_d = m1 - step0 * m2
    d_a_d = r_a_r + 2.0 * beta * r_a_d + beta * beta * m1
    step1 = jnp.minimum(rr1 / (jnp.maximum(d_a_d, 0.0) + TINY), MAX_STEP)
    c0 = step0 + step1 * (1.0 + beta)
    c1 = -step0 * step1
    mix = [c0[0:1] * c0[1:2], c0[0:1] * c1[1:2], c1[0:1] * c0[1:2], c1[0:1] * c1[1:2]]

    def back(ch, k):
        dst = lax.rem(me + k, n_dev)
        part = pl.ds(ch * rows, rows)
        return pltpu.make_async_remote_copy(
            src_ref=bsend.at[dst, part],
            dst_ref=out.at[me, part],
            send_sem=b_send.at[ch, k - 1],
            recv_sem=b_recv.at[ch, k - 1],
            device_id={"gx": gx, "gy": gy, "dev": dst},
            device_id_type=MESH,
        )

    def back_in(ch, k):
        src = lax.rem(me + n_dev - k, n_dev)
        part = pl.ds(ch * rows, rows)
        return pltpu.make_async_remote_copy(
            src_ref=bsend.at[src, part],
            dst_ref=out.at[src, part],
            send_sem=b_send.at[ch, k - 1],
            recv_sem=b_recv.at[ch, k - 1],
            device_id={"gx": gx, "gy": gy, "dev": src},
            device_id_type=MESH,
        )

    def pair_planes(p, carry):
        v = None
        for j in range(4):
            add = mix[j] * sarr[j, pl.ds(2 * p, 2)]
            v = add if v is None else v + add
        for d in range(n_dev):
            two = v[:, 8 * d : 8 * d + 8, :].reshape(16, nz)
            bsend[d, pl.ds(pl.multiple_of(p * 16, 16), 16), :] = two.astype(BF16)
        return carry

    for ch in range(CHUNKS):
        lax.fori_loop(ch * per // 2, (ch + 1) * per // 2, pair_planes, 0, unroll=2)
        for k in (2, 1, 3):
            back(ch, k).start()
    own = pltpu.make_async_copy(bsend.at[me], out.at[me], o_sem.at[0])
    own.start()
    for k in range(1, 16):
        gather2(k).wait_send()
    own.wait()
    for ch in range(CHUNKS):
        for k in (2, 1, 3):
            back(ch, k).wait_send()
            back_in(ch, k).wait_recv()


def expand_kernel(
    offs_hbm, wts_hbm, s_hbm, d_hbm, o_hbm, offs, wts, sbuf, dbuf, obuf, wexp, tap_sem, i_sem, o_sem
):
    n_dev, rows, nz = sbuf.shape
    nx = rows // 8
    per = nx // STEPS

    def fetch(c):
        part = pl.ds(c * per * 8, per * 8)
        return (
            pltpu.make_async_copy(s_hbm.at[:, part], sbuf.at[:, part], i_sem.at[0, c]),
            pltpu.make_async_copy(d_hbm.at[:, part], dbuf.at[:, part], i_sem.at[1, c]),
        )

    def store(c, l):
        return pltpu.make_async_copy(
            obuf.at[l, pl.ds(c * 2 * per, 2 * per)],
            o_hbm.at[pl.ds(c * 2 * per, 2 * per), :, pl.ds(128 * l, 128)],
            o_sem.at[c, l],
        )

    taps_in = [
        pltpu.make_async_copy(offs_hbm, offs, tap_sem.at[0]),
        pltpu.make_async_copy(wts_hbm, wts, tap_sem.at[1]),
    ]
    for c in taps_in:
        c.start()
    for c in range(STEPS):
        for copy in fetch(c):
            copy.start()
    for c in taps_in:
        c.wait()
    kid = child_rows(offs, wts, 256)
    row_i = lax.broadcasted_iota(I32, (256, 256), 0)
    col_i = lax.broadcasted_iota(I32, (256, 256), 1)
    paired = col_i // 2 == lax.rem(row_i, 128)
    even = lax.rem(col_i, 2) == 0
    for ab in range(4):
        e = jnp.where(even, kid[2 * ab], kid[2 * ab + 1])
        wexp[ab] = jnp.where(paired, e, 0.0).astype(BF16)

    for c in range(STEPS):
        part = pl.ds(c * per * 8, per * 8)
        for copy in fetch(c):
            copy.wait()
        for d in range(n_dev):
            dens = dbuf[d, part]
            v = (-1.5 * (1.0 - FLOOR) * GAIN) * dens * dens * sbuf[d, part].astype(F32)
            high = v.astype(BF16)
            low = (v - high.astype(F32)).astype(BF16)
            lhs = jnp.concatenate([high, low], axis=1)
            for a in range(2):
                for b in range(2):
                    t = jnp.dot(lhs, wexp[2 * a + b], preferred_element_type=F32)
                    for i in range(per):
                        for h in range(2):
                            obuf[2 * d + h, 2 * (c * per + i) + a, pl.ds(b, 8, stride=2), :] = t[
                                8 * i : 8 * i + 8, 128 * h : 128 * h + 128
                            ]
            for h in range(2):
                store(c, 2 * d + h).start()
    for c in range(STEPS):
        for l in range(2 * n_dev):
            store(c, l).wait()


def solution(mesh):
    n_gx, n_gy, n_dev = mesh.shape["gx"], mesh.shape["gy"], mesh.shape["dev"]

    def body(design, tap_offsets, tap_weights, input_load, input_mask, output_mask, fixed_mask):
        nx, ny, nz = input_load.shape
        cell = (nx, ny, nz)
        plane = (ny, nz)
        padded = ((nx + 2) * ny, nz)
        hbm = pl.BlockSpec(memory_space=pl.ANY)
        vm = lambda *shape: pltpu.VMEM(shape, F32)
        dma = lambda *shape: pltpu.SemaphoreType.DMA(shape)
        taps = [pltpu.SMEM((3, 16), I32), pltpu.SMEM((16,), F32)]
        scratch = [
            pltpu.VMEM((nx, 2, 16, 1024), BF16),
            vm(*cell), pltpu.VMEM(cell, I32), pltpu.VMEM(cell, I32), pltpu.VMEM(cell, I32),
            pltpu.VMEM((2, 256, 256), BF16),
            vm(n_dev, 2, nx // CHUNKS * 16, 128),
            vm(n_dev, nx * 8, nz),
            pltpu.VMEM((n_dev, nx * 8, nz), I16),
            pltpu.VMEM((n_dev, nx * 8, nz), I16),
            vm(*padded), vm(2, *padded), vm(2, *padded),
            vm(*cell), vm(2, *cell), vm(2, *cell),
            vm(*cell), vm(*padded), vm(*cell), vm(*cell),
            vm(4, *cell),
            vm(4, *plane),
            vm(2, *plane), vm(2, 2, *plane), vm(2, 2, *plane),
            vm(2, nx, nz), vm(2, 2, nx, nz), vm(2, 2, nx, nz),
            vm(2, nx, nz), vm(2, 2, nx, nz), vm(2, 2, nx, nz),
            vm(*plane), vm(*plane), vm(*plane),
            vm(2, *plane), vm(2, *plane), vm(2, *plane),
            vm(2, 2, nx, nz), vm(*plane), vm(*plane), vm(2, nx, nz), vm(2, *plane), vm(2, *plane),
            vm(2, 4, nx, nz), vm(2, *plane),
            vm(8, 8, 128), vm(16, 8, 128), vm(8, 128),
            pltpu.VMEM((n_dev, nx * 8, nz), BF16),
            *taps, dma(2),
            dma(CHUNKS + 4), dma(CHUNKS, 3), dma(CHUNKS, 3), dma(3, 6), dma(3, 6),
            dma(8), dma(8), dma(16), dma(16), dma(CHUNKS, 3), dma(CHUNKS, 3), dma(2),
            pltpu.SemaphoreType.REGULAR,
        ]
        returned, local = pl.pallas_call(
            functools.partial(step_kernel, n_gx, n_gy, n_dev),
            out_shape=(
                jax.ShapeDtypeStruct((n_dev, nx * 8, nz), BF16),
                jax.ShapeDtypeStruct((n_dev, nx * 8, nz), F32),
            ),
            in_specs=[hbm] * 7,
            out_specs=(hbm, hbm),
            scratch_shapes=scratch,
            compiler_params=pltpu.CompilerParams(collective_id=0, has_side_effects=True),
            name="step",
        )(
            design.reshape(nx, 2, 16, 1024), input_load, input_mask, output_mask, fixed_mask,
            tap_offsets.T, tap_weights,
        )
        return pl.pallas_call(
            expand_kernel,
            out_shape=jax.ShapeDtypeStruct(design.shape, F32),
            in_specs=[hbm] * 4,
            out_specs=hbm,
            scratch_shapes=[
                *taps,
                pltpu.VMEM((n_dev, nx * 8, nz), BF16),
                vm(n_dev, nx * 8, nz),
                vm(2 * n_dev, 2 * nx, 16, 128),
                pltpu.VMEM((4, 256, 256), BF16),
                dma(2),
                dma(2, STEPS),
                dma(STEPS, 2 * n_dev),
            ],
            name="expand",
        )(tap_offsets.T, tap_weights, returned, local)

    block = P("gx", "gy", "dev")
    owner = P("gx", ("gy", "dev"), None)
    return jax.shard_map(
        body, mesh=mesh,
        in_specs=(owner, P(), P(), block, block, block, block),
        out_specs=owner,
        check_vma=False,
    )
```

```python
import functools

import jax
import jax.numpy as jnp
from jax import lax
from jax.experimental import pallas as pl
from jax.experimental.pallas import tpu as pltpu
from jax.sharding import PartitionSpec as P

MESH = pl.DeviceIdType.MESH

FLOOR = 0.01
GROUND = 0.1
PORT = 0.5
GAIN = 64.0
TINY = 1e-06
MAX_STEP = 10.0

CODE = 32000.0
ORDER = (0, 3, 1, 2)
CHUNKS = len(ORDER)
STEPS = 4
F32 = jnp.float32
BF16 = jnp.bfloat16
I16 = jnp.int16
I32 = jnp.int32

ST, RH, QH = 0, 1, 2


def child_rows(offs, wts, lanes):
    taps = wts.shape[0]
    total = wts[0]
    for t in range(1, taps):
        total = total + wts[t]
    sums = [jnp.float32(0.0)] * 8
    for t in range(taps):
        code = offs[0, t] * 4 + offs[1, t] * 2 + offs[2, t]
        for c in range(8):
            sums[c] = sums[c] + jnp.where(code == c, wts[t], jnp.float32(0.0))
    below = jnp.full((1, lanes), total, F32)
    return [jnp.full((1, lanes), s, F32) / below for s in sums]


def between(a, b):
    return 2.0 * a * b / (a + b)


def step_kernel(
    n_gx, n_gy, n_dev,
    design, load, imask, omask, fmask, offs_hbm, wts_hbm,
    out, dloc, wout,
    dbuf, lbuf, ibuf, obuf, fbuf,
    wmat, pbuf, isend, irecv, st, rs, qq, diag, dzu, dzl,
    cx, cy, czu, czl, sarr, gprev,
    xr_st, xr_r, xr_q,
    ys_st, ys_r, ys_q, yr_st, yr_r, yr_q,
    zs_st, zs_r, zs_q, zr_st, zr_r, zr_q,
    yflux, zflux, zcon, ycon, xcon, zhal,
    ysb, zsb,
    ar1, ar2, coef, bsend, xq,
    offs, wts, tap_sem, in_sem, a_send, a_recv, h_send, h_recv, s_send, s_recv, t_send, t_recv,
    b_send, b_recv, o_sem, ready,
):
    gx = lax.axis_index("gx")
    gy = lax.axis_index("gy")
    me = lax.axis_index("dev")
    nx, ny, nz = lbuf.shape
    per = nx // CHUNKS
    rows = per * 8
    core = lax.rem(gy, 2)
    half = gy // 2
    ypos = lax.rem(gx, 4)
    zpos = gx // 4 * 2 + half

    taps_in = [
        pltpu.make_async_copy(offs_hbm, offs, tap_sem.at[0]),
        pltpu.make_async_copy(wts_hbm, wts, tap_sem.at[1]),
    ]
    for c in taps_in:
        c.start()
    ins = {}
    for ch in ORDER:
        c = pltpu.make_async_copy(
            design.at[pl.ds(ch * per, per)], dbuf.at[pl.ds(ch * per, per)], in_sem.at[ch]
        )
        c.start()
        ins[ch] = c
    fields_in = []
    for k, (a, b) in enumerate(((load, lbuf), (imask, ibuf), (omask, obuf), (fmask, fbuf))):
        c = pltpu.make_async_copy(a, b, in_sem.at[CHUNKS + k])
        c.start()
        fields_in.append(c)

    for ref in (xr_st, xr_r, xr_q, yr_st, yr_r, yr_q, zr_st, zr_r, zr_q):
        ref[...] = jnp.zeros_like(ref)

    id1 = me * 2 + core
    id2 = gx * 2 + half

    def peer1(k):
        other = lax.rem(id1 + k, 8)
        return {"gx": gx, "gy": half * 2 + lax.rem(other, 2), "dev": other // 2}

    def peer2(k):
        other = lax.rem(id2 + k, 16)
        return {"gx": other // 2, "gy": lax.rem(other, 2) * 2 + core, "dev": me}

    def peer_y(k):
        return {"gx": gx // 4 * 4 + lax.rem(ypos + k, 4), "gy": gy, "dev": me}

    def peer_z(k):
        z = lax.rem(zpos + k, 4)
        return {"gx": z // 2 * 4 + ypos, "gy": lax.rem(z, 2) * 2 + core, "dev": me}

    barrier = pltpu.get_barrier_semaphore()
    near = [peer1(k) for k in range(1, 8)] + [peer_y(k) for k in range(1, 4)]
    near += [peer_z(k) for k in range(1, 4)] + [{"gx": gx, "gy": n_gy - 1 - gy, "dev": me}]
    for peer in near:
        pl.semaphore_signal(barrier, inc=1, device_id=peer, device_id_type=MESH)

    for c in taps_in:
        c.wait()
    kid = child_rows(offs, wts, 256)
    row_i = lax.broadcasted_iota(I32, (256, 256), 0)
    col_i = lax.broadcasted_iota(I32, (256, 256), 1)
    paired = row_i // 2 == lax.rem(col_i, 128)
    even = lax.rem(row_i, 2) == 0
    left = col_i < 128
    for a in range(2):
        e = jnp.where(
            even,
            jnp.where(left, kid[4 * a], kid[4 * a + 2]),
            jnp.where(left, kid[4 * a + 1], kid[4 * a + 3]),
        )
        wmat[a] = jnp.where(paired, e, 0.0).astype(BF16)

    def a2a(ch, k):
        dst = lax.rem(me + k, n_dev)
        part = pl.ds(ch * rows, rows)
        return pltpu.make_async_remote_copy(
            src_ref=isend.at[dst, part],
            dst_ref=irecv.at[me, part],
            send_sem=a_send.at[ch, k - 1],
            recv_sem=a_recv.at[ch, k - 1],
            device_id={"gx": gx, "gy": gy, "dev": dst},
            device_id_type=MESH,
        )

    def a2a_in(ch, k):
        src = lax.rem(me + n_dev - k, n_dev)
        part = pl.ds(ch * rows, rows)
        return pltpu.make_async_remote_copy(
            src_ref=isend.at[src, part],
            dst_ref=irecv.at[src, part],
            send_sem=a_send.at[ch, k - 1],
            recv_sem=a_recv.at[ch, k - 1],
            device_id={"gx": gx, "gy": gy, "dev": src},
            device_id_type=MESH,
        )

    for ch in ORDER:
        ins[ch].wait()
        part = pl.ds(ch * rows, rows)
        for c in range(n_dev):
            total = None
            for a in range(2):
                lhs = dbuf[pl.ds(ch * per, per), a, :, pl.ds(256 * c, 256)].reshape(per * 16, 256)
                add = jnp.dot(lhs, wmat[a], preferred_element_type=F32)
                total = add if total is None else total + add
            pbuf[c, 0] = total[:, :128]
            pbuf[c, 1] = total[:, 128:]
            d = pbuf[c, 0, pl.ds(0, rows, stride=2), :] + pbuf[c, 1, pl.ds(1, rows, stride=2), :]
            dloc[c, part] = d
            isend[c, part] = (d * CODE + 0.5).astype(I32).astype(I16)
        if ch == ORDER[0]:
            pl.semaphore_wait(barrier, len(near))
        for k in (2, 1, 3):
            a2a(ch, k).start()
        irecv[me, part] = isend[me, part]
    for k in range(1, 4):
        pl.semaphore_signal(ready, inc=1, device_id=peer_y(k), device_id_type=MESH)

    def plane_of(i):
        return pl.ds(pl.multiple_of((i + 1) * ny, ny), ny)

    def xsend(e, side):
        where = plane_of(0 if side == 0 else nx - 1)
        if e == ST:
            return st.at[where]
        return rs.at[:, where] if e == RH else xq.at[side]

    xrecv = {ST: xr_st, RH: xr_r, QH: xr_q}
    ysend = {ST: ys_st, RH: ys_r, QH: ys_q}
    yrecv = {ST: yr_st, RH: yr_r, QH: yr_q}
    zsend = {ST: zs_st, RH: zs_r, QH: zs_q}
    zrecv = {ST: zr_st, RH: zr_r, QH: zr_q}
    spot = {"gx": (gx, n_gx), "gy": (gy, n_gy), "dev": (me, n_dev)}

    def face(e, axis, side):
        k = {"gx": 0, "gy": 2, "dev": 4}[axis] + side
        if axis == "gx":
            src, dst = xsend(e, side), xrecv[e].at[1 - side]
        elif axis == "gy":
            src, dst = ysend[e].at[side], yrecv[e].at[1 - side]
        else:
            src, dst = zsend[e], zrecv[e].at[1 - side]
        pos, size = spot[axis]
        target = {"gx": gx, "gy": gy, "dev": me}
        target[axis] = jnp.clip(pos - 1 if side == 0 else pos + 1, 0, size - 1)
        copy = pltpu.make_async_remote_copy(
            src_ref=src, dst_ref=dst, send_sem=h_send.at[e, k], recv_sem=h_recv.at[e, k],
            device_id=target, device_id_type=MESH,
        )
        sends = pos > 0 if side == 0 else pos < size - 1
        gets = pos < size - 1 if side == 0 else pos > 0
        return copy, sends, gets

    def start_face(e, axis, side):
        copy, sends, _ = face(e, axis, side)

        @pl.when(sends)
        def _():
            copy.start()

    def wait_face(e, axis, side):
        copy, _, gets = face(e, axis, side)

        @pl.when(gets)
        def _():
            copy.wait_recv()

    def end_face(e, axis, side):
        copy, sends, _ = face(e, axis, side)

        @pl.when(sends)
        def _():
            copy.wait_send()

    faces = [(axis, side) for axis in ("gx", "gy", "dev") for side in range(2)]

    iy = lax.broadcasted_iota(I32, (ny, nz), 0)
    iz = lax.broadcasted_iota(I32, (ny, nz), 1)
    first_y, last_y = iy == 0, iy == ny - 1
    first_z, last_z = iz == 0, iz == nz - 1
    ends_z = jnp.logical_or(first_z, last_z)
    key = ((iz + 1) // 2) % 64
    low_lane = lax.rem(iz, 2) == 0
    field0 = key < 32
    top8 = lax.broadcasted_iota(I32, (8, nz), 0) == 0
    end8 = lax.broadcasted_iota(I32, (8, nz), 0) == 7
    zero = jnp.zeros((ny, nz), F32)
    none = jnp.zeros((8, nz), F32)

    def fold(v):
        return jnp.sum(v.reshape(ny // 8, 8, nz), axis=0)

    def pack(into, v, f, i):
        return jnp.where(key == 32 * f + i, pltpu.roll(v, 64 * f + 2 * i, 1), into)

    def unpack(packed, f, i):
        by = 2 * nz - 64 * f - 2 * i
        by = by % nz if isinstance(i, int) else lax.rem(by, nz)
        return jnp.where(ends_z, pltpu.roll(packed, by, 1), 0.0)

    def add_rows(v, low, high):
        return jnp.concatenate(
            [v[:8] + jnp.where(top8, low, 0.0), v[8:-8], v[-8:] + jnp.where(end8, high, 0.0)], axis=0
        )

    def z_halo(ref):
        return jnp.where(low_lane, pltpu.roll(ref[0], 1, 1), pltpu.roll(ref[1], nz - 1, 1))

    for c in fields_in:
        c.wait()
    for ends in (pl.ds(0, ny), pl.ds((nx + 1) * ny, ny)):
        st[ends] = zero
        cy[ends] = zero
        for f in range(2):
            rs[f, ends] = zero
            qq[f, ends] = zero

    def load_plane(i, carry):
        zpack, m0r, m0s = carry
        im, om = ibuf[i].astype(F32), obuf[i].astype(F32)
        r, s = im * lbuf[i], om
        diag[i] = GROUND + fbuf[i].astype(F32) + PORT * (im + om)
        for f, v in enumerate((r, s)):
            rs[f, plane_of(i)] = v
            dzu[f, i] = v - pltpu.roll(v, nz - 1, 1)
            dzl[f, i] = v - pltpu.roll(v, 1, 1)
            ys_r[0, f, pl.ds(i, 1), :] = v[0:1]
            ys_r[1, f, pl.ds(i, 1), :] = v[ny - 1 : ny]
            zpack = pack(zpack, v, f, i)
        return zpack, m0r + fold(r * r), m0s + fold(s * s)

    zpack, m0r, m0s = lax.fori_loop(0, nx, load_plane, (zero, none, none), unroll=2)
    zs_r[...] = zpack
    pl.semaphore_wait(ready, 3)
    for axis, side in faces:
        start_face(RH, axis, side)

    def stiff_pair(p, zpack):
        d = [
            irecv[src, pl.ds(pl.multiple_of(16 * p, 16), 16)].astype(I32).astype(F32) * (1.0 / CODE)
            for src in range(n_dev)
        ]
        s = [FLOOR + (1.0 - FLOOR) * v * v * v for v in d]
        for h in range(2):
            i = 2 * p + h
            v = jnp.concatenate([t[8 * h : 8 * h + 8] for t in s], axis=0)
            st[plane_of(i)] = v
            ys_st[0, pl.ds(i, 1), :] = v[0:1]
            ys_st[1, pl.ds(i, 1), :] = v[ny - 1 : ny]
            zpack = pack(zpack, v, 0, i)
        return zpack

    zpack = zero
    for ch in ORDER:
        for k in (1, 3, 2):
            a2a_in(ch, k).wait_recv()
        zpack = lax.fori_loop(ch * per // 2, (ch + 1) * per // 2, stiff_pair, zpack, unroll=2)
        if ch == 0:
            start_face(ST, "gx", 0)
        if ch == CHUNKS - 1:
            start_face(ST, "gx", 1)
    zs_st[...] = jnp.where(field0, zpack, pltpu.roll(zpack, nz // 2, 1))
    for axis, side in faces[2:]:
        start_face(ST, axis, side)

    def inner_plane(i, carry):
        at = pl.multiple_of((i + 1) * ny, ny)
        here, after, up, down = pl.ds(at, ny), pl.ds(at + ny, ny), pl.ds(at + 1, ny), pl.ds(at - 1, ny)
        s = st[here]
        kx = between(s, st[after])
        kyu = between(s, jnp.where(last_y, 0.0, st[up]))
        kyl = between(s, jnp.where(first_y, 0.0, st[down]))
        kzu = between(s, jnp.where(last_z, 0.0, pltpu.roll(s, nz - 1, 1)))
        kzl = between(s, jnp.where(first_z, 0.0, pltpu.roll(s, 1, 1)))
        cx[i] = kx
        cy[here] = kyu
        czu[i] = kzu
        czl[i] = kzl
        dg = diag[i]
        new = []
        for f in range(2):
            v = rs[f, here]
            fx = kx * (v - rs[f, after])
            q = dg * v + (fx - carry[f])
            q += kyu * (v - rs[f, up]) + kyl * (v - rs[f, down])
            q += kzu * dzu[f, i] + kzl * dzl[f, i]
            qq[f, here] = q
            new.append(fx)
        return tuple(new)

    lax.fori_loop(0, nx, inner_plane, (zero, zero), unroll=2)

    for axis, side in faces:
        wait_face(RH, axis, side)
    for axis, side in faces[2:]:
        wait_face(ST, axis, side)

    kz = between(zs_st[...], z_halo(zr_st))
    zcon[...] = kz
    zhal[0] = zs_r[...] - z_halo(zr_r)
    zflux[...] = kz * zhal[0]
    for side in range(2):
        ycon[side] = between(ys_st[side], yr_st[side])
        for f in range(2):
            yflux[side, f] = ycon[side] * (ys_r[side, f] - yr_r[side, f])

    def with_edges(f, i):
        q = qq[f, plane_of(i)] + unpack(zflux[...], f, i)
        return add_rows(q, yflux[0, f, pl.ds(i, 1), :], yflux[1, f, pl.ds(i, 1), :])

    def finish(f, i, q, zpack, sums):
        qq[f, plane_of(i)] = q
        ys_q[0, f, pl.ds(i, 1), :] = q[0:1]
        ys_q[1, f, pl.ds(i, 1), :] = q[ny - 1 : ny]
        sums[f] += fold(rs[f, plane_of(i)] * q)
        sums[2 + f] += fold(q * q)
        return pack(zpack, q, f, i)

    def edge_plane(i, carry):
        zpack, sums = carry
        sums = list(sums)
        for f in range(2):
            zpack = finish(f, i, with_edges(f, i), zpack, sums)
        return zpack, tuple(sums)

    for side in range(2):
        for f in range(2):
            xq[side, f] = with_edges(f, 0 if side == 0 else nx - 1)
        start_face(QH, "gx", side)
    for side in range(2):
        wait_face(ST, "gx", side)
    zpack, sums = zero, [none] * 4
    for side in range(2):
        xcon[side] = between(st[plane_of(0 if side == 0 else nx - 1)], xr_st[side])
    for side in range(2):
        i = 0 if side == 0 else nx - 1
        for f in range(2):
            q = xq[side, f] + xcon[side] * (rs[f, plane_of(i)] - xr_r[side, f])
            zpack = finish(f, i, q, zpack, sums)
    carry = (zpack, tuple(sums))
    zpack, sums12 = lax.fori_loop(1, nx - 1, edge_plane, carry, unroll=2)
    zs_q[...] = zpack
    for axis, side in faces[2:]:
        start_face(QH, axis, side)

    gprev[...] = jnp.zeros_like(gprev)
    forms = ((0, 1), (0, 3), (2, 1), (2, 3))

    def product_plane(i, carry):
        e_r, e_s = carry
        at = pl.multiple_of((i + 1) * ny, ny)
        here, after, up, down = pl.ds(at, ny), pl.ds(at + ny, ny), pl.ds(at + 1, ny), pl.ds(at - 1, ny)

        def get(where):
            return [rs[0, where], rs[1, where], qq[0, where], qq[1, where]]

        v = get(here)
        dg = diag[i]
        e_r += fold(dg * v[2] * v[2])
        e_s += fold(dg * v[3] * v[3])
        q_up = [pltpu.roll(v[f], nz - 1, 1) for f in (2, 3)]
        q_down = [pltpu.roll(v[f], 1, 1) for f in (2, 3)]

        def diffs(o):
            return [a - b for a, b in zip(v, o)]

        d = diffs(get(after))
        k = cx[i]
        t = [k * a for a in d]
        e_r += fold(t[2] * d[2])
        e_s += fold(t[3] * d[3])
        held = []
        for j, (a, b) in enumerate(forms):
            g = t[a] * t[b]
            held.append(g + gprev[j])
            gprev[j] = g
        sides = (
            (True, cy[here], lambda: diffs(get(up))),
            (False, cy[down], lambda: diffs(get(down))),
            (True, czu[i], lambda: [dzu[0, i], dzu[1, i], v[2] - q_up[0], v[3] - q_up[1]]),
            (False, czl[i], lambda: [dzl[0, i], dzl[1, i], v[2] - q_down[0], v[3] - q_down[1]]),
        )
        for own, k, make in sides:
            d = make()
            t = [k * a for a in d]
            if own:
                e_r += fold(t[2] * d[2])
                e_s += fold(t[3] * d[3])
            for j, (a, b) in enumerate(forms):
                held[j] += t[a] * t[b]
        for j in range(4):
            sarr[j, i] = held[j]
        return e_r, e_s

    e_r, e_s = lax.fori_loop(0, nx, product_plane, (none, none))

    for axis, side in faces:
        wait_face(QH, axis, side)
    for side in range(2):
        edge = plane_of(0 if side == 0 else nx - 1)
        for f in range(2):
            xr_q[side, f] += xcon[side] * (xr_r[side, f] - rs[f, edge])

    zhal[1] = zs_q[...] - z_halo(zr_q)
    dz = zcon[...] * zhal[1] * zhal[1]
    parts = []
    for f in range(2):
        dx = qq[f, plane_of(nx - 1)] - xr_q[1, f]
        dy = ys_q[1, f] - yr_q[1, f]
        own = jnp.logical_and(jnp.logical_not(low_lane), field0 if f == 0 else jnp.logical_not(field0))
        parts.append(fold(xcon[1] * dx * dx + ycon[1] * dy * dy + jnp.where(own, dz, 0.0)))
    e_r += parts[0]
    e_s += parts[1]

    row8 = lax.broadcasted_iota(I32, (8, nz), 0)
    lane8 = lax.broadcasted_iota(I32, (8, nz), 1)
    tile = none
    for k, v in enumerate((m0r, m0s) + tuple(sums12) + (e_r, e_s)):
        tile = jnp.where(row8 == k, jnp.sum(v, axis=0, keepdims=True), tile)
    tile = jnp.where(row8 == lane8, jnp.sum(tile, axis=1, keepdims=True), 0.0)
    ar1[id1] = jnp.sum(tile, axis=0, keepdims=True)

    def gather1(k):
        return pltpu.make_async_remote_copy(
            src_ref=ar1.at[id1], dst_ref=ar1.at[id1], send_sem=s_send.at[k], recv_sem=s_recv.at[k],
            device_id=peer1(k), device_id_type=MESH,
        )

    def gather1_in(k):
        src = lax.rem(id1 + 8 - k, 8)
        return pltpu.make_async_remote_copy(
            src_ref=ar1.at[src], dst_ref=ar1.at[src], send_sem=s_send.at[k], recv_sem=s_recv.at[k],
            device_id=peer1(8 - k), device_id_type=MESH,
        )

    def gather2(k):
        return pltpu.make_async_remote_copy(
            src_ref=ar2.at[id2], dst_ref=ar2.at[id2], send_sem=t_send.at[k], recv_sem=t_recv.at[k],
            device_id=peer2(k), device_id_type=MESH,
        )

    def gather2_in(k):
        src = lax.rem(id2 + 16 - k, 16)
        return pltpu.make_async_remote_copy(
            src_ref=ar2.at[src], dst_ref=ar2.at[src], send_sem=t_send.at[k], recv_sem=t_recv.at[k],
            device_id=peer2(16 - k), device_id_type=MESH,
        )

    for k in range(1, 8):
        gather1(k).start()

    col_k = lax.rem(row_i, 128)
    paired = col_i // 2 == col_k
    even = lax.rem(col_i, 2) == 0
    for ab in range(4):
        e = jnp.where(even, kid[2 * ab], kid[2 * ab + 1])
        wout[ab] = jnp.where(paired, e, 0.0).astype(BF16)

    for side in range(2):
        edge = plane_of(0 if side == 0 else nx - 1)
        k = xcon[side]
        d = [k * (rs[f, edge] - xr_r[side, f]) for f in range(2)]
        d += [k * (qq[f, edge] - xr_q[side, f]) for f in range(2)]
        for j, (a, b) in enumerate(forms):
            sarr[j, 0 if side == 0 else nx - 1] += d[a] * d[b]
        k = ycon[side]
        d = [k * (ys_r[side, f] - yr_r[side, f]) for f in range(2)]
        d += [k * (ys_q[side, f] - yr_q[side, f]) for f in range(2)]
        for j, (a, b) in enumerate(forms):
            ysb[side, j] = d[a] * d[b]
    dr, dq = zcon[...] * zhal[0], zcon[...] * zhal[1]
    dr2, dq2 = pltpu.roll(dr, nz // 2, 1), pltpu.roll(dq, nz // 2, 1)
    zsb[0] = jnp.where(field0, dr * dr2, dq * dq2)
    zsb[1] = dr * dq2
    packed_at = ((0, 0), (1, 0), (1, 1), (0, 1))

    def scale_plane(i, carry):
        s = st[plane_of(i)]
        scale = 1.0 / (s * s)
        for j in range(4):
            buf, f = packed_at[j]
            g = sarr[j, i] + unpack(zsb[buf], f, i)
            g = add_rows(g, ysb[0, j, pl.ds(i, 1), :], ysb[1, j, pl.ds(i, 1), :])
            sarr[j, i] = scale * g
        return carry

    lax.fori_loop(0, nx // 2, scale_plane, 0, unroll=2)

    for k in range(1, 8):
        gather1_in(k).wait_recv()
    part = ar1[0]
    for k in range(1, 8):
        part = part + ar1[k]
    ar2[id2] = part
    for k in range(1, 16):
        gather2(k).start()

    lax.fori_loop(nx // 2, nx, scale_plane, 0, unroll=2)

    for ch in range(CHUNKS):
        for k in range(1, 4):
            a2a(ch, k).wait_send()
    for e in (ST, RH, QH):
        for axis, side in faces:
            end_face(e, axis, side)
    for k in range(1, 8):
        gather1(k).wait_send()

    for k in range(1, 16):
        gather2_in(k).wait_recv()
    whole = ar2[0]
    for k in range(1, 16):
        whole = whole + ar2[k]

    whole = jnp.where(row8 == lane8, whole, 0.0)
    coef[...] = jnp.broadcast_to(jnp.sum(whole, axis=1, keepdims=True), coef.shape)
    m0, m1, m2, m3 = (coef[pl.ds(2 * k, 2), :] for k in range(4))
    step0 = m0 / (m1 + TINY)
    rr1 = jnp.maximum(m0 - 2.0 * step0 * m1 + step0 * step0 * m2, 0.0)
    beta = rr1 / (m0 + TINY)
    r_a_r = m1 - 2.0 * step0 * m2 + step0 * step0 * m3
    r_a_d = m1 - step0 * m2
    d_a_d = r_a_r + 2.0 * beta * r_a_d + beta * beta * m1
    step1 = jnp.minimum(rr1 / (jnp.maximum(d_a_d, 0.0) + TINY), MAX_STEP)
    c0 = step0 + step1 * (1.0 + beta)
    c1 = -step0 * step1
    mix = [c0[0:1] * c0[1:2], c0[0:1] * c1[1:2], c1[0:1] * c0[1:2], c1[0:1] * c1[1:2]]

    def back(ch, k):
        dst = lax.rem(me + k, n_dev)
        part = pl.ds(ch * rows, rows)
        return pltpu.make_async_remote_copy(
            src_ref=bsend.at[dst, part],
            dst_ref=out.at[me, part],
            send_sem=b_send.at[ch, k - 1],
            recv_sem=b_recv.at[ch, k - 1],
            device_id={"gx": gx, "gy": gy, "dev": dst},
            device_id_type=MESH,
        )

    def back_in(ch, k):
        src = lax.rem(me + n_dev - k, n_dev)
        part = pl.ds(ch * rows, rows)
        return pltpu.make_async_remote_copy(
            src_ref=bsend.at[src, part],
            dst_ref=out.at[src, part],
            send_sem=b_send.at[ch, k - 1],
            recv_sem=b_recv.at[ch, k - 1],
            device_id={"gx": gx, "gy": gy, "dev": src},
            device_id_type=MESH,
        )

    def pair_planes(p, carry):
        v = None
        for j in range(4):
            add = mix[j] * sarr[j, pl.ds(2 * p, 2)]
            v = add if v is None else v + add
        for d in range(n_dev):
            two = v[:, 8 * d : 8 * d + 8, :].reshape(16, nz)
            bsend[d, pl.ds(pl.multiple_of(p * 16, 16), 16), :] = two.astype(BF16)
        return carry

    for ch in range(CHUNKS):
        lax.fori_loop(ch * per // 2, (ch + 1) * per // 2, pair_planes, 0, unroll=2)
        for k in (2, 1, 3):
            back(ch, k).start()
    own = pltpu.make_async_copy(bsend.at[me], out.at[me], o_sem)
    own.start()
    for k in range(1, 16):
        gather2(k).wait_send()
    own.wait()
    for ch in range(CHUNKS):
        for k in (2, 1, 3):
            back(ch, k).wait_send()
            back_in(ch, k).wait_recv()


def expand_kernel(s_ref, d_ref, w_ref, o_hbm, obuf, o_sem):
    n_dev, rows, nz = s_ref.shape
    nx = rows // 8
    per = nx // STEPS

    def store(c, l):
        return pltpu.make_async_copy(
            obuf.at[l, pl.ds(c * 2 * per, 2 * per)],
            o_hbm.at[pl.ds(c * 2 * per, 2 * per), :, pl.ds(128 * l, 128)],
            o_sem.at[c, l],
        )

    for c in range(STEPS):
        part = pl.ds(c * per * 8, per * 8)
        for d in range(n_dev):
            dens = d_ref[d, part]
            v = (-1.5 * (1.0 - FLOOR) * GAIN) * dens * dens * s_ref[d, part].astype(F32)
            high = v.astype(BF16)
            low = (v - high.astype(F32)).astype(BF16)
            lhs = jnp.concatenate([high, low], axis=1)
            for a in range(2):
                for b in range(2):
                    t = jnp.dot(lhs, w_ref[2 * a + b], preferred_element_type=F32)
                    for i in range(per):
                        for h in range(2):
                            obuf[2 * d + h, 2 * (c * per + i) + a, pl.ds(b, 8, stride=2), :] = t[
                                8 * i : 8 * i + 8, 128 * h : 128 * h + 128
                            ]
            for h in range(2):
                store(c, 2 * d + h).start()
    for c in range(STEPS):
        for l in range(2 * n_dev):
            store(c, l).wait()


def solution(mesh):
    n_gx, n_gy, n_dev = mesh.shape["gx"], mesh.shape["gy"], mesh.shape["dev"]

    def body(design, tap_offsets, tap_weights, input_load, input_mask, output_mask, fixed_mask):
        nx, ny, nz = input_load.shape
        cell = (nx, ny, nz)
        plane = (ny, nz)
        padded = ((nx + 2) * ny, nz)
        hbm = pl.BlockSpec(memory_space=pl.ANY)
        vmem = pl.BlockSpec(memory_space=pltpu.VMEM)
        vm = lambda *shape: pltpu.VMEM(shape, F32)
        dma = lambda *shape: pltpu.SemaphoreType.DMA(shape)
        taps = [pltpu.SMEM((3, 16), I32), pltpu.SMEM((16,), F32)]
        scratch = [
            pltpu.VMEM((nx, 2, 16, 1024), BF16),
            vm(*cell), pltpu.VMEM(cell, I32), pltpu.VMEM(cell, I32), pltpu.VMEM(cell, I32),
            pltpu.VMEM((2, 256, 256), BF16),
            vm(n_dev, 2, nx // CHUNKS * 16, 128),
            pltpu.VMEM((n_dev, nx * 8, nz), I16),
            pltpu.VMEM((n_dev, nx * 8, nz), I16),
            vm(*padded), vm(2, *padded), vm(2, *padded),
            vm(*cell), vm(2, *cell), vm(2, *cell),
            vm(*cell), vm(*padded), vm(*cell), vm(*cell),
            vm(4, *cell),
            vm(4, *plane),
            vm(2, *plane), vm(2, 2, *plane), vm(2, 2, *plane),
            vm(2, nx, nz), vm(2, 2, nx, nz), vm(2, 2, nx, nz),
            vm(2, nx, nz), vm(2, 2, nx, nz), vm(2, 2, nx, nz),
            vm(*plane), vm(*plane), vm(*plane),
            vm(2, *plane), vm(2, *plane), vm(2, *plane),
            vm(2, 2, nx, nz), vm(*plane), vm(*plane), vm(2, nx, nz), vm(2, *plane), vm(2, *plane),
            vm(2, 4, nx, nz), vm(2, *plane),
            vm(8, 1, 128), vm(16, 1, 128), vm(8, 128),
            pltpu.VMEM((n_dev, nx * 8, nz), BF16),
            vm(2, 2, *plane),
            *taps, dma(2),
            dma(CHUNKS + 4), dma(CHUNKS, 3), dma(CHUNKS, 3), dma(3, 6), dma(3, 6),
            dma(8), dma(8), dma(16), dma(16), dma(CHUNKS, 3), dma(CHUNKS, 3), pltpu.SemaphoreType.DMA,
            pltpu.SemaphoreType.REGULAR,
        ]
        returned, local, fold = pl.pallas_call(
            functools.partial(step_kernel, n_gx, n_gy, n_dev),
            out_shape=(
                jax.ShapeDtypeStruct((n_dev, nx * 8, nz), BF16),
                jax.ShapeDtypeStruct((n_dev, nx * 8, nz), F32),
                jax.ShapeDtypeStruct((4, 256, 256), BF16),
            ),
            in_specs=[hbm] * 7,
            out_specs=(vmem, vmem, vmem),
            scratch_shapes=scratch,
            compiler_params=pltpu.CompilerParams(
                collective_id=0, has_side_effects=True, vmem_limit_bytes=40000 * 1024
            ),
            name="step",
        )(
            *(
                pltpu.with_memory_space_constraint(v, pltpu.HBM)
                for v in (
                    design.reshape(nx, 2, 16, 1024), input_load, input_mask, output_mask, fixed_mask,
                    tap_offsets.T, tap_weights,
                )
            )
        )
        return pl.pallas_call(
            expand_kernel,
            out_shape=jax.ShapeDtypeStruct(design.shape, F32),
            in_specs=[vmem] * 3,
            out_specs=hbm,
            scratch_shapes=[vm(2 * n_dev, 2 * nx, 16, 128), dma(STEPS, 2 * n_dev)],
            compiler_params=pltpu.CompilerParams(vmem_limit_bytes=32 * 1024 * 1024),
            name="expand",
        )(returned, local, fold)

    block = P("gx", "gy", "dev")
    owner = P("gx", ("gy", "dev"), None)
    return jax.shard_map(
        body, mesh=mesh,
        in_specs=(owner, P(), P(), block, block, block, block),
        out_specs=owner,
        check_vma=False,
    )
```

```python
import functools

import jax
import jax.numpy as jnp
from jax import lax
from jax.experimental import pallas as pl
from jax.experimental.pallas import tpu as pltpu
from jax.sharding import PartitionSpec as P

MESH = pl.DeviceIdType.MESH

FLOOR = 0.01
GROUND = 0.1
PORT = 0.5
GAIN = 64.0
TINY = 1e-06
MAX_STEP = 10.0

CODE = 32000.0
ORDER = (0, 3, 1, 2)
CHUNKS = len(ORDER)
STEPS = 4
F32 = jnp.float32
BF16 = jnp.bfloat16
I16 = jnp.int16
I32 = jnp.int32

ST, RH, QH = 0, 1, 2


def child_rows(offs, wts, lanes):
    taps = wts.shape[0]
    total = wts[0]
    for t in range(1, taps):
        total = total + wts[t]
    sums = [jnp.float32(0.0)] * 8
    for t in range(taps):
        code = offs[0, t] * 4 + offs[1, t] * 2 + offs[2, t]
        for c in range(8):
            sums[c] = sums[c] + jnp.where(code == c, wts[t], jnp.float32(0.0))
    below = jnp.full((1, lanes), total, F32)
    return [jnp.full((1, lanes), s, F32) / below for s in sums]


def between(a, b):
    return 2.0 * a * b / (a + b)


def step_kernel(
    n_gx, n_gy, n_dev,
    design, load, imask, omask, fmask, offs_hbm, wts_hbm,
    out, dloc, wout,
    dbuf, lbuf, ibuf, obuf, fbuf,
    wmat, pbuf, isend, irecv, st, rs, qq, diag, dzu, dzl,
    cx, cy, czu, czl, sarr, gprev,
    xr_st, xr_r, xr_q,
    ys_st, ys_r, ys_q, yr_st, yr_r, yr_q,
    zs_st, zs_r, zs_q, zr_st, zr_r, zr_q,
    yflux, zflux, zcon, ycon, xcon, zhal,
    ysb, zsb,
    ar1, ar2, coef, bsend, xq,
    offs, wts, tap_sem, in_sem, a_send, a_recv, h_send, h_recv, s_send, s_recv, t_send, t_recv,
    b_send, b_recv, o_sem, ready,
):
    gx = lax.axis_index("gx")
    gy = lax.axis_index("gy")
    me = lax.axis_index("dev")
    nx, ny, nz = lbuf.shape
    per = nx // CHUNKS
    rows = per * 8
    core = lax.rem(gy, 2)
    half = gy // 2
    ypos = lax.rem(gx, 4)
    zpos = gx // 4 * 2 + half

    taps_in = [
        pltpu.make_async_copy(offs_hbm, offs, tap_sem.at[0]),
        pltpu.make_async_copy(wts_hbm, wts, tap_sem.at[1]),
    ]
    for c in taps_in:
        c.start()
    ins = {}
    for ch in ORDER:
        c = pltpu.make_async_copy(
            design.at[pl.ds(ch * per, per)], dbuf.at[pl.ds(ch * per, per)], in_sem.at[ch]
        )
        c.start()
        ins[ch] = c
    fields_in = []
    for k, (a, b) in enumerate(((load, lbuf), (imask, ibuf), (omask, obuf), (fmask, fbuf))):
        c = pltpu.make_async_copy(a, b, in_sem.at[CHUNKS + k])
        c.start()
        fields_in.append(c)

    for ref in (xr_st, xr_r, xr_q, yr_st, yr_r, yr_q, zr_st, zr_r, zr_q):
        ref[...] = jnp.zeros_like(ref)

    id1 = me * 2 + core
    id2 = gx * 2 + half

    def peer1(k):
        other = lax.rem(id1 + k, 8)
        return {"gx": gx, "gy": half * 2 + lax.rem(other, 2), "dev": other // 2}

    def peer2(k):
        other = lax.rem(id2 + k, 16)
        return {"gx": other // 2, "gy": lax.rem(other, 2) * 2 + core, "dev": me}

    def peer_y(k):
        return {"gx": gx // 4 * 4 + lax.rem(ypos + k, 4), "gy": gy, "dev": me}

    def peer_z(k):
        z = lax.rem(zpos + k, 4)
        return {"gx": z // 2 * 4 + ypos, "gy": lax.rem(z, 2) * 2 + core, "dev": me}

    barrier = pltpu.get_barrier_semaphore()
    near = [peer1(k) for k in range(1, 8)] + [peer_y(k) for k in range(1, 4)]
    near += [peer_z(k) for k in range(1, 4)] + [{"gx": gx, "gy": n_gy - 1 - gy, "dev": me}]
    for peer in near:
        pl.semaphore_signal(barrier, inc=1, device_id=peer, device_id_type=MESH)

    for c in taps_in:
        c.wait()
    kid = child_rows(offs, wts, 256)
    row_i = lax.broadcasted_iota(I32, (256, 256), 0)
    col_i = lax.broadcasted_iota(I32, (256, 256), 1)
    paired = row_i // 2 == lax.rem(col_i, 128)
    even = lax.rem(row_i, 2) == 0
    left = col_i < 128
    for a in range(2):
        e = jnp.where(
            even,
            jnp.where(left, kid[4 * a], kid[4 * a + 2]),
            jnp.where(left, kid[4 * a + 1], kid[4 * a + 3]),
        )
        wmat[a] = jnp.where(paired, e, 0.0).astype(BF16)

    def a2a(ch, k):
        dst = lax.rem(me + k, n_dev)
        part = pl.ds(ch * rows, rows)
        return pltpu.make_async_remote_copy(
            src_ref=isend.at[dst, part],
            dst_ref=irecv.at[me, part],
            send_sem=a_send.at[ch, k - 1],
            recv_sem=a_recv.at[ch, k - 1],
            device_id={"gx": gx, "gy": gy, "dev": dst},
            device_id_type=MESH,
        )

    def a2a_in(ch, k):
        src = lax.rem(me + n_dev - k, n_dev)
        part = pl.ds(ch * rows, rows)
        return pltpu.make_async_remote_copy(
            src_ref=isend.at[src, part],
            dst_ref=irecv.at[src, part],
            send_sem=a_send.at[ch, k - 1],
            recv_sem=a_recv.at[ch, k - 1],
            device_id={"gx": gx, "gy": gy, "dev": src},
            device_id_type=MESH,
        )

    for ch in ORDER:
        ins[ch].wait()
        part = pl.ds(ch * rows, rows)
        for c in range(n_dev):
            total = None
            for a in range(2):
                lhs = dbuf[pl.ds(ch * per, per), a, :, pl.ds(256 * c, 256)].reshape(per * 16, 256)
                add = jnp.dot(lhs, wmat[a], preferred_element_type=F32)
                total = add if total is None else total + add
            pbuf[c, 0] = total[:, :128]
            pbuf[c, 1] = total[:, 128:]
            d = pbuf[c, 0, pl.ds(0, rows, stride=2), :] + pbuf[c, 1, pl.ds(1, rows, stride=2), :]
            dloc[c, part] = d
            isend[c, part] = (d * CODE + 0.5).astype(I32).astype(I16)
        if ch == ORDER[0]:
            pl.semaphore_wait(barrier, len(near))
        for k in (2, 1, 3):
            a2a(ch, k).start()
        irecv[me, part] = isend[me, part]
    for k in range(1, 4):
        pl.semaphore_signal(ready, inc=1, device_id=peer_y(k), device_id_type=MESH)

    def plane_of(i):
        return pl.ds(pl.multiple_of((i + 1) * ny, ny), ny)

    def xsend(e, side):
        where = plane_of(0 if side == 0 else nx - 1)
        if e == ST:
            return st.at[where]
        return rs.at[:, where] if e == RH else xq.at[side]

    xrecv = {ST: xr_st, RH: xr_r, QH: xr_q}
    ysend = {ST: ys_st, RH: ys_r, QH: ys_q}
    yrecv = {ST: yr_st, RH: yr_r, QH: yr_q}
    zsend = {ST: zs_st, RH: zs_r, QH: zs_q}
    zrecv = {ST: zr_st, RH: zr_r, QH: zr_q}
    spot = {"gx": (gx, n_gx), "gy": (gy, n_gy), "dev": (me, n_dev)}

    def face(e, axis, side):
        k = {"gx": 0, "gy": 2, "dev": 4}[axis] + side
        if axis == "gx":
            src, dst = xsend(e, side), xrecv[e].at[1 - side]
        elif axis == "gy":
            src, dst = ysend[e].at[side], yrecv[e].at[1 - side]
        else:
            src, dst = zsend[e], zrecv[e].at[1 - side]
        pos, size = spot[axis]
        target = {"gx": gx, "gy": gy, "dev": me}
        target[axis] = jnp.clip(pos - 1 if side == 0 else pos + 1, 0, size - 1)
        copy = pltpu.make_async_remote_copy(
            src_ref=src, dst_ref=dst, send_sem=h_send.at[e, k], recv_sem=h_recv.at[e, k],
            device_id=target, device_id_type=MESH,
        )
        sends = pos > 0 if side == 0 else pos < size - 1
        gets = pos < size - 1 if side == 0 else pos > 0
        return copy, sends, gets

    def start_face(e, axis, side):
        copy, sends, _ = face(e, axis, side)

        @pl.when(sends)
        def _():
            copy.start()

    def wait_face(e, axis, side):
        copy, _, gets = face(e, axis, side)

        @pl.when(gets)
        def _():
            copy.wait_recv()

    def end_face(e, axis, side):
        copy, sends, _ = face(e, axis, side)

        @pl.when(sends)
        def _():
            copy.wait_send()

    faces = [(axis, side) for axis in ("gx", "gy", "dev") for side in range(2)]

    iy = lax.broadcasted_iota(I32, (ny, nz), 0)
    iz = lax.broadcasted_iota(I32, (ny, nz), 1)
    first_y, last_y = iy == 0, iy == ny - 1
    first_z, last_z = iz == 0, iz == nz - 1
    ends_z = jnp.logical_or(first_z, last_z)
    key = ((iz + 1) // 2) % 64
    low_lane = lax.rem(iz, 2) == 0
    field0 = key < 32
    top8 = lax.broadcasted_iota(I32, (8, nz), 0) == 0
    end8 = lax.broadcasted_iota(I32, (8, nz), 0) == 7
    zero = jnp.zeros((ny, nz), F32)
    none = jnp.zeros((8, nz), F32)

    def fold(v):
        return jnp.sum(v.reshape(ny // 8, 8, nz), axis=0)

    def pack(into, v, f, i):
        return jnp.where(key == 32 * f + i, pltpu.roll(v, 64 * f + 2 * i, 1), into)

    def unpack(packed, f, i):
        by = 2 * nz - 64 * f - 2 * i
        by = by % nz if isinstance(i, int) else lax.rem(by, nz)
        return jnp.where(ends_z, pltpu.roll(packed, by, 1), 0.0)

    def add_rows(v, low, high):
        return jnp.concatenate(
            [v[:8] + jnp.where(top8, low, 0.0), v[8:-8], v[-8:] + jnp.where(end8, high, 0.0)], axis=0
        )

    def z_halo(ref):
        return jnp.where(low_lane, pltpu.roll(ref[0], 1, 1), pltpu.roll(ref[1], nz - 1, 1))

    for c in fields_in:
        c.wait()
    for ends in (pl.ds(0, ny), pl.ds((nx + 1) * ny, ny)):
        st[ends] = zero
        cy[ends] = zero
        for f in range(2):
            rs[f, ends] = zero
            qq[f, ends] = zero

    def load_plane(i, carry):
        zpack, m0r, m0s = carry
        im, om = ibuf[i].astype(F32), obuf[i].astype(F32)
        r, s = im * lbuf[i], om
        diag[i] = GROUND + fbuf[i].astype(F32) + PORT * (im + om)
        for f, v in enumerate((r, s)):
            rs[f, plane_of(i)] = v
            dzu[f, i] = v - pltpu.roll(v, nz - 1, 1)
            dzl[f, i] = v - pltpu.roll(v, 1, 1)
            ys_r[0, f, pl.ds(i, 1), :] = v[0:1]
            ys_r[1, f, pl.ds(i, 1), :] = v[ny - 1 : ny]
            zpack = pack(zpack, v, f, i)
        return zpack, m0r + fold(r * r), m0s + fold(s * s)

    zpack, m0r, m0s = lax.fori_loop(0, nx, load_plane, (zero, none, none), unroll=2)
    zs_r[...] = zpack
    pl.semaphore_wait(ready, 3)
    for axis, side in faces:
        start_face(RH, axis, side)

    def stiff_pair(p, zpack):
        d = [
            irecv[src, pl.ds(pl.multiple_of(16 * p, 16), 16)].astype(I32).astype(F32) * (1.0 / CODE)
            for src in range(n_dev)
        ]
        s = [FLOOR + (1.0 - FLOOR) * v * v * v for v in d]
        for h in range(2):
            i = 2 * p + h
            v = jnp.concatenate([t[8 * h : 8 * h + 8] for t in s], axis=0)
            st[plane_of(i)] = v
            ys_st[0, pl.ds(i, 1), :] = v[0:1]
            ys_st[1, pl.ds(i, 1), :] = v[ny - 1 : ny]
            zpack = pack(zpack, v, 0, i)
        return zpack

    zpack = zero
    for ch in ORDER:
        for k in (1, 3, 2):
            a2a_in(ch, k).wait_recv()
        zpack = lax.fori_loop(ch * per // 2, (ch + 1) * per // 2, stiff_pair, zpack, unroll=4)
        if ch == 0:
            start_face(ST, "gx", 0)
        if ch == CHUNKS - 1:
            start_face(ST, "gx", 1)
    zs_st[...] = jnp.where(field0, zpack, pltpu.roll(zpack, nz // 2, 1))
    for axis, side in faces[2:]:
        start_face(ST, axis, side)

    def inner_plane(i, carry):
        at = pl.multiple_of((i + 1) * ny, ny)
        here, after, up, down = pl.ds(at, ny), pl.ds(at + ny, ny), pl.ds(at + 1, ny), pl.ds(at - 1, ny)
        s = st[here]
        kx = between(s, st[after])
        kyu = between(s, jnp.where(last_y, 0.0, st[up]))
        kyl = between(s, jnp.where(first_y, 0.0, st[down]))
        kzu = between(s, jnp.where(last_z, 0.0, pltpu.roll(s, nz - 1, 1)))
        kzl = between(s, jnp.where(first_z, 0.0, pltpu.roll(s, 1, 1)))
        cx[i] = kx
        cy[here] = kyu
        czu[i] = kzu
        czl[i] = kzl
        dg = diag[i]
        new = []
        for f in range(2):
            v = rs[f, here]
            fx = kx * (v - rs[f, after])
            q = dg * v + (fx - carry[f])
            q += kyu * (v - rs[f, up]) + kyl * (v - rs[f, down])
            q += kzu * dzu[f, i] + kzl * dzl[f, i]
            qq[f, here] = q
            new.append(fx)
        return tuple(new)

    lax.fori_loop(0, nx, inner_plane, (zero, zero), unroll=2)

    for axis, side in faces:
        wait_face(RH, axis, side)
    for axis, side in faces[2:]:
        wait_face(ST, axis, side)

    kz = between(zs_st[...], z_halo(zr_st))
    zcon[...] = kz
    zhal[0] = zs_r[...] - z_halo(zr_r)
    zflux[...] = kz * zhal[0]
    for side in range(2):
        ycon[side] = between(ys_st[side], yr_st[side])
        for f in range(2):
            yflux[side, f] = ycon[side] * (ys_r[side, f] - yr_r[side, f])

    def with_edges(f, i):
        q = qq[f, plane_of(i)] + unpack(zflux[...], f, i)
        return add_rows(q, yflux[0, f, pl.ds(i, 1), :], yflux[1, f, pl.ds(i, 1), :])

    def finish(f, i, q, zpack, sums):
        qq[f, plane_of(i)] = q
        ys_q[0, f, pl.ds(i, 1), :] = q[0:1]
        ys_q[1, f, pl.ds(i, 1), :] = q[ny - 1 : ny]
        sums[f] += fold(rs[f, plane_of(i)] * q)
        sums[2 + f] += fold(q * q)
        return pack(zpack, q, f, i)

    def edge_plane(i, carry):
        zpack, sums = carry
        sums = list(sums)
        for f in range(2):
            zpack = finish(f, i, with_edges(f, i), zpack, sums)
        return zpack, tuple(sums)

    for side in range(2):
        for f in range(2):
            xq[side, f] = with_edges(f, 0 if side == 0 else nx - 1)
        start_face(QH, "gx", side)
    zpack, sums = lax.fori_loop(1, nx - 1, edge_plane, (zero, (none,) * 4), unroll=6)
    sums = list(sums)
    for side in range(2):
        wait_face(ST, "gx", side)
    for side in range(2):
        i = 0 if side == 0 else nx - 1
        xcon[side] = between(st[plane_of(i)], xr_st[side])
        for f in range(2):
            q = xq[side, f] + xcon[side] * (rs[f, plane_of(i)] - xr_r[side, f])
            zpack = finish(f, i, q, zpack, sums)
    sums12 = sums
    zs_q[...] = zpack
    for axis, side in faces[2:]:
        start_face(QH, axis, side)

    gprev[...] = jnp.zeros_like(gprev)
    forms = ((0, 1), (0, 3), (2, 1), (2, 3))

    def product_plane(i, carry):
        e_r, e_s = carry
        at = pl.multiple_of((i + 1) * ny, ny)
        here, after, up, down = pl.ds(at, ny), pl.ds(at + ny, ny), pl.ds(at + 1, ny), pl.ds(at - 1, ny)

        def get(where):
            return [rs[0, where], rs[1, where], qq[0, where], qq[1, where]]

        v = get(here)
        dg = diag[i]
        e_r += fold(dg * v[2] * v[2])
        e_s += fold(dg * v[3] * v[3])
        q_up = [pltpu.roll(v[f], nz - 1, 1) for f in (2, 3)]
        q_down = [pltpu.roll(v[f], 1, 1) for f in (2, 3)]

        def diffs(o):
            return [a - b for a, b in zip(v, o)]

        d = diffs(get(after))
        k = cx[i]
        t = [k * a for a in d]
        e_r += fold(t[2] * d[2])
        e_s += fold(t[3] * d[3])
        held = []
        for j, (a, b) in enumerate(forms):
            g = t[a] * t[b]
            held.append(g + gprev[j])
            gprev[j] = g
        sides = (
            (True, cy[here], lambda: diffs(get(up))),
            (False, cy[down], lambda: diffs(get(down))),
            (True, czu[i], lambda: [dzu[0, i], dzu[1, i], v[2] - q_up[0], v[3] - q_up[1]]),
            (False, czl[i], lambda: [dzl[0, i], dzl[1, i], v[2] - q_down[0], v[3] - q_down[1]]),
        )
        for own, k, make in sides:
            d = make()
            t = [k * a for a in d]
            if own:
                e_r += fold(t[2] * d[2])
                e_s += fold(t[3] * d[3])
            for j, (a, b) in enumerate(forms):
                held[j] += t[a] * t[b]
        for j in range(4):
            sarr[j, i] = held[j]
        return e_r, e_s

    e_r, e_s = lax.fori_loop(0, nx, product_plane, (none, none), unroll=2)

    for axis, side in faces:
        wait_face(QH, axis, side)
    for side in range(2):
        edge = plane_of(0 if side == 0 else nx - 1)
        for f in range(2):
            xr_q[side, f] += xcon[side] * (xr_r[side, f] - rs[f, edge])

    zhal[1] = zs_q[...] - z_halo(zr_q)
    dz = zcon[...] * zhal[1] * zhal[1]
    parts = []
    for f in range(2):
        dx = qq[f, plane_of(nx - 1)] - xr_q[1, f]
        dy = ys_q[1, f] - yr_q[1, f]
        own = jnp.logical_and(jnp.logical_not(low_lane), field0 if f == 0 else jnp.logical_not(field0))
        parts.append(fold(xcon[1] * dx * dx + ycon[1] * dy * dy + jnp.where(own, dz, 0.0)))
    e_r += parts[0]
    e_s += parts[1]

    row8 = lax.broadcasted_iota(I32, (8, nz), 0)
    lane8 = lax.broadcasted_iota(I32, (8, nz), 1)
    tile = none
    for k, v in enumerate((m0r, m0s) + tuple(sums12) + (e_r, e_s)):
        tile = jnp.where(row8 == k, jnp.sum(v, axis=0, keepdims=True), tile)
    tile = jnp.where(row8 == lane8, jnp.sum(tile, axis=1, keepdims=True), 0.0)
    ar1[id1] = jnp.sum(tile, axis=0, keepdims=True)

    def gather1(k):
        return pltpu.make_async_remote_copy(
            src_ref=ar1.at[id1], dst_ref=ar1.at[id1], send_sem=s_send.at[k], recv_sem=s_recv.at[k],
            device_id=peer1(k), device_id_type=MESH,
        )

    def gather1_in(k):
        src = lax.rem(id1 + 8 - k, 8)
        return pltpu.make_async_remote_copy(
            src_ref=ar1.at[src], dst_ref=ar1.at[src], send_sem=s_send.at[k], recv_sem=s_recv.at[k],
            device_id=peer1(8 - k), device_id_type=MESH,
        )

    def gather2(k):
        return pltpu.make_async_remote_copy(
            src_ref=ar2.at[id2], dst_ref=ar2.at[id2], send_sem=t_send.at[k], recv_sem=t_recv.at[k],
            device_id=peer2(k), device_id_type=MESH,
        )

    def gather2_in(k):
        src = lax.rem(id2 + 16 - k, 16)
        return pltpu.make_async_remote_copy(
            src_ref=ar2.at[src], dst_ref=ar2.at[src], send_sem=t_send.at[k], recv_sem=t_recv.at[k],
            device_id=peer2(16 - k), device_id_type=MESH,
        )

    for k in range(1, 8):
        gather1(k).start()

    col_k = lax.rem(row_i, 128)
    paired = col_i // 2 == col_k
    even = lax.rem(col_i, 2) == 0
    for ab in range(4):
        e = jnp.where(even, kid[2 * ab], kid[2 * ab + 1])
        wout[ab] = jnp.where(paired, e, 0.0).astype(BF16)

    for side in range(2):
        edge = plane_of(0 if side == 0 else nx - 1)
        k = xcon[side]
        d = [k * (rs[f, edge] - xr_r[side, f]) for f in range(2)]
        d += [k * (qq[f, edge] - xr_q[side, f]) for f in range(2)]
        for j, (a, b) in enumerate(forms):
            sarr[j, 0 if side == 0 else nx - 1] += d[a] * d[b]
        k = ycon[side]
        d = [k * (ys_r[side, f] - yr_r[side, f]) for f in range(2)]
        d += [k * (ys_q[side, f] - yr_q[side, f]) for f in range(2)]
        for j, (a, b) in enumerate(forms):
            ysb[side, j] = d[a] * d[b]
    dr, dq = zcon[...] * zhal[0], zcon[...] * zhal[1]
    dr2, dq2 = pltpu.roll(dr, nz // 2, 1), pltpu.roll(dq, nz // 2, 1)
    zsb[0] = jnp.where(field0, dr * dr2, dq * dq2)
    zsb[1] = dr * dq2
    packed_at = ((0, 0), (1, 0), (1, 1), (0, 1))

    def scale_plane(i, carry):
        s = st[plane_of(i)]
        scale = 1.0 / (s * s)
        for j in range(4):
            buf, f = packed_at[j]
            g = sarr[j, i] + unpack(zsb[buf], f, i)
            g = add_rows(g, ysb[0, j, pl.ds(i, 1), :], ysb[1, j, pl.ds(i, 1), :])
            sarr[j, i] = scale * g
        return carry

    lax.fori_loop(0, nx // 2, scale_plane, 0, unroll=4)

    for k in range(1, 8):
        gather1_in(k).wait_recv()
    part = ar1[0]
    for k in range(1, 8):
        part = part + ar1[k]
    ar2[id2] = part
    for k in range(1, 16):
        gather2(k).start()

    lax.fori_loop(nx // 2, nx, scale_plane, 0, unroll=4)

    for ch in range(CHUNKS):
        for k in range(1, 4):
            a2a(ch, k).wait_send()
    for e in (ST, RH, QH):
        for axis, side in faces:
            end_face(e, axis, side)
    for k in range(1, 8):
        gather1(k).wait_send()

    for k in range(1, 16):
        gather2_in(k).wait_recv()
    whole = ar2[0]
    for k in range(1, 16):
        whole = whole + ar2[k]

    whole = jnp.where(row8 == lane8, whole, 0.0)
    coef[...] = jnp.broadcast_to(jnp.sum(whole, axis=1, keepdims=True), coef.shape)
    m0, m1, m2, m3 = (coef[pl.ds(2 * k, 2), :] for k in range(4))
    step0 = m0 / (m1 + TINY)
    rr1 = jnp.maximum(m0 - 2.0 * step0 * m1 + step0 * step0 * m2, 0.0)
    beta = rr1 / (m0 + TINY)
    r_a_r = m1 - 2.0 * step0 * m2 + step0 * step0 * m3
    r_a_d = m1 - step0 * m2
    d_a_d = r_a_r + 2.0 * beta * r_a_d + beta * beta * m1
    step1 = jnp.minimum(rr1 / (jnp.maximum(d_a_d, 0.0) + TINY), MAX_STEP)
    c0 = step0 + step1 * (1.0 + beta)
    c1 = -step0 * step1
    mix = [c0[0:1] * c0[1:2], c0[0:1] * c1[1:2], c1[0:1] * c0[1:2], c1[0:1] * c1[1:2]]

    def back(ch, k):
        dst = lax.rem(me + k, n_dev)
        part = pl.ds(ch * rows, rows)
        return pltpu.make_async_remote_copy(
            src_ref=bsend.at[dst, part],
            dst_ref=out.at[me, part],
            send_sem=b_send.at[ch, k - 1],
            recv_sem=b_recv.at[ch, k - 1],
            device_id={"gx": gx, "gy": gy, "dev": dst},
            device_id_type=MESH,
        )

    def back_in(ch, k):
        src = lax.rem(me + n_dev - k, n_dev)
        part = pl.ds(ch * rows, rows)
        return pltpu.make_async_remote_copy(
            src_ref=bsend.at[src, part],
            dst_ref=out.at[src, part],
            send_sem=b_send.at[ch, k - 1],
            recv_sem=b_recv.at[ch, k - 1],
            device_id={"gx": gx, "gy": gy, "dev": src},
            device_id_type=MESH,
        )

    def pair_planes(p, carry):
        v = None
        for j in range(4):
            add = mix[j] * sarr[j, pl.ds(2 * p, 2)]
            v = add if v is None else v + add
        for d in range(n_dev):
            two = v[:, 8 * d : 8 * d + 8, :].reshape(16, nz)
            bsend[d, pl.ds(pl.multiple_of(p * 16, 16), 16), :] = two.astype(BF16)
        return carry

    for ch in range(CHUNKS):
        lax.fori_loop(ch * per // 2, (ch + 1) * per // 2, pair_planes, 0, unroll=4)
        for k in (2, 1, 3):
            back(ch, k).start()
    own = pltpu.make_async_copy(bsend.at[me], out.at[me], o_sem)
    own.start()
    for k in range(1, 16):
        gather2(k).wait_send()
    own.wait()
    for ch in range(CHUNKS):
        for k in (2, 1, 3):
            back(ch, k).wait_send()
            back_in(ch, k).wait_recv()


def expand_kernel(s_ref, d_ref, w_ref, o_hbm, obuf, o_sem):
    n_dev, rows, nz = s_ref.shape
    nx = rows // 8
    per = nx // STEPS

    def store(c, l):
        return pltpu.make_async_copy(
            obuf.at[l, pl.ds(c * 2 * per, 2 * per)],
            o_hbm.at[pl.ds(c * 2 * per, 2 * per), :, pl.ds(128 * l, 128)],
            o_sem.at[c, l],
        )

    for c in range(STEPS):
        part = pl.ds(c * per * 8, per * 8)
        for d in range(n_dev):
            dens = d_ref[d, part]
            v = (-1.5 * (1.0 - FLOOR) * GAIN) * dens * dens * s_ref[d, part].astype(F32)
            high = v.astype(BF16)
            low = (v - high.astype(F32)).astype(BF16)
            lhs = jnp.concatenate([high, low], axis=1)
            for a in range(2):
                for b in range(2):
                    t = jnp.dot(lhs, w_ref[2 * a + b], preferred_element_type=F32)
                    for i in range(per):
                        for h in range(2):
                            obuf[2 * d + h, 2 * (c * per + i) + a, pl.ds(b, 8, stride=2), :] = t[
                                8 * i : 8 * i + 8, 128 * h : 128 * h + 128
                            ]
            for h in range(2):
                store(c, 2 * d + h).start()
    for c in range(STEPS):
        for l in range(2 * n_dev):
            store(c, l).wait()


def solution(mesh):
    n_gx, n_gy, n_dev = mesh.shape["gx"], mesh.shape["gy"], mesh.shape["dev"]

    def body(design, tap_offsets, tap_weights, input_load, input_mask, output_mask, fixed_mask):
        nx, ny, nz = input_load.shape
        cell = (nx, ny, nz)
        plane = (ny, nz)
        padded = ((nx + 2) * ny, nz)
        hbm = pl.BlockSpec(memory_space=pl.ANY)
        vmem = pl.BlockSpec(memory_space=pltpu.VMEM)
        vm = lambda *shape: pltpu.VMEM(shape, F32)
        dma = lambda *shape: pltpu.SemaphoreType.DMA(shape)
        taps = [pltpu.SMEM((3, 16), I32), pltpu.SMEM((16,), F32)]
        scratch = [
            pltpu.VMEM((nx, 2, 16, 1024), BF16),
            vm(*cell), pltpu.VMEM(cell, I32), pltpu.VMEM(cell, I32), pltpu.VMEM(cell, I32),
            pltpu.VMEM((2, 256, 256), BF16),
            vm(n_dev, 2, nx // CHUNKS * 16, 128),
            pltpu.VMEM((n_dev, nx * 8, nz), I16),
            pltpu.VMEM((n_dev, nx * 8, nz), I16),
            vm(*padded), vm(2, *padded), vm(2, *padded),
            vm(*cell), vm(2, *cell), vm(2, *cell),
            vm(*cell), vm(*padded), vm(*cell), vm(*cell),
            vm(4, *cell),
            vm(4, *plane),
            vm(2, *plane), vm(2, 2, *plane), vm(2, 2, *plane),
            vm(2, nx, nz), vm(2, 2, nx, nz), vm(2, 2, nx, nz),
            vm(2, nx, nz), vm(2, 2, nx, nz), vm(2, 2, nx, nz),
            vm(*plane), vm(*plane), vm(*plane),
            vm(2, *plane), vm(2, *plane), vm(2, *plane),
            vm(2, 2, nx, nz), vm(*plane), vm(*plane), vm(2, nx, nz), vm(2, *plane), vm(2, *plane),
            vm(2, 4, nx, nz), vm(2, *plane),
            vm(8, 1, 128), vm(16, 1, 128), vm(8, 128),
            pltpu.VMEM((n_dev, nx * 8, nz), BF16),
            vm(2, 2, *plane),
            *taps, dma(2),
            dma(CHUNKS + 4), dma(CHUNKS, 3), dma(CHUNKS, 3), dma(3, 6), dma(3, 6),
            dma(8), dma(8), dma(16), dma(16), dma(CHUNKS, 3), dma(CHUNKS, 3), pltpu.SemaphoreType.DMA,
            pltpu.SemaphoreType.REGULAR,
        ]
        returned, local, fold = pl.pallas_call(
            functools.partial(step_kernel, n_gx, n_gy, n_dev),
            out_shape=(
                jax.ShapeDtypeStruct((n_dev, nx * 8, nz), BF16),
                jax.ShapeDtypeStruct((n_dev, nx * 8, nz), F32),
                jax.ShapeDtypeStruct((4, 256, 256), BF16),
            ),
            in_specs=[hbm] * 7,
            out_specs=(vmem, vmem, vmem),
            scratch_shapes=scratch,
            compiler_params=pltpu.CompilerParams(
                collective_id=0, has_side_effects=True, vmem_limit_bytes=40000 * 1024
            ),
            name="step",
        )(
            *(
                pltpu.with_memory_space_constraint(v, pltpu.HBM)
                for v in (
                    design.reshape(nx, 2, 16, 1024), input_load, input_mask, output_mask, fixed_mask,
                    tap_offsets.T, tap_weights,
                )
            )
        )
        return pl.pallas_call(
            expand_kernel,
            out_shape=jax.ShapeDtypeStruct(design.shape, F32),
            in_specs=[vmem] * 3,
            out_specs=hbm,
            scratch_shapes=[vm(2 * n_dev, 2 * nx, 16, 128), dma(STEPS, 2 * n_dev)],
            compiler_params=pltpu.CompilerParams(vmem_limit_bytes=32 * 1024 * 1024),
            name="expand",
        )(returned, local, fold)

    block = P("gx", "gy", "dev")
    owner = P("gx", ("gy", "dev"), None)
    return jax.shard_map(
        body, mesh=mesh,
        in_specs=(owner, P(), P(), block, block, block, block),
        out_specs=owner,
        check_vma=False,
    )
```

```python
import functools

import jax
import jax.numpy as jnp
from jax import lax
from jax.experimental import pallas as pl
from jax.experimental.pallas import tpu as pltpu
from jax.sharding import PartitionSpec as P

MESH = pl.DeviceIdType.MESH

FLOOR = 0.01
GROUND = 0.1
PORT = 0.5
GAIN = 64.0
TINY = 1e-06
MAX_STEP = 10.0

CODE = 32000.0
ORDER = (0, 3, 1, 2)
CHUNKS = len(ORDER)
BACKS = 1
STEPS = 1
F32 = jnp.float32
BF16 = jnp.bfloat16
I16 = jnp.int16
I32 = jnp.int32

ST, RH, QH = 0, 1, 2


def child_rows(offs, wts, lanes):
    taps = wts.shape[0]
    total = wts[0]
    for t in range(1, taps):
        total = total + wts[t]
    sums = [jnp.float32(0.0)] * 8
    for t in range(taps):
        code = offs[0, t] * 4 + offs[1, t] * 2 + offs[2, t]
        for c in range(8):
            sums[c] = sums[c] + jnp.where(code == c, wts[t], jnp.float32(0.0))
    below = jnp.full((1, lanes), total, F32)
    return [jnp.full((1, lanes), s, F32) / below for s in sums]


def between(a, b):
    return 2.0 * a * b / (a + b)


def step_kernel(
    n_gx, n_gy, n_dev,
    design, load, imask, omask, fmask, offs_hbm, wts_hbm,
    out, dloc, wout,
    dbuf, lbuf, ibuf, obuf, fbuf,
    wmat, pbuf, isend, irecv, st, rs, qq, diag, dzu, dzl,
    cx, cy, czu, czl, sarr, gprev,
    xr_st, xr_r, xr_q,
    ys_st, ys_r, ys_q, yr_st, yr_r, yr_q,
    zs_st, zs_r, zs_q, zr_st, zr_r, zr_q,
    yflux, zflux, zcon, ycon, xcon, zhal,
    ysb, zsb,
    ar1, ar2, coef, bsend, xq,
    offs, wts, tap_sem, in_sem, a_send, a_recv, h_send, h_recv, s_send, s_recv, t_send, t_recv,
    b_send, b_recv, o_sem, ready,
):
    gx = lax.axis_index("gx")
    gy = lax.axis_index("gy")
    me = lax.axis_index("dev")
    nx, ny, nz = lbuf.shape
    per = nx // CHUNKS
    rows = per * 8
    core = lax.rem(gy, 2)
    half = gy // 2
    ypos = lax.rem(gx, 4)
    zpos = gx // 4 * 2 + half

    taps_in = [
        pltpu.make_async_copy(offs_hbm, offs, tap_sem.at[0]),
        pltpu.make_async_copy(wts_hbm, wts, tap_sem.at[1]),
    ]
    for c in taps_in:
        c.start()
    ins = {}
    for ch in ORDER:
        c = pltpu.make_async_copy(
            design.at[pl.ds(ch * per, per)], dbuf.at[pl.ds(ch * per, per)], in_sem.at[ch]
        )
        c.start()
        ins[ch] = c
    fields_in = []
    for k, (a, b) in enumerate(((load, lbuf), (imask, ibuf), (omask, obuf), (fmask, fbuf))):
        c = pltpu.make_async_copy(a, b, in_sem.at[CHUNKS + k])
        c.start()
        fields_in.append(c)

    for ref in (xr_st, xr_r, xr_q, yr_st, yr_r, yr_q, zr_st, zr_r, zr_q):
        ref[...] = jnp.zeros_like(ref)

    id1 = me * 2 + core
    id2 = gx * 2 + half

    def peer1(k):
        other = lax.rem(id1 + k, 8)
        return {"gx": gx, "gy": half * 2 + lax.rem(other, 2), "dev": other // 2}

    def peer2(k):
        other = lax.rem(id2 + k, 16)
        return {"gx": other // 2, "gy": lax.rem(other, 2) * 2 + core, "dev": me}

    def peer_y(k):
        return {"gx": gx // 4 * 4 + lax.rem(ypos + k, 4), "gy": gy, "dev": me}

    def peer_z(k):
        z = lax.rem(zpos + k, 4)
        return {"gx": z // 2 * 4 + ypos, "gy": lax.rem(z, 2) * 2 + core, "dev": me}

    barrier = pltpu.get_barrier_semaphore()
    near = [peer1(k) for k in range(1, 8)] + [peer_y(k) for k in range(1, 4)]
    near += [peer_z(k) for k in range(1, 4)] + [{"gx": gx, "gy": n_gy - 1 - gy, "dev": me}]
    for peer in near:
        pl.semaphore_signal(barrier, inc=1, device_id=peer, device_id_type=MESH)

    for c in taps_in:
        c.wait()
    kid = child_rows(offs, wts, 256)
    row_i = lax.broadcasted_iota(I32, (256, 256), 0)
    col_i = lax.broadcasted_iota(I32, (256, 256), 1)
    paired = row_i // 2 == lax.rem(col_i, 128)
    even = lax.rem(row_i, 2) == 0
    left = col_i < 128
    for a in range(2):
        e = jnp.where(
            even,
            jnp.where(left, kid[4 * a], kid[4 * a + 2]),
            jnp.where(left, kid[4 * a + 1], kid[4 * a + 3]),
        )
        wmat[a] = jnp.where(paired, e, 0.0).astype(BF16)

    def a2a(ch, k):
        dst = lax.rem(me + k, n_dev)
        part = pl.ds(ch * rows, rows)
        return pltpu.make_async_remote_copy(
            src_ref=isend.at[dst, part],
            dst_ref=irecv.at[me, part],
            send_sem=a_send.at[ch, k - 1],
            recv_sem=a_recv.at[ch, k - 1],
            device_id={"gx": gx, "gy": gy, "dev": dst},
            device_id_type=MESH,
        )

    def a2a_in(ch, k):
        src = lax.rem(me + n_dev - k, n_dev)
        part = pl.ds(ch * rows, rows)
        return pltpu.make_async_remote_copy(
            src_ref=isend.at[src, part],
            dst_ref=irecv.at[src, part],
            send_sem=a_send.at[ch, k - 1],
            recv_sem=a_recv.at[ch, k - 1],
            device_id={"gx": gx, "gy": gy, "dev": src},
            device_id_type=MESH,
        )

    for ch in ORDER:
        ins[ch].wait()
        part = pl.ds(ch * rows, rows)
        for c in range(n_dev):
            total = None
            for a in range(2):
                lhs = dbuf[pl.ds(ch * per, per), a, :, pl.ds(256 * c, 256)].reshape(per * 16, 256)
                add = jnp.dot(lhs, wmat[a], preferred_element_type=F32)
                total = add if total is None else total + add
            pbuf[c, 0] = total[:, :128]
            pbuf[c, 1] = total[:, 128:]
            d = pbuf[c, 0, pl.ds(0, rows, stride=2), :] + pbuf[c, 1, pl.ds(1, rows, stride=2), :]
            dloc[c, part] = d
            isend[c, part] = (d * CODE + 0.5).astype(I32).astype(I16)
        if ch == ORDER[0]:
            pl.semaphore_wait(barrier, len(near))
        for k in (2, 1, 3):
            a2a(ch, k).start()
        irecv[me, part] = isend[me, part]
    for k in range(1, 4):
        pl.semaphore_signal(ready, inc=1, device_id=peer_y(k), device_id_type=MESH)

    def plane_of(i):
        return pl.ds(pl.multiple_of((i + 1) * ny, ny), ny)

    def xsend(e, side):
        where = plane_of(0 if side == 0 else nx - 1)
        if e == ST:
            return st.at[where]
        return rs.at[:, where] if e == RH else xq.at[side]

    xrecv = {ST: xr_st, RH: xr_r, QH: xr_q}
    ysend = {ST: ys_st, RH: ys_r, QH: ys_q}
    yrecv = {ST: yr_st, RH: yr_r, QH: yr_q}
    zsend = {ST: zs_st, RH: zs_r, QH: zs_q}
    zrecv = {ST: zr_st, RH: zr_r, QH: zr_q}
    spot = {"gx": (gx, n_gx), "gy": (gy, n_gy), "dev": (me, n_dev)}

    def face(e, axis, side):
        k = {"gx": 0, "gy": 2, "dev": 4}[axis] + side
        if axis == "gx":
            src, dst = xsend(e, side), xrecv[e].at[1 - side]
        elif axis == "gy":
            src, dst = ysend[e].at[side], yrecv[e].at[1 - side]
        else:
            src, dst = zsend[e], zrecv[e].at[1 - side]
        pos, size = spot[axis]
        target = {"gx": gx, "gy": gy, "dev": me}
        target[axis] = jnp.clip(pos - 1 if side == 0 else pos + 1, 0, size - 1)
        copy = pltpu.make_async_remote_copy(
            src_ref=src, dst_ref=dst, send_sem=h_send.at[e, k], recv_sem=h_recv.at[e, k],
            device_id=target, device_id_type=MESH,
        )
        sends = pos > 0 if side == 0 else pos < size - 1
        gets = pos < size - 1 if side == 0 else pos > 0
        return copy, sends, gets

    def start_face(e, axis, side):
        copy, sends, _ = face(e, axis, side)

        @pl.when(sends)
        def _():
            copy.start()

    def wait_face(e, axis, side):
        copy, _, gets = face(e, axis, side)

        @pl.when(gets)
        def _():
            copy.wait_recv()

    def end_face(e, axis, side):
        copy, sends, _ = face(e, axis, side)

        @pl.when(sends)
        def _():
            copy.wait_send()

    faces = [(axis, side) for axis in ("gx", "gy", "dev") for side in range(2)]

    iy = lax.broadcasted_iota(I32, (ny, nz), 0)
    iz = lax.broadcasted_iota(I32, (ny, nz), 1)
    first_y, last_y = iy == 0, iy == ny - 1
    first_z, last_z = iz == 0, iz == nz - 1
    ends_z = jnp.logical_or(first_z, last_z)
    key = ((iz + 1) // 2) % 64
    low_lane = lax.rem(iz, 2) == 0
    field0 = key < 32
    top8 = lax.broadcasted_iota(I32, (8, nz), 0) == 0
    end8 = lax.broadcasted_iota(I32, (8, nz), 0) == 7
    zero = jnp.zeros((ny, nz), F32)
    none = jnp.zeros((8, nz), F32)

    def fold(v):
        return jnp.sum(v.reshape(ny // 8, 8, nz), axis=0)

    def pack(into, v, f, i):
        return jnp.where(key == 32 * f + i, pltpu.roll(v, 64 * f + 2 * i, 1), into)

    def unpack(packed, f, i):
        by = 2 * nz - 64 * f - 2 * i
        by = by % nz if isinstance(i, int) else lax.rem(by, nz)
        return jnp.where(ends_z, pltpu.roll(packed, by, 1), 0.0)

    def add_rows(v, low, high):
        return jnp.concatenate(
            [v[:8] + jnp.where(top8, low, 0.0), v[8:-8], v[-8:] + jnp.where(end8, high, 0.0)], axis=0
        )

    def z_halo(ref):
        return jnp.where(low_lane, pltpu.roll(ref[0], 1, 1), pltpu.roll(ref[1], nz - 1, 1))

    for c in fields_in:
        c.wait()
    for ends in (pl.ds(0, ny), pl.ds((nx + 1) * ny, ny)):
        st[ends] = zero
        cy[ends] = zero
        for f in range(2):
            rs[f, ends] = zero
            qq[f, ends] = zero

    def load_plane(i, carry):
        zpack, m0r, m0s = carry
        im, om = ibuf[i].astype(F32), obuf[i].astype(F32)
        r, s = im * lbuf[i], om
        diag[i] = GROUND + fbuf[i].astype(F32) + PORT * (im + om)
        for f, v in enumerate((r, s)):
            rs[f, plane_of(i)] = v
            dzu[f, i] = v - pltpu.roll(v, nz - 1, 1)
            dzl[f, i] = v - pltpu.roll(v, 1, 1)
            ys_r[0, f, pl.ds(i, 1), :] = v[0:1]
            ys_r[1, f, pl.ds(i, 1), :] = v[ny - 1 : ny]
            zpack = pack(zpack, v, f, i)
        return zpack, m0r + fold(r * r), m0s + fold(s * s)

    zpack, m0r, m0s = lax.fori_loop(0, nx, load_plane, (zero, none, none), unroll=2)
    zs_r[...] = zpack
    pl.semaphore_wait(ready, 3)
    for axis, side in faces:
        start_face(RH, axis, side)

    def stiff_pair(p, zpack):
        d = [
            irecv[src, pl.ds(pl.multiple_of(16 * p, 16), 16)].astype(I32).astype(F32) * (1.0 / CODE)
            for src in range(n_dev)
        ]
        s = [FLOOR + (1.0 - FLOOR) * v * v * v for v in d]
        for h in range(2):
            i = 2 * p + h
            v = jnp.concatenate([t[8 * h : 8 * h + 8] for t in s], axis=0)
            st[plane_of(i)] = v
            ys_st[0, pl.ds(i, 1), :] = v[0:1]
            ys_st[1, pl.ds(i, 1), :] = v[ny - 1 : ny]
            zpack = pack(zpack, v, 0, i)
        return zpack

    zpack = zero
    for ch in ORDER:
        for k in (1, 3, 2):
            a2a_in(ch, k).wait_recv()
        zpack = lax.fori_loop(ch * per // 2, (ch + 1) * per // 2, stiff_pair, zpack, unroll=4)
        if ch == 0:
            start_face(ST, "gx", 0)
        if ch == CHUNKS - 1:
            start_face(ST, "gx", 1)
    zs_st[...] = jnp.where(field0, zpack, pltpu.roll(zpack, nz // 2, 1))
    for axis, side in faces[2:]:
        start_face(ST, axis, side)

    def inner_plane(i, carry):
        at = pl.multiple_of((i + 1) * ny, ny)
        here, after, up, down = pl.ds(at, ny), pl.ds(at + ny, ny), pl.ds(at + 1, ny), pl.ds(at - 1, ny)
        s = st[here]
        kx = between(s, st[after])
        kyu = between(s, jnp.where(last_y, 0.0, st[up]))
        kyl = between(s, jnp.where(first_y, 0.0, st[down]))
        kzu = between(s, jnp.where(last_z, 0.0, pltpu.roll(s, nz - 1, 1)))
        kzl = between(s, jnp.where(first_z, 0.0, pltpu.roll(s, 1, 1)))
        cx[i] = kx
        cy[here] = kyu
        czu[i] = kzu
        czl[i] = kzl
        dg = diag[i]
        new = []
        for f in range(2):
            v = rs[f, here]
            fx = kx * (v - rs[f, after])
            q = dg * v + (fx - carry[f])
            q += kyu * (v - rs[f, up]) + kyl * (v - rs[f, down])
            q += kzu * dzu[f, i] + kzl * dzl[f, i]
            qq[f, here] = q
            new.append(fx)
        return tuple(new)

    lax.fori_loop(0, nx, inner_plane, (zero, zero), unroll=2)

    for axis, side in faces:
        wait_face(RH, axis, side)
    for axis, side in faces[2:]:
        wait_face(ST, axis, side)

    kz = between(zs_st[...], z_halo(zr_st))
    zcon[...] = kz
    zhal[0] = zs_r[...] - z_halo(zr_r)
    zflux[...] = kz * zhal[0]
    for side in range(2):
        ycon[side] = between(ys_st[side], yr_st[side])
        for f in range(2):
            yflux[side, f] = ycon[side] * (ys_r[side, f] - yr_r[side, f])

    def with_edges(f, i):
        q = qq[f, plane_of(i)] + unpack(zflux[...], f, i)
        return add_rows(q, yflux[0, f, pl.ds(i, 1), :], yflux[1, f, pl.ds(i, 1), :])

    def finish(f, i, q, zpack, sums):
        qq[f, plane_of(i)] = q
        ys_q[0, f, pl.ds(i, 1), :] = q[0:1]
        ys_q[1, f, pl.ds(i, 1), :] = q[ny - 1 : ny]
        sums[f] += fold(rs[f, plane_of(i)] * q)
        sums[2 + f] += fold(q * q)
        return pack(zpack, q, f, i)

    def edge_plane(i, carry):
        zpack, sums = carry
        sums = list(sums)
        for f in range(2):
            zpack = finish(f, i, with_edges(f, i), zpack, sums)
        return zpack, tuple(sums)

    for side in range(2):
        for f in range(2):
            xq[side, f] = with_edges(f, 0 if side == 0 else nx - 1)
        start_face(QH, "gx", side)
    zpack, sums = lax.fori_loop(1, nx - 1, edge_plane, (zero, (none,) * 4), unroll=6)
    sums = list(sums)
    for side in range(2):
        wait_face(ST, "gx", side)
    for side in range(2):
        i = 0 if side == 0 else nx - 1
        xcon[side] = between(st[plane_of(i)], xr_st[side])
        for f in range(2):
            q = xq[side, f] + xcon[side] * (rs[f, plane_of(i)] - xr_r[side, f])
            zpack = finish(f, i, q, zpack, sums)
    sums12 = sums
    zs_q[...] = zpack
    for axis, side in faces[2:]:
        start_face(QH, axis, side)

    gprev[...] = jnp.zeros_like(gprev)
    forms = ((0, 1), (0, 3), (2, 1), (2, 3))

    def product_plane(i, carry):
        e_r, e_s = carry
        at = pl.multiple_of((i + 1) * ny, ny)
        here, after, up, down = pl.ds(at, ny), pl.ds(at + ny, ny), pl.ds(at + 1, ny), pl.ds(at - 1, ny)

        def get(where):
            return [rs[0, where], rs[1, where], qq[0, where], qq[1, where]]

        v = get(here)
        dg = diag[i]
        e_r += fold(dg * v[2] * v[2])
        e_s += fold(dg * v[3] * v[3])
        q_up = [pltpu.roll(v[f], nz - 1, 1) for f in (2, 3)]
        q_down = [pltpu.roll(v[f], 1, 1) for f in (2, 3)]

        def diffs(o):
            return [a - b for a, b in zip(v, o)]

        d = diffs(get(after))
        k = cx[i]
        t = [k * a for a in d]
        e_r += fold(t[2] * d[2])
        e_s += fold(t[3] * d[3])
        held = []
        for j, (a, b) in enumerate(forms):
            g = t[a] * t[b]
            held.append(g + gprev[j])
            gprev[j] = g
        sides = (
            (True, cy[here], lambda: diffs(get(up))),
            (False, cy[down], lambda: diffs(get(down))),
            (True, czu[i], lambda: [dzu[0, i], dzu[1, i], v[2] - q_up[0], v[3] - q_up[1]]),
            (False, czl[i], lambda: [dzl[0, i], dzl[1, i], v[2] - q_down[0], v[3] - q_down[1]]),
        )
        for own, k, make in sides:
            d = make()
            t = [k * a for a in d]
            if own:
                e_r += fold(t[2] * d[2])
                e_s += fold(t[3] * d[3])
            for j, (a, b) in enumerate(forms):
                held[j] += t[a] * t[b]
        for j in range(4):
            sarr[j, i] = held[j]
        return e_r, e_s

    e_r, e_s = lax.fori_loop(0, nx, product_plane, (none, none), unroll=2)

    for axis, side in faces:
        wait_face(QH, axis, side)
    for side in range(2):
        edge = plane_of(0 if side == 0 else nx - 1)
        for f in range(2):
            xr_q[side, f] += xcon[side] * (xr_r[side, f] - rs[f, edge])

    zhal[1] = zs_q[...] - z_halo(zr_q)
    dz = zcon[...] * zhal[1] * zhal[1]
    parts = []
    for f in range(2):
        dx = qq[f, plane_of(nx - 1)] - xr_q[1, f]
        dy = ys_q[1, f] - yr_q[1, f]
        own = jnp.logical_and(jnp.logical_not(low_lane), field0 if f == 0 else jnp.logical_not(field0))
        parts.append(fold(xcon[1] * dx * dx + ycon[1] * dy * dy + jnp.where(own, dz, 0.0)))
    e_r += parts[0]
    e_s += parts[1]

    row8 = lax.broadcasted_iota(I32, (8, nz), 0)
    lane8 = lax.broadcasted_iota(I32, (8, nz), 1)
    tile = none
    for k, v in enumerate((m0r, m0s) + tuple(sums12) + (e_r, e_s)):
        tile = jnp.where(row8 == k, jnp.sum(v, axis=0, keepdims=True), tile)
    tile = jnp.where(row8 == lane8, jnp.sum(tile, axis=1, keepdims=True), 0.0)
    ar1[id1] = jnp.sum(tile, axis=0, keepdims=True)

    def gather1(k):
        return pltpu.make_async_remote_copy(
            src_ref=ar1.at[id1], dst_ref=ar1.at[id1], send_sem=s_send.at[k], recv_sem=s_recv.at[k],
            device_id=peer1(k), device_id_type=MESH,
        )

    def gather1_in(k):
        src = lax.rem(id1 + 8 - k, 8)
        return pltpu.make_async_remote_copy(
            src_ref=ar1.at[src], dst_ref=ar1.at[src], send_sem=s_send.at[k], recv_sem=s_recv.at[k],
            device_id=peer1(8 - k), device_id_type=MESH,
        )

    def gather2(k):
        return pltpu.make_async_remote_copy(
            src_ref=ar2.at[id2], dst_ref=ar2.at[id2], send_sem=t_send.at[k], recv_sem=t_recv.at[k],
            device_id=peer2(k), device_id_type=MESH,
        )

    def gather2_in(k):
        src = lax.rem(id2 + 16 - k, 16)
        return pltpu.make_async_remote_copy(
            src_ref=ar2.at[src], dst_ref=ar2.at[src], send_sem=t_send.at[k], recv_sem=t_recv.at[k],
            device_id=peer2(16 - k), device_id_type=MESH,
        )

    for k in (4, 5, 3, 2, 6, 7, 1):
        gather1(k).start()

    col_k = lax.rem(row_i, 128)
    paired = col_i // 2 == col_k
    even = lax.rem(col_i, 2) == 0
    for ab in range(4):
        e = jnp.where(even, kid[2 * ab], kid[2 * ab + 1])
        wout[ab] = jnp.where(paired, e, 0.0).astype(BF16)

    for side in range(2):
        edge = plane_of(0 if side == 0 else nx - 1)
        k = xcon[side]
        d = [k * (rs[f, edge] - xr_r[side, f]) for f in range(2)]
        d += [k * (qq[f, edge] - xr_q[side, f]) for f in range(2)]
        for j, (a, b) in enumerate(forms):
            sarr[j, 0 if side == 0 else nx - 1] += d[a] * d[b]
        k = ycon[side]
        d = [k * (ys_r[side, f] - yr_r[side, f]) for f in range(2)]
        d += [k * (ys_q[side, f] - yr_q[side, f]) for f in range(2)]
        for j, (a, b) in enumerate(forms):
            ysb[side, j] = d[a] * d[b]
    dr, dq = zcon[...] * zhal[0], zcon[...] * zhal[1]
    dr2, dq2 = pltpu.roll(dr, nz // 2, 1), pltpu.roll(dq, nz // 2, 1)
    zsb[0] = jnp.where(field0, dr * dr2, dq * dq2)
    zsb[1] = dr * dq2
    packed_at = ((0, 0), (1, 0), (1, 1), (0, 1))

    def scale_plane(i, carry):
        s = st[plane_of(i)]
        scale = 1.0 / (s * s)
        for j in range(4):
            buf, f = packed_at[j]
            g = sarr[j, i] + unpack(zsb[buf], f, i)
            g = add_rows(g, ysb[0, j, pl.ds(i, 1), :], ysb[1, j, pl.ds(i, 1), :])
            sarr[j, i] = scale * g
        return carry

    lax.fori_loop(0, nx // 2, scale_plane, 0, unroll=4)

    for k in range(1, 8):
        gather1_in(k).wait_recv()
    part = ar1[0]
    for k in range(1, 8):
        part = part + ar1[k]
    ar2[id2] = part
    for k in (12, 4, 13, 11, 5, 3, 8, 10, 14, 6, 2, 9, 7, 1, 15):
        gather2(k).start()

    lax.fori_loop(nx // 2, nx, scale_plane, 0, unroll=4)

    for ch in range(CHUNKS):
        for k in range(1, 4):
            a2a(ch, k).wait_send()
    for e in (ST, RH, QH):
        for axis, side in faces:
            end_face(e, axis, side)
    for k in range(1, 8):
        gather1(k).wait_send()

    for k in range(1, 16):
        gather2_in(k).wait_recv()
    whole = ar2[0]
    for k in range(1, 16):
        whole = whole + ar2[k]

    whole = jnp.where(row8 == lane8, whole, 0.0)
    coef[...] = jnp.broadcast_to(jnp.sum(whole, axis=1, keepdims=True), coef.shape)
    m0, m1, m2, m3 = (coef[pl.ds(2 * k, 2), :] for k in range(4))
    step0 = m0 / (m1 + TINY)
    rr1 = jnp.maximum(m0 - 2.0 * step0 * m1 + step0 * step0 * m2, 0.0)
    beta = rr1 / (m0 + TINY)
    r_a_r = m1 - 2.0 * step0 * m2 + step0 * step0 * m3
    r_a_d = m1 - step0 * m2
    d_a_d = r_a_r + 2.0 * beta * r_a_d + beta * beta * m1
    step1 = jnp.minimum(rr1 / (jnp.maximum(d_a_d, 0.0) + TINY), MAX_STEP)
    c0 = step0 + step1 * (1.0 + beta)
    c1 = -step0 * step1
    mix = [c0[0:1] * c0[1:2], c0[0:1] * c1[1:2], c1[0:1] * c0[1:2], c1[0:1] * c1[1:2]]

    def back(ch, k):
        dst = lax.rem(me + k, n_dev)
        part = pl.ds(ch * nx * 8 // BACKS, nx * 8 // BACKS)
        return pltpu.make_async_remote_copy(
            src_ref=bsend.at[dst, part],
            dst_ref=out.at[me, part],
            send_sem=b_send.at[ch, k - 1],
            recv_sem=b_recv.at[ch, k - 1],
            device_id={"gx": gx, "gy": gy, "dev": dst},
            device_id_type=MESH,
        )

    def back_in(ch, k):
        src = lax.rem(me + n_dev - k, n_dev)
        part = pl.ds(ch * nx * 8 // BACKS, nx * 8 // BACKS)
        return pltpu.make_async_remote_copy(
            src_ref=bsend.at[src, part],
            dst_ref=out.at[src, part],
            send_sem=b_send.at[ch, k - 1],
            recv_sem=b_recv.at[ch, k - 1],
            device_id={"gx": gx, "gy": gy, "dev": src},
            device_id_type=MESH,
        )

    def pair_planes(p, carry):
        v = None
        for j in range(4):
            add = mix[j] * sarr[j, pl.ds(2 * p, 2)]
            v = add if v is None else v + add
        for d in range(n_dev):
            two = v[:, 8 * d : 8 * d + 8, :].reshape(16, nz)
            bsend[d, pl.ds(pl.multiple_of(p * 16, 16), 16), :] = two.astype(BF16)
        return carry

    for ch in range(BACKS):
        lax.fori_loop(ch * nx // 2 // BACKS, (ch + 1) * nx // 2 // BACKS, pair_planes, 0, unroll=4)
        for k in (2, 1, 3):
            back(ch, k).start()
    own = pltpu.make_async_copy(bsend.at[me], out.at[me], o_sem)
    own.start()
    for k in range(1, 16):
        gather2(k).wait_send()
    own.wait()
    for ch in range(BACKS):
        for k in (2, 1, 3):
            back(ch, k).wait_send()
            back_in(ch, k).wait_recv()


def expand_kernel(s_ref, d_ref, w_ref, o_hbm, obuf, o_sem):
    n_dev, rows, nz = s_ref.shape
    nx = rows // 8
    per = nx // STEPS

    def store(c, l):
        return pltpu.make_async_copy(
            obuf.at[l, pl.ds(c * 2 * per, 2 * per)],
            o_hbm.at[pl.ds(c * 2 * per, 2 * per), :, pl.ds(128 * l, 128)],
            o_sem.at[c, l],
        )

    for c in range(STEPS):
        part = pl.ds(c * per * 8, per * 8)
        for d in range(n_dev):
            dens = d_ref[d, part]
            v = (-1.5 * (1.0 - FLOOR) * GAIN) * dens * dens * s_ref[d, part].astype(F32)
            high = v.astype(BF16)
            low = (v - high.astype(F32)).astype(BF16)
            lhs = jnp.concatenate([high, low], axis=1)
            for a in range(2):
                for b in range(2):
                    t = jnp.dot(lhs, w_ref[2 * a + b], preferred_element_type=F32)
                    for i in range(per):
                        for h in range(2):
                            obuf[2 * d + h, 2 * (c * per + i) + a, pl.ds(b, 8, stride=2), :] = t[
                                8 * i : 8 * i + 8, 128 * h : 128 * h + 128
                            ]
            for h in range(2):
                store(c, 2 * d + h).start()
    for c in range(STEPS):
        for l in range(2 * n_dev):
            store(c, l).wait()


def solution(mesh):
    n_gx, n_gy, n_dev = mesh.shape["gx"], mesh.shape["gy"], mesh.shape["dev"]

    def body(design, tap_offsets, tap_weights, input_load, input_mask, output_mask, fixed_mask):
        nx, ny, nz = input_load.shape
        cell = (nx, ny, nz)
        plane = (ny, nz)
        padded = ((nx + 2) * ny, nz)
        hbm = pl.BlockSpec(memory_space=pl.ANY)
        vmem = pl.BlockSpec(memory_space=pltpu.VMEM)
        vm = lambda *shape: pltpu.VMEM(shape, F32)
        dma = lambda *shape: pltpu.SemaphoreType.DMA(shape)
        taps = [pltpu.SMEM((3, 16), I32), pltpu.SMEM((16,), F32)]
        scratch = [
            pltpu.VMEM((nx, 2, 16, 1024), BF16),
            vm(*cell), pltpu.VMEM(cell, I32), pltpu.VMEM(cell, I32), pltpu.VMEM(cell, I32),
            pltpu.VMEM((2, 256, 256), BF16),
            vm(n_dev, 2, nx // CHUNKS * 16, 128),
            pltpu.VMEM((n_dev, nx * 8, nz), I16),
            pltpu.VMEM((n_dev, nx * 8, nz), I16),
            vm(*padded), vm(2, *padded), vm(2, *padded),
            vm(*cell), vm(2, *cell), vm(2, *cell),
            vm(*cell), vm(*padded), vm(*cell), vm(*cell),
            vm(4, *cell),
            vm(4, *plane),
            vm(2, *plane), vm(2, 2, *plane), vm(2, 2, *plane),
            vm(2, nx, nz), vm(2, 2, nx, nz), vm(2, 2, nx, nz),
            vm(2, nx, nz), vm(2, 2, nx, nz), vm(2, 2, nx, nz),
            vm(*plane), vm(*plane), vm(*plane),
            vm(2, *plane), vm(2, *plane), vm(2, *plane),
            vm(2, 2, nx, nz), vm(*plane), vm(*plane), vm(2, nx, nz), vm(2, *plane), vm(2, *plane),
            vm(2, 4, nx, nz), vm(2, *plane),
            vm(8, 1, 128), vm(16, 1, 128), vm(8, 128),
            pltpu.VMEM((n_dev, nx * 8, nz), BF16),
            vm(2, 2, *plane),
            *taps, dma(2),
            dma(CHUNKS + 4), dma(CHUNKS, 3), dma(CHUNKS, 3), dma(3, 6), dma(3, 6),
            dma(8), dma(8), dma(16), dma(16), dma(BACKS, 3), dma(BACKS, 3), pltpu.SemaphoreType.DMA,
            pltpu.SemaphoreType.REGULAR,
        ]
        returned, local, fold = pl.pallas_call(
            functools.partial(step_kernel, n_gx, n_gy, n_dev),
            out_shape=(
                jax.ShapeDtypeStruct((n_dev, nx * 8, nz), BF16),
                jax.ShapeDtypeStruct((n_dev, nx * 8, nz), F32),
                jax.ShapeDtypeStruct((4, 256, 256), BF16),
            ),
            in_specs=[hbm] * 7,
            out_specs=(vmem, vmem, vmem),
            scratch_shapes=scratch,
            compiler_params=pltpu.CompilerParams(
                collective_id=0, has_side_effects=True, vmem_limit_bytes=40000 * 1024
            ),
            name="step",
        )(
            *(
                pltpu.with_memory_space_constraint(v, pltpu.HBM)
                for v in (
                    design.reshape(nx, 2, 16, 1024), input_load, input_mask, output_mask, fixed_mask,
                    tap_offsets.T, tap_weights,
                )
            )
        )
        return pl.pallas_call(
            expand_kernel,
            out_shape=jax.ShapeDtypeStruct(design.shape, F32),
            in_specs=[vmem] * 3,
            out_specs=hbm,
            scratch_shapes=[vm(2 * n_dev, 2 * nx, 16, 128), dma(STEPS, 2 * n_dev)],
            compiler_params=pltpu.CompilerParams(vmem_limit_bytes=32 * 1024 * 1024),
            name="expand",
        )(returned, local, fold)

    block = P("gx", "gy", "dev")
    owner = P("gx", ("gy", "dev"), None)
    return jax.shard_map(
        body, mesh=mesh,
        in_specs=(owner, P(), P(), block, block, block, block),
        out_specs=owner,
        check_vma=False,
    )
```

```python
import functools

import jax
import jax.numpy as jnp
from jax import lax
from jax.experimental import pallas as pl
from jax.experimental.pallas import tpu as pltpu
from jax.sharding import PartitionSpec as P

MESH = pl.DeviceIdType.MESH

FLOOR = 0.01
GROUND = 0.1
PORT = 0.5
GAIN = 64.0
TINY = 1e-06
MAX_STEP = 10.0

CODE = 32000.0
ORDER = (0, 3, 1, 2)
CHUNKS = len(ORDER)
BACKS = 1
STEPS = 1
F32 = jnp.float32
BF16 = jnp.bfloat16
I16 = jnp.int16
I32 = jnp.int32

ST, RH, QH = 0, 1, 2


def child_rows(offs, wts, lanes):
    taps = wts.shape[0]
    total = wts[0]
    for t in range(1, taps):
        total = total + wts[t]
    sums = [jnp.float32(0.0)] * 8
    for t in range(taps):
        code = offs[0, t] * 4 + offs[1, t] * 2 + offs[2, t]
        for c in range(8):
            sums[c] = sums[c] + jnp.where(code == c, wts[t], jnp.float32(0.0))
    below = jnp.full((1, lanes), total, F32)
    return [jnp.full((1, lanes), s, F32) / below for s in sums]


def between(a, b):
    return 2.0 * a * b / (a + b)


def step_kernel(
    n_gx, n_gy, n_dev,
    design, load, imask, omask, fmask, offs_hbm, wts_hbm,
    out, dloc, wout,
    dbuf, lbuf, ibuf, obuf, fbuf,
    wmat, pbuf, isend, irecv, st, rs, qq, diag, dzu, dzl,
    cx, cy, czu, czl, sarr, gprev,
    xr_st, xr_r, xr_q,
    ys_st, ys_r, ys_q, yr_st, yr_r, yr_q,
    zs_st, zs_r, zs_q, zr_st, zr_r, zr_q,
    yflux, zflux, zcon, ycon, xcon, zhal,
    ysb, zsb,
    ar1, ar2, coef, bsend, xq,
    offs, wts, tap_sem, in_sem, a_send, a_recv, h_send, h_recv, s_send, s_recv, t_send, t_recv,
    b_send, b_recv, ready,
):
    gx = lax.axis_index("gx")
    gy = lax.axis_index("gy")
    me = lax.axis_index("dev")
    nx, ny, nz = lbuf.shape
    per = nx // CHUNKS
    rows = per * 8
    core = lax.rem(gy, 2)
    half = gy // 2
    ypos = lax.rem(gx, 4)
    zpos = gx // 4 * 2 + half

    taps_in = [
        pltpu.make_async_copy(offs_hbm, offs, tap_sem.at[0]),
        pltpu.make_async_copy(wts_hbm, wts, tap_sem.at[1]),
    ]
    for c in taps_in:
        c.start()
    ins = {}
    for ch in ORDER:
        c = pltpu.make_async_copy(
            design.at[pl.ds(ch * per, per)], dbuf.at[pl.ds(ch * per, per)], in_sem.at[ch]
        )
        c.start()
        ins[ch] = c
    for ref in (xr_st, xr_r, xr_q, yr_st, yr_r, yr_q, zr_st, zr_r, zr_q):
        ref[...] = jnp.zeros_like(ref)

    id1 = me * 2 + core
    id2 = gx * 2 + half

    def peer1(k):
        other = lax.rem(id1 + k, 8)
        return {"gx": gx, "gy": half * 2 + lax.rem(other, 2), "dev": other // 2}

    def peer2(k):
        other = lax.rem(id2 + k, 16)
        return {"gx": other // 2, "gy": lax.rem(other, 2) * 2 + core, "dev": me}

    def peer_y(k):
        return {"gx": gx // 4 * 4 + lax.rem(ypos + k, 4), "gy": gy, "dev": me}

    def peer_z(k):
        z = lax.rem(zpos + k, 4)
        return {"gx": z // 2 * 4 + ypos, "gy": lax.rem(z, 2) * 2 + core, "dev": me}

    barrier = pltpu.get_barrier_semaphore()
    near = [peer1(k) for k in (4, 5, 3)] + [peer_y(2), peer_z(2)] + [peer1(k) for k in (2, 6, 7, 1)]
    near += [at(k) for at in (peer_y, peer_z) for k in (1, 3)]
    near += [{"gx": gx, "gy": n_gy - 1 - gy, "dev": me}]
    for peer in near:
        pl.semaphore_signal(barrier, inc=1, device_id=peer, device_id_type=MESH)

    fields_in = []
    for k, (a, b) in enumerate(((load, lbuf), (imask, ibuf), (omask, obuf), (fmask, fbuf))):
        c = pltpu.make_async_copy(a, b, in_sem.at[CHUNKS + k])
        c.start()
        fields_in.append(c)

    for c in taps_in:
        c.wait()
    kid = child_rows(offs, wts, 256)
    row_i = lax.broadcasted_iota(I32, (256, 256), 0)
    col_i = lax.broadcasted_iota(I32, (256, 256), 1)
    paired = row_i // 2 == lax.rem(col_i, 128)
    even = lax.rem(row_i, 2) == 0
    left = col_i < 128
    for a in range(2):
        e = jnp.where(
            even,
            jnp.where(left, kid[4 * a], kid[4 * a + 2]),
            jnp.where(left, kid[4 * a + 1], kid[4 * a + 3]),
        )
        wmat[a] = jnp.where(paired, e, 0.0).astype(BF16)

    def a2a(ch, k):
        dst = lax.rem(me + k, n_dev)
        part = pl.ds(ch * rows, rows)
        return pltpu.make_async_remote_copy(
            src_ref=isend.at[dst, part],
            dst_ref=irecv.at[me, part],
            send_sem=a_send.at[ch, k - 1],
            recv_sem=a_recv.at[ch, k - 1],
            device_id={"gx": gx, "gy": gy, "dev": dst},
            device_id_type=MESH,
        )

    def a2a_in(ch, k):
        src = lax.rem(me + n_dev - k, n_dev)
        part = pl.ds(ch * rows, rows)
        return pltpu.make_async_remote_copy(
            src_ref=isend.at[src, part],
            dst_ref=irecv.at[src, part],
            send_sem=a_send.at[ch, k - 1],
            recv_sem=a_recv.at[ch, k - 1],
            device_id={"gx": gx, "gy": gy, "dev": src},
            device_id_type=MESH,
        )

    for ch in ORDER:
        ins[ch].wait()
        part = pl.ds(ch * rows, rows)
        for c in range(n_dev):
            total = None
            for a in range(2):
                lhs = dbuf[pl.ds(ch * per, per), a, :, pl.ds(256 * c, 256)].reshape(per * 16, 256)
                add = jnp.dot(lhs, wmat[a], preferred_element_type=F32)
                total = add if total is None else total + add
            pbuf[c, 0] = total[:, :128]
            pbuf[c, 1] = total[:, 128:]
            d = pbuf[c, 0, pl.ds(0, rows, stride=2), :] + pbuf[c, 1, pl.ds(1, rows, stride=2), :]
            dloc[c, part] = d
            isend[c, part] = (d * CODE + 0.5).astype(I32).astype(I16)
        if ch == ORDER[0]:
            pl.semaphore_wait(barrier, len(near))
        for k in (2, 1, 3):
            a2a(ch, k).start()
        irecv[me, part] = isend[me, part]
    for k in range(1, 4):
        pl.semaphore_signal(ready, inc=1, device_id=peer_y(k), device_id_type=MESH)

    def plane_of(i):
        return pl.ds(pl.multiple_of((i + 1) * ny, ny), ny)

    def xsend(e, side):
        where = plane_of(0 if side == 0 else nx - 1)
        if e == ST:
            return st.at[where]
        return rs.at[:, where] if e == RH else xq.at[side]

    xrecv = {ST: xr_st, RH: xr_r, QH: xr_q}
    ysend = {ST: ys_st, RH: ys_r, QH: ys_q}
    yrecv = {ST: yr_st, RH: yr_r, QH: yr_q}
    zsend = {ST: zs_st, RH: zs_r, QH: zs_q}
    zrecv = {ST: zr_st, RH: zr_r, QH: zr_q}
    spot = {"gx": (gx, n_gx), "gy": (gy, n_gy), "dev": (me, n_dev)}

    def face(e, axis, side):
        k = {"gx": 0, "gy": 2, "dev": 4}[axis] + side
        if axis == "gx":
            src, dst = xsend(e, side), xrecv[e].at[1 - side]
        elif axis == "gy":
            src, dst = ysend[e].at[side], yrecv[e].at[1 - side]
        else:
            src, dst = zsend[e], zrecv[e].at[1 - side]
        pos, size = spot[axis]
        target = {"gx": gx, "gy": gy, "dev": me}
        target[axis] = jnp.clip(pos - 1 if side == 0 else pos + 1, 0, size - 1)
        copy = pltpu.make_async_remote_copy(
            src_ref=src, dst_ref=dst, send_sem=h_send.at[e, k], recv_sem=h_recv.at[e, k],
            device_id=target, device_id_type=MESH,
        )
        sends = pos > 0 if side == 0 else pos < size - 1
        gets = pos < size - 1 if side == 0 else pos > 0
        return copy, sends, gets

    def start_face(e, axis, side):
        copy, sends, _ = face(e, axis, side)

        @pl.when(sends)
        def _():
            copy.start()

    def wait_face(e, axis, side):
        copy, _, gets = face(e, axis, side)

        @pl.when(gets)
        def _():
            copy.wait_recv()

    def end_face(e, axis, side):
        copy, sends, _ = face(e, axis, side)

        @pl.when(sends)
        def _():
            copy.wait_send()

    faces = [(axis, side) for axis in ("gx", "gy", "dev") for side in range(2)]

    iy = lax.broadcasted_iota(I32, (ny, nz), 0)
    iz = lax.broadcasted_iota(I32, (ny, nz), 1)
    first_y, last_y = iy == 0, iy == ny - 1
    first_z, last_z = iz == 0, iz == nz - 1
    ends_z = jnp.logical_or(first_z, last_z)
    key = ((iz + 1) // 2) % 64
    low_lane = lax.rem(iz, 2) == 0
    field0 = key < 32
    top8 = lax.broadcasted_iota(I32, (8, nz), 0) == 0
    end8 = lax.broadcasted_iota(I32, (8, nz), 0) == 7
    zero = jnp.zeros((ny, nz), F32)
    none = jnp.zeros((8, nz), F32)

    def fold(v):
        return jnp.sum(v.reshape(ny // 8, 8, nz), axis=0)

    def pack(into, v, f, i):
        return jnp.where(key == 32 * f + i, pltpu.roll(v, 64 * f + 2 * i, 1), into)

    def unpack(packed, f, i):
        by = 2 * nz - 64 * f - 2 * i
        by = by % nz if isinstance(i, int) else lax.rem(by, nz)
        return jnp.where(ends_z, pltpu.roll(packed, by, 1), 0.0)

    def add_rows(v, low, high):
        return jnp.concatenate(
            [v[:8] + jnp.where(top8, low, 0.0), v[8:-8], v[-8:] + jnp.where(end8, high, 0.0)], axis=0
        )

    def z_halo(ref):
        return jnp.where(low_lane, pltpu.roll(ref[0], 1, 1), pltpu.roll(ref[1], nz - 1, 1))

    for c in fields_in:
        c.wait()
    for ends in (pl.ds(0, ny), pl.ds((nx + 1) * ny, ny)):
        st[ends] = zero
        cy[ends] = zero
        for f in range(2):
            rs[f, ends] = zero
            qq[f, ends] = zero

    def load_plane(i, carry):
        zpack, m0r, m0s = carry
        im, om = ibuf[i].astype(F32), obuf[i].astype(F32)
        r, s = im * lbuf[i], om
        diag[i] = GROUND + fbuf[i].astype(F32) + PORT * (im + om)
        for f, v in enumerate((r, s)):
            rs[f, plane_of(i)] = v
            dzu[f, i] = v - pltpu.roll(v, nz - 1, 1)
            dzl[f, i] = v - pltpu.roll(v, 1, 1)
            ys_r[0, f, pl.ds(i, 1), :] = v[0:1]
            ys_r[1, f, pl.ds(i, 1), :] = v[ny - 1 : ny]
            zpack = pack(zpack, v, f, i)
        return zpack, m0r + fold(r * r), m0s + fold(s * s)

    zpack, m0r, m0s = lax.fori_loop(0, nx, load_plane, (zero, none, none), unroll=2)
    zs_r[...] = zpack
    pl.semaphore_wait(ready, 3)
    for axis, side in faces:
        start_face(RH, axis, side)

    def stiff_pair(p, zpack):
        d = [
            irecv[src, pl.ds(pl.multiple_of(16 * p, 16), 16)].astype(I32).astype(F32) * (1.0 / CODE)
            for src in range(n_dev)
        ]
        s = [FLOOR + (1.0 - FLOOR) * v * v * v for v in d]
        for h in range(2):
            i = 2 * p + h
            v = jnp.concatenate([t[8 * h : 8 * h + 8] for t in s], axis=0)
            st[plane_of(i)] = v
            ys_st[0, pl.ds(i, 1), :] = v[0:1]
            ys_st[1, pl.ds(i, 1), :] = v[ny - 1 : ny]
            zpack = pack(zpack, v, 0, i)
        return zpack

    zpack = zero
    for ch in ORDER:
        for k in (1, 3, 2):
            a2a_in(ch, k).wait_recv()
        zpack = lax.fori_loop(ch * per // 2, (ch + 1) * per // 2, stiff_pair, zpack, unroll=4)
        if ch == 0:
            start_face(ST, "gx", 0)
        if ch == CHUNKS - 1:
            start_face(ST, "gx", 1)
    zs_st[...] = jnp.where(field0, zpack, pltpu.roll(zpack, nz // 2, 1))
    for axis, side in faces[2:]:
        start_face(ST, axis, side)

    def inner_plane(i, carry):
        at = pl.multiple_of((i + 1) * ny, ny)
        here, after, up, down = pl.ds(at, ny), pl.ds(at + ny, ny), pl.ds(at + 1, ny), pl.ds(at - 1, ny)
        s = st[here]
        kx = between(s, st[after])
        kyu = between(s, jnp.where(last_y, 0.0, st[up]))
        kyl = between(s, jnp.where(first_y, 0.0, st[down]))
        kzu = between(s, jnp.where(last_z, 0.0, pltpu.roll(s, nz - 1, 1)))
        kzl = between(s, jnp.where(first_z, 0.0, pltpu.roll(s, 1, 1)))
        cx[i] = kx
        cy[here] = kyu
        czu[i] = kzu
        czl[i] = kzl
        dg = diag[i]
        new = []
        for f in range(2):
            v = rs[f, here]
            fx = kx * (v - rs[f, after])
            q = dg * v + (fx - carry[f])
            q += kyu * (v - rs[f, up]) + kyl * (v - rs[f, down])
            q += kzu * dzu[f, i] + kzl * dzl[f, i]
            qq[f, here] = q
            new.append(fx)
        return tuple(new)

    lax.fori_loop(0, nx, inner_plane, (zero, zero), unroll=2)

    for axis, side in faces:
        wait_face(RH, axis, side)
    for axis, side in faces[2:]:
        wait_face(ST, axis, side)

    kz = between(zs_st[...], z_halo(zr_st))
    zcon[...] = kz
    zhal[0] = zs_r[...] - z_halo(zr_r)
    zflux[...] = kz * zhal[0]
    for side in range(2):
        ycon[side] = between(ys_st[side], yr_st[side])
        for f in range(2):
            yflux[side, f] = ycon[side] * (ys_r[side, f] - yr_r[side, f])

    def with_edges(f, i):
        q = qq[f, plane_of(i)] + unpack(zflux[...], f, i)
        return add_rows(q, yflux[0, f, pl.ds(i, 1), :], yflux[1, f, pl.ds(i, 1), :])

    def finish(f, i, q, zpack, sums):
        qq[f, plane_of(i)] = q
        ys_q[0, f, pl.ds(i, 1), :] = q[0:1]
        ys_q[1, f, pl.ds(i, 1), :] = q[ny - 1 : ny]
        sums[f] += fold(rs[f, plane_of(i)] * q)
        sums[2 + f] += fold(q * q)
        return pack(zpack, q, f, i)

    def edge_plane(i, carry):
        zpack, sums = carry
        sums = list(sums)
        for f in range(2):
            zpack = finish(f, i, with_edges(f, i), zpack, sums)
        return zpack, tuple(sums)

    for side in range(2):
        for f in range(2):
            xq[side, f] = with_edges(f, 0 if side == 0 else nx - 1)
        start_face(QH, "gx", side)
    zpack, sums = lax.fori_loop(1, nx - 1, edge_plane, (zero, (none,) * 4), unroll=6)
    sums = list(sums)
    for side in range(2):
        wait_face(ST, "gx", side)
    for side in range(2):
        i = 0 if side == 0 else nx - 1
        xcon[side] = between(st[plane_of(i)], xr_st[side])
        for f in range(2):
            q = xq[side, f] + xcon[side] * (rs[f, plane_of(i)] - xr_r[side, f])
            zpack = finish(f, i, q, zpack, sums)
    sums12 = sums
    zs_q[...] = zpack
    for axis, side in faces[2:]:
        start_face(QH, axis, side)

    gprev[...] = jnp.zeros_like(gprev)
    forms = ((0, 1), (0, 3), (2, 1), (2, 3))

    def product_plane(i, carry):
        e_r, e_s = carry
        at = pl.multiple_of((i + 1) * ny, ny)
        here, after, up, down = pl.ds(at, ny), pl.ds(at + ny, ny), pl.ds(at + 1, ny), pl.ds(at - 1, ny)

        def get(where):
            return [rs[0, where], rs[1, where], qq[0, where], qq[1, where]]

        v = get(here)
        dg = diag[i]
        e_r += fold(dg * v[2] * v[2])
        e_s += fold(dg * v[3] * v[3])
        q_up = [pltpu.roll(v[f], nz - 1, 1) for f in (2, 3)]
        q_down = [pltpu.roll(v[f], 1, 1) for f in (2, 3)]

        def diffs(o):
            return [a - b for a, b in zip(v, o)]

        d = diffs(get(after))
        k = cx[i]
        t = [k * a for a in d]
        e_r += fold(t[2] * d[2])
        e_s += fold(t[3] * d[3])
        held = []
        for j, (a, b) in enumerate(forms):
            g = t[a] * t[b]
            held.append(g + gprev[j])
            gprev[j] = g
        sides = (
            (True, cy[here], lambda: diffs(get(up))),
            (False, cy[down], lambda: diffs(get(down))),
            (True, czu[i], lambda: [dzu[0, i], dzu[1, i], v[2] - q_up[0], v[3] - q_up[1]]),
            (False, czl[i], lambda: [dzl[0, i], dzl[1, i], v[2] - q_down[0], v[3] - q_down[1]]),
        )
        for own, k, make in sides:
            d = make()
            t = [k * a for a in d]
            if own:
                e_r += fold(t[2] * d[2])
                e_s += fold(t[3] * d[3])
            for j, (a, b) in enumerate(forms):
                held[j] += t[a] * t[b]
        for j in range(4):
            sarr[j, i] = held[j]
        return e_r, e_s

    e_r, e_s = lax.fori_loop(0, nx, product_plane, (none, none), unroll=2)

    for axis, side in faces:
        if side == 0:
            wait_face(QH, axis, side)
    for f in range(2):
        xr_q[1, f] += xcon[1] * (xr_r[1, f] - rs[f, plane_of(nx - 1)])

    dz = zs_q[...] - pltpu.roll(zr_q[1], nz - 1, 1)
    dz = zcon[...] * dz * dz
    parts = []
    for f in range(2):
        dx = qq[f, plane_of(nx - 1)] - xr_q[1, f]
        dy = ys_q[1, f] - yr_q[1, f]
        own = jnp.logical_and(jnp.logical_not(low_lane), field0 if f == 0 else jnp.logical_not(field0))
        parts.append(fold(xcon[1] * dx * dx + ycon[1] * dy * dy + jnp.where(own, dz, 0.0)))
    e_r += parts[0]
    e_s += parts[1]

    row8 = lax.broadcasted_iota(I32, (8, nz), 0)
    lane8 = lax.broadcasted_iota(I32, (8, nz), 1)
    tile = none
    for k, v in enumerate((m0r, m0s) + tuple(sums12) + (e_r, e_s)):
        tile = jnp.where(row8 == k, jnp.sum(v, axis=0, keepdims=True), tile)
    tile = jnp.where(row8 == lane8, jnp.sum(tile, axis=1, keepdims=True), 0.0)
    ar1[id1] = jnp.sum(tile, axis=0, keepdims=True)

    def gather1(k):
        return pltpu.make_async_remote_copy(
            src_ref=ar1.at[id1], dst_ref=ar1.at[id1], send_sem=s_send.at[k], recv_sem=s_recv.at[k],
            device_id=peer1(k), device_id_type=MESH,
        )

    def gather1_in(k):
        src = lax.rem(id1 + 8 - k, 8)
        return pltpu.make_async_remote_copy(
            src_ref=ar1.at[src], dst_ref=ar1.at[src], send_sem=s_send.at[k], recv_sem=s_recv.at[k],
            device_id=peer1(8 - k), device_id_type=MESH,
        )

    def gather2(k):
        return pltpu.make_async_remote_copy(
            src_ref=ar2.at[id2], dst_ref=ar2.at[id2], send_sem=t_send.at[k], recv_sem=t_recv.at[k],
            device_id=peer2(k), device_id_type=MESH,
        )

    def gather2_in(k):
        src = lax.rem(id2 + 16 - k, 16)
        return pltpu.make_async_remote_copy(
            src_ref=ar2.at[src], dst_ref=ar2.at[src], send_sem=t_send.at[k], recv_sem=t_recv.at[k],
            device_id=peer2(16 - k), device_id_type=MESH,
        )

    for k in (4, 5, 3, 2, 6, 7, 1):
        gather1(k).start()

    col_k = lax.rem(row_i, 128)
    paired = col_i // 2 == col_k
    even = lax.rem(col_i, 2) == 0
    for ab in range(4):
        e = jnp.where(even, kid[2 * ab], kid[2 * ab + 1])
        wout[ab] = jnp.where(paired, e, 0.0).astype(BF16)

    for axis, side in faces:
        if side == 1:
            wait_face(QH, axis, side)
    for f in range(2):
        xr_q[0, f] += xcon[0] * (xr_r[0, f] - rs[f, plane_of(0)])
    zhal[1] = zs_q[...] - z_halo(zr_q)
    for side in range(2):
        edge = plane_of(0 if side == 0 else nx - 1)
        k = xcon[side]
        d = [k * (rs[f, edge] - xr_r[side, f]) for f in range(2)]
        d += [k * (qq[f, edge] - xr_q[side, f]) for f in range(2)]
        for j, (a, b) in enumerate(forms):
            sarr[j, 0 if side == 0 else nx - 1] += d[a] * d[b]
        k = ycon[side]
        d = [k * (ys_r[side, f] - yr_r[side, f]) for f in range(2)]
        d += [k * (ys_q[side, f] - yr_q[side, f]) for f in range(2)]
        for j, (a, b) in enumerate(forms):
            ysb[side, j] = d[a] * d[b]
    dr, dq = zcon[...] * zhal[0], zcon[...] * zhal[1]
    dr2, dq2 = pltpu.roll(dr, nz // 2, 1), pltpu.roll(dq, nz // 2, 1)
    zsb[0] = jnp.where(field0, dr * dr2, dq * dq2)
    zsb[1] = dr * dq2
    packed_at = ((0, 0), (1, 0), (1, 1), (0, 1))

    def scale_plane(i, carry):
        s = st[plane_of(i)]
        scale = 1.0 / (s * s)
        for j in range(4):
            buf, f = packed_at[j]
            g = sarr[j, i] + unpack(zsb[buf], f, i)
            g = add_rows(g, ysb[0, j, pl.ds(i, 1), :], ysb[1, j, pl.ds(i, 1), :])
            sarr[j, i] = scale * g
        return carry

    lax.fori_loop(0, nx // 2, scale_plane, 0, unroll=4)

    for k in range(1, 8):
        gather1_in(k).wait_recv()
    part = ar1[0]
    for k in range(1, 8):
        part = part + ar1[k]
    ar2[id2] = part
    for k in (12, 4, 13, 11, 5, 3, 8, 10, 14, 6, 2, 9, 7, 1, 15):
        gather2(k).start()

    lax.fori_loop(nx // 2, nx, scale_plane, 0, unroll=4)

    for ch in range(CHUNKS):
        for k in range(1, 4):
            a2a(ch, k).wait_send()
    for e in (ST, RH, QH):
        for axis, side in faces:
            end_face(e, axis, side)
    for k in range(1, 8):
        gather1(k).wait_send()

    for k in range(1, 16):
        gather2_in(k).wait_recv()
    whole = ar2[0]
    for k in range(1, 16):
        whole = whole + ar2[k]

    whole = jnp.where(row8 == lane8, whole, 0.0)
    coef[...] = jnp.broadcast_to(jnp.sum(whole, axis=1, keepdims=True), coef.shape)
    m0, m1, m2, m3 = (coef[pl.ds(2 * k, 2), :] for k in range(4))
    step0 = m0 / (m1 + TINY)
    rr1 = jnp.maximum(m0 - 2.0 * step0 * m1 + step0 * step0 * m2, 0.0)
    beta = rr1 / (m0 + TINY)
    r_a_r = m1 - 2.0 * step0 * m2 + step0 * step0 * m3
    r_a_d = m1 - step0 * m2
    d_a_d = r_a_r + 2.0 * beta * r_a_d + beta * beta * m1
    step1 = jnp.minimum(rr1 / (jnp.maximum(d_a_d, 0.0) + TINY), MAX_STEP)
    c0 = step0 + step1 * (1.0 + beta)
    c1 = -step0 * step1
    mix = [c0[0:1] * c0[1:2], c0[0:1] * c1[1:2], c1[0:1] * c0[1:2], c1[0:1] * c1[1:2]]

    def back(ch, k):
        dst = lax.rem(me + k, n_dev)
        part = pl.ds(ch * nx * 8 // BACKS, nx * 8 // BACKS)
        return pltpu.make_async_remote_copy(
            src_ref=bsend.at[dst, part],
            dst_ref=out.at[me, part],
            send_sem=b_send.at[ch, k - 1],
            recv_sem=b_recv.at[ch, k - 1],
            device_id={"gx": gx, "gy": gy, "dev": dst},
            device_id_type=MESH,
        )

    def back_in(ch, k):
        src = lax.rem(me + n_dev - k, n_dev)
        part = pl.ds(ch * nx * 8 // BACKS, nx * 8 // BACKS)
        return pltpu.make_async_remote_copy(
            src_ref=bsend.at[src, part],
            dst_ref=out.at[src, part],
            send_sem=b_send.at[ch, k - 1],
            recv_sem=b_recv.at[ch, k - 1],
            device_id={"gx": gx, "gy": gy, "dev": src},
            device_id_type=MESH,
        )

    def combine(into, slot, group):
        lines = pl.ds(pl.multiple_of(8 * group, 8), 8)

        def pair_planes(p, carry):
            v = None
            for j in range(4):
                add = mix[j] * sarr[j, pl.ds(2 * p, 2), lines]
                v = add if v is None else v + add
            into[slot, pl.ds(pl.multiple_of(p * 16, 16), 16)] = v.reshape(16, nz).astype(BF16)
            return carry

        lax.fori_loop(0, nx // 2, pair_planes, 0, unroll=8)

    for k in (2, 1, 3):
        dst = lax.rem(me + k, n_dev)
        combine(bsend, dst, dst)
        back(0, k).start()
    combine(out, me, me)
    for k in range(1, 16):
        gather2(k).wait_send()
    for ch in range(BACKS):
        for k in (2, 1, 3):
            back(ch, k).wait_send()
            back_in(ch, k).wait_recv()


def expand_kernel(s_ref, d_ref, w_ref, o_hbm, obuf, o_sem):
    n_dev, rows, nz = s_ref.shape
    nx = rows // 8
    per = nx // STEPS

    def store(c, l):
        return pltpu.make_async_copy(
            obuf.at[l, pl.ds(c * 2 * per, 2 * per)],
            o_hbm.at[pl.ds(c * 2 * per, 2 * per), :, pl.ds(128 * l, 128)],
            o_sem.at[c, l],
        )

    for c in range(STEPS):
        part = pl.ds(c * per * 8, per * 8)
        for d in range(n_dev):
            dens = d_ref[d, part]
            v = (-1.5 * (1.0 - FLOOR) * GAIN) * dens * dens * s_ref[d, part].astype(F32)
            high = v.astype(BF16)
            low = (v - high.astype(F32)).astype(BF16)
            lhs = jnp.concatenate([high, low], axis=1)
            for a in range(2):
                for b in range(2):
                    t = jnp.dot(lhs, w_ref[2 * a + b], preferred_element_type=F32)
                    for i in range(per):
                        for h in range(2):
                            obuf[2 * d + h, 2 * (c * per + i) + a, pl.ds(b, 8, stride=2), :] = t[
                                8 * i : 8 * i + 8, 128 * h : 128 * h + 128
                            ]
            for h in range(2):
                store(c, 2 * d + h).start()
    for c in range(STEPS):
        for l in range(2 * n_dev):
            store(c, l).wait()


def solution(mesh):
    n_gx, n_gy, n_dev = mesh.shape["gx"], mesh.shape["gy"], mesh.shape["dev"]

    def body(design, tap_offsets, tap_weights, input_load, input_mask, output_mask, fixed_mask):
        nx, ny, nz = input_load.shape
        cell = (nx, ny, nz)
        plane = (ny, nz)
        padded = ((nx + 2) * ny, nz)
        hbm = pl.BlockSpec(memory_space=pl.ANY)
        vmem = pl.BlockSpec(memory_space=pltpu.VMEM)
        vm = lambda *shape: pltpu.VMEM(shape, F32)
        dma = lambda *shape: pltpu.SemaphoreType.DMA(shape)
        taps = [pltpu.SMEM((3, 16), I32), pltpu.SMEM((16,), F32)]
        scratch = [
            pltpu.VMEM((nx, 2, 16, 1024), BF16),
            vm(*cell), pltpu.VMEM(cell, I32), pltpu.VMEM(cell, I32), pltpu.VMEM(cell, I32),
            pltpu.VMEM((2, 256, 256), BF16),
            vm(n_dev, 2, nx // CHUNKS * 16, 128),
            pltpu.VMEM((n_dev, nx * 8, nz), I16),
            pltpu.VMEM((n_dev, nx * 8, nz), I16),
            vm(*padded), vm(2, *padded), vm(2, *padded),
            vm(*cell), vm(2, *cell), vm(2, *cell),
            vm(*cell), vm(*padded), vm(*cell), vm(*cell),
            vm(4, *cell),
            vm(4, *plane),
            vm(2, *plane), vm(2, 2, *plane), vm(2, 2, *plane),
            vm(2, nx, nz), vm(2, 2, nx, nz), vm(2, 2, nx, nz),
            vm(2, nx, nz), vm(2, 2, nx, nz), vm(2, 2, nx, nz),
            vm(*plane), vm(*plane), vm(*plane),
            vm(2, *plane), vm(2, *plane), vm(2, *plane),
            vm(2, 2, nx, nz), vm(*plane), vm(*plane), vm(2, nx, nz), vm(2, *plane), vm(2, *plane),
            vm(2, 4, nx, nz), vm(2, *plane),
            vm(8, 1, 128), vm(16, 1, 128), vm(8, 128),
            pltpu.VMEM((n_dev, nx * 8, nz), BF16),
            vm(2, 2, *plane),
            *taps, dma(2),
            dma(CHUNKS + 4), dma(CHUNKS, 3), dma(CHUNKS, 3), dma(3, 6), dma(3, 6),
            dma(8), dma(8), dma(16), dma(16), dma(BACKS, 3), dma(BACKS, 3),
            pltpu.SemaphoreType.REGULAR,
        ]
        returned, local, fold = pl.pallas_call(
            functools.partial(step_kernel, n_gx, n_gy, n_dev),
            out_shape=(
                jax.ShapeDtypeStruct((n_dev, nx * 8, nz), BF16),
                jax.ShapeDtypeStruct((n_dev, nx * 8, nz), F32),
                jax.ShapeDtypeStruct((4, 256, 256), BF16),
            ),
            in_specs=[hbm] * 7,
            out_specs=(vmem, vmem, vmem),
            scratch_shapes=scratch,
            compiler_params=pltpu.CompilerParams(
                collective_id=0, has_side_effects=True, vmem_limit_bytes=40000 * 1024
            ),
            name="step",
        )(
            *(
                pltpu.with_memory_space_constraint(v, pltpu.HBM)
                for v in (
                    design.reshape(nx, 2, 16, 1024), input_load, input_mask, output_mask, fixed_mask,
                    tap_offsets.T, tap_weights,
                )
            )
        )
        return pl.pallas_call(
            expand_kernel,
            out_shape=jax.ShapeDtypeStruct(design.shape, F32),
            in_specs=[vmem] * 3,
            out_specs=hbm,
            scratch_shapes=[vm(2 * n_dev, 2 * nx, 16, 128), dma(STEPS, 2 * n_dev)],
            compiler_params=pltpu.CompilerParams(vmem_limit_bytes=32 * 1024 * 1024),
            name="expand",
        )(returned, local, fold)

    block = P("gx", "gy", "dev")
    owner = P("gx", ("gy", "dev"), None)
    return jax.shard_map(
        body, mesh=mesh,
        in_specs=(owner, P(), P(), block, block, block, block),
        out_specs=owner,
        check_vma=False,
    )
```

```python
import functools

import jax
import jax.numpy as jnp
from jax import lax
from jax.experimental import pallas as pl
from jax.experimental.pallas import tpu as pltpu
from jax.sharding import PartitionSpec as P

MESH = pl.DeviceIdType.MESH

FLOOR = 0.01
GROUND = 0.1
PORT = 0.5
GAIN = 64.0
TINY = 1e-06
MAX_STEP = 10.0

CODE = 32000.0
ORDER = (0, 3, 1, 2)
CHUNKS = len(ORDER)
BACKS = 1
STEPS = 1
F32 = jnp.float32
BF16 = jnp.bfloat16
I16 = jnp.int16
I32 = jnp.int32

ST, RH, QH = 0, 1, 2


def child_rows(offs, wts, lanes):
    taps = wts.shape[0]
    total = wts[0]
    for t in range(1, taps):
        total = total + wts[t]
    sums = [jnp.float32(0.0)] * 8
    for t in range(taps):
        code = offs[0, t] * 4 + offs[1, t] * 2 + offs[2, t]
        for c in range(8):
            sums[c] = sums[c] + jnp.where(code == c, wts[t], jnp.float32(0.0))
    below = jnp.full((1, lanes), total, F32)
    return [jnp.full((1, lanes), s, F32) / below for s in sums]


def between(a, b):
    return 2.0 * a * b / (a + b)


def step_kernel(
    n_gx, n_gy, n_dev,
    design, load, imask, omask, fmask, offs_hbm, wts_hbm,
    out, dloc, wout,
    dbuf, lbuf, ibuf, obuf, fbuf,
    wmat, pbuf, isend, irecv, st, rs, qq, diag, dzu, dzl,
    cx, cy, czu, czl, sarr, gprev,
    xr_st, xr_r, xr_q,
    ys_st, ys_r, ys_q, yr_st, yr_r, yr_q,
    zs_st, zs_r, zs_q, zr_st, zr_r, zr_q,
    yflux, zflux, zcon, ycon, xcon, zhal,
    ysb, zsb,
    ar1, ar2, coef, bsend, xq,
    offs, wts, tap_sem, in_sem, a_send, a_recv, h_send, h_recv, s_send, s_recv, t_send, t_recv,
    b_send, b_recv, ready,
):
    gx = lax.axis_index("gx")
    gy = lax.axis_index("gy")
    me = lax.axis_index("dev")
    nx, ny, nz = lbuf.shape
    per = nx // CHUNKS
    rows = per * 8
    core = lax.rem(gy, 2)
    half = gy // 2
    ypos = lax.rem(gx, 4)
    zpos = gx // 4 * 2 + half

    taps_in = [
        pltpu.make_async_copy(offs_hbm, offs, tap_sem.at[0]),
        pltpu.make_async_copy(wts_hbm, wts, tap_sem.at[1]),
    ]
    for c in taps_in:
        c.start()
    ins = {}
    for ch in ORDER:
        c = pltpu.make_async_copy(
            design.at[pl.ds(ch * per, per)], dbuf.at[pl.ds(ch * per, per)], in_sem.at[ch]
        )
        c.start()
        ins[ch] = c
    for ref in (xr_st, xr_r, xr_q, yr_st, yr_r, yr_q, zr_st, zr_r, zr_q):
        ref[...] = jnp.zeros_like(ref)

    id1 = me * 2 + core
    id2 = gx * 2 + half

    def peer1(k):
        other = lax.rem(id1 + k, 8)
        return {"gx": gx, "gy": half * 2 + lax.rem(other, 2), "dev": other // 2}

    def peer2(k):
        other = lax.rem(id2 + k, 16)
        return {"gx": other // 2, "gy": lax.rem(other, 2) * 2 + core, "dev": me}

    def peer_y(k):
        return {"gx": gx // 4 * 4 + lax.rem(ypos + k, 4), "gy": gy, "dev": me}

    def peer_z(k):
        z = lax.rem(zpos + k, 4)
        return {"gx": z // 2 * 4 + ypos, "gy": lax.rem(z, 2) * 2 + core, "dev": me}

    barrier = pltpu.get_barrier_semaphore()
    near = [peer1(k) for k in (4, 5, 3)] + [peer_y(2), peer_z(2)] + [peer1(k) for k in (2, 6, 7, 1)]
    near += [at(k) for at in (peer_y, peer_z) for k in (1, 3)]
    near += [{"gx": gx, "gy": n_gy - 1 - gy, "dev": me}]
    for peer in near:
        pl.semaphore_signal(barrier, inc=1, device_id=peer, device_id_type=MESH)

    fields_in = []
    for k, (a, b) in enumerate(((load, lbuf), (imask, ibuf), (omask, obuf), (fmask, fbuf))):
        c = pltpu.make_async_copy(a, b, in_sem.at[CHUNKS + k])
        c.start()
        fields_in.append(c)

    for c in taps_in:
        c.wait()
    kid = child_rows(offs, wts, 256)
    row_i = lax.broadcasted_iota(I32, (256, 256), 0)
    col_i = lax.broadcasted_iota(I32, (256, 256), 1)
    paired = row_i // 2 == lax.rem(col_i, 128)
    even = lax.rem(row_i, 2) == 0
    left = col_i < 128
    for a in range(2):
        e = jnp.where(
            even,
            jnp.where(left, kid[4 * a], kid[4 * a + 2]),
            jnp.where(left, kid[4 * a + 1], kid[4 * a + 3]),
        )
        wmat[a] = jnp.where(paired, e, 0.0).astype(BF16)

    def a2a(ch, k):
        dst = lax.rem(me + k, n_dev)
        part = pl.ds(ch * rows, rows)
        return pltpu.make_async_remote_copy(
            src_ref=isend.at[dst, part],
            dst_ref=irecv.at[me, part],
            send_sem=a_send.at[ch, k - 1],
            recv_sem=a_recv.at[ch, k - 1],
            device_id={"gx": gx, "gy": gy, "dev": dst},
            device_id_type=MESH,
        )

    def a2a_in(ch, k):
        src = lax.rem(me + n_dev - k, n_dev)
        part = pl.ds(ch * rows, rows)
        return pltpu.make_async_remote_copy(
            src_ref=isend.at[src, part],
            dst_ref=irecv.at[src, part],
            send_sem=a_send.at[ch, k - 1],
            recv_sem=a_recv.at[ch, k - 1],
            device_id={"gx": gx, "gy": gy, "dev": src},
            device_id_type=MESH,
        )

    for ch in ORDER:
        ins[ch].wait()
        part = pl.ds(ch * rows, rows)
        for c in range(n_dev):
            total = None
            for a in range(2):
                lhs = dbuf[pl.ds(ch * per, per), a, :, pl.ds(256 * c, 256)].reshape(per * 16, 256)
                add = jnp.dot(lhs, wmat[a], preferred_element_type=F32)
                total = add if total is None else total + add
            pbuf[c, 0] = total[:, :128]
            pbuf[c, 1] = total[:, 128:]
            d = pbuf[c, 0, pl.ds(0, rows, stride=2), :] + pbuf[c, 1, pl.ds(1, rows, stride=2), :]
            dloc[c, part] = d
            isend[c, part] = (d * CODE + 0.5).astype(I32).astype(I16)
        if ch == ORDER[0]:
            pl.semaphore_wait(barrier, len(near))
        for k in (2, 1, 3):
            a2a(ch, k).start()
        irecv[me, part] = isend[me, part]
    for k in range(1, 4):
        pl.semaphore_signal(ready, inc=1, device_id=peer_y(k), device_id_type=MESH)

    def plane_of(i):
        return pl.ds(pl.multiple_of((i + 1) * ny, ny), ny)

    def xsend(e, side):
        where = plane_of(0 if side == 0 else nx - 1)
        if e == ST:
            return st.at[where]
        return rs.at[:, where] if e == RH else xq.at[side]

    xrecv = {ST: xr_st, RH: xr_r, QH: xr_q}
    ysend = {ST: ys_st, RH: ys_r, QH: ys_q}
    yrecv = {ST: yr_st, RH: yr_r, QH: yr_q}
    zsend = {ST: zs_st, RH: zs_r, QH: zs_q}
    zrecv = {ST: zr_st, RH: zr_r, QH: zr_q}
    spot = {"gx": (gx, n_gx), "gy": (gy, n_gy), "dev": (me, n_dev)}

    def face(e, axis, side):
        k = {"gx": 0, "gy": 2, "dev": 4}[axis] + side
        if axis == "gx":
            src, dst = xsend(e, side), xrecv[e].at[1 - side]
        elif axis == "gy":
            src, dst = ysend[e].at[side], yrecv[e].at[1 - side]
        else:
            src, dst = zsend[e], zrecv[e].at[1 - side]
        pos, size = spot[axis]
        target = {"gx": gx, "gy": gy, "dev": me}
        target[axis] = jnp.clip(pos - 1 if side == 0 else pos + 1, 0, size - 1)
        copy = pltpu.make_async_remote_copy(
            src_ref=src, dst_ref=dst, send_sem=h_send.at[e, k], recv_sem=h_recv.at[e, k],
            device_id=target, device_id_type=MESH,
        )
        sends = pos > 0 if side == 0 else pos < size - 1
        gets = pos < size - 1 if side == 0 else pos > 0
        return copy, sends, gets

    def start_face(e, axis, side):
        copy, sends, _ = face(e, axis, side)

        @pl.when(sends)
        def _():
            copy.start()

    def wait_face(e, axis, side):
        copy, _, gets = face(e, axis, side)

        @pl.when(gets)
        def _():
            copy.wait_recv()

    def end_face(e, axis, side):
        copy, sends, _ = face(e, axis, side)

        @pl.when(sends)
        def _():
            copy.wait_send()

    faces = [(axis, side) for axis in ("gx", "gy", "dev") for side in range(2)]

    iy = lax.broadcasted_iota(I32, (ny, nz), 0)
    iz = lax.broadcasted_iota(I32, (ny, nz), 1)
    first_y, last_y = iy == 0, iy == ny - 1
    first_z, last_z = iz == 0, iz == nz - 1
    ends_z = jnp.logical_or(first_z, last_z)
    key = ((iz + 1) // 2) % 64
    low_lane = lax.rem(iz, 2) == 0
    field0 = key < 32
    top8 = lax.broadcasted_iota(I32, (8, nz), 0) == 0
    end8 = lax.broadcasted_iota(I32, (8, nz), 0) == 7
    zero = jnp.zeros((ny, nz), F32)
    none = jnp.zeros((8, nz), F32)

    def fold(v):
        return jnp.sum(v.reshape(ny // 8, 8, nz), axis=0)

    def pack(into, v, f, i):
        return jnp.where(key == 32 * f + i, pltpu.roll(v, 64 * f + 2 * i, 1), into)

    def unpack(packed, f, i):
        by = 2 * nz - 64 * f - 2 * i
        by = by % nz if isinstance(i, int) else lax.rem(by, nz)
        return jnp.where(ends_z, pltpu.roll(packed, by, 1), 0.0)

    def add_rows(v, low, high):
        return jnp.concatenate(
            [v[:8] + jnp.where(top8, low, 0.0), v[8:-8], v[-8:] + jnp.where(end8, high, 0.0)], axis=0
        )

    def z_halo(ref):
        return jnp.where(low_lane, pltpu.roll(ref[0], 1, 1), pltpu.roll(ref[1], nz - 1, 1))

    for c in fields_in:
        c.wait()
    for ends in (pl.ds(0, ny), pl.ds((nx + 1) * ny, ny)):
        st[ends] = zero
        cy[ends] = zero
        for f in range(2):
            rs[f, ends] = zero
            qq[f, ends] = zero

    def load_plane(i, carry):
        zpack, m0r, m0s = carry
        im, om = ibuf[i].astype(F32), obuf[i].astype(F32)
        r, s = im * lbuf[i], om
        diag[i] = GROUND + fbuf[i].astype(F32) + PORT * (im + om)
        for f, v in enumerate((r, s)):
            rs[f, plane_of(i)] = v
            dzu[f, i] = v - pltpu.roll(v, nz - 1, 1)
            dzl[f, i] = v - pltpu.roll(v, 1, 1)
            ys_r[0, f, pl.ds(i, 1), :] = v[0:1]
            ys_r[1, f, pl.ds(i, 1), :] = v[ny - 1 : ny]
            zpack = pack(zpack, v, f, i)
        return zpack, m0r + fold(r * r), m0s + fold(s * s)

    zpack, m0r, m0s = lax.fori_loop(0, nx, load_plane, (zero, none, none), unroll=2)
    zs_r[...] = zpack
    pl.semaphore_wait(ready, 3)
    for axis, side in faces:
        start_face(RH, axis, side)

    def stiff_pair(p, zpack):
        d = [
            irecv[src, pl.ds(pl.multiple_of(16 * p, 16), 16)].astype(I32).astype(F32) * (1.0 / CODE)
            for src in range(n_dev)
        ]
        s = [FLOOR + (1.0 - FLOOR) * v * v * v for v in d]
        for h in range(2):
            i = 2 * p + h
            v = jnp.concatenate([t[8 * h : 8 * h + 8] for t in s], axis=0)
            st[plane_of(i)] = v
            ys_st[0, pl.ds(i, 1), :] = v[0:1]
            ys_st[1, pl.ds(i, 1), :] = v[ny - 1 : ny]
            zpack = pack(zpack, v, 0, i)
        return zpack

    zpack = zero
    for ch in ORDER:
        for k in (1, 3, 2):
            a2a_in(ch, k).wait_recv()
        zpack = lax.fori_loop(ch * per // 2, (ch + 1) * per // 2, stiff_pair, zpack, unroll=4)
        if ch == 0:
            start_face(ST, "gx", 0)
        if ch == CHUNKS - 1:
            start_face(ST, "gx", 1)
    zs_st[...] = jnp.where(field0, zpack, pltpu.roll(zpack, nz // 2, 1))
    for axis, side in faces[2:]:
        start_face(ST, axis, side)

    def inner_plane(i, carry):
        at = pl.multiple_of((i + 1) * ny, ny)
        here, after, up, down = pl.ds(at, ny), pl.ds(at + ny, ny), pl.ds(at + 1, ny), pl.ds(at - 1, ny)
        s = st[here]
        kx = between(s, st[after])
        kyu = between(s, jnp.where(last_y, 0.0, st[up]))
        kyl = between(s, jnp.where(first_y, 0.0, st[down]))
        kzu = between(s, jnp.where(last_z, 0.0, pltpu.roll(s, nz - 1, 1)))
        kzl = between(s, jnp.where(first_z, 0.0, pltpu.roll(s, 1, 1)))
        cx[i] = kx
        cy[here] = kyu
        czu[i] = kzu
        czl[i] = kzl
        dg = diag[i]
        new = []
        for f in range(2):
            v = rs[f, here]
            fx = kx * (v - rs[f, after])
            q = dg * v + (fx - carry[f])
            q += kyu * (v - rs[f, up]) + kyl * (v - rs[f, down])
            q += kzu * dzu[f, i] + kzl * dzl[f, i]
            qq[f, here] = q
            new.append(fx)
        return tuple(new)

    lax.fori_loop(0, nx, inner_plane, (zero, zero), unroll=2)

    for axis, side in faces:
        wait_face(RH, axis, side)
    for axis, side in faces[2:]:
        wait_face(ST, axis, side)

    kz = between(zs_st[...], z_halo(zr_st))
    zcon[...] = kz
    zhal[0] = zs_r[...] - z_halo(zr_r)
    zflux[...] = kz * zhal[0]
    for side in range(2):
        ycon[side] = between(ys_st[side], yr_st[side])
        for f in range(2):
            yflux[side, f] = ycon[side] * (ys_r[side, f] - yr_r[side, f])

    def with_edges(f, i):
        q = qq[f, plane_of(i)] + unpack(zflux[...], f, i)
        return add_rows(q, yflux[0, f, pl.ds(i, 1), :], yflux[1, f, pl.ds(i, 1), :])

    def finish(f, i, q, zpack, sums):
        qq[f, plane_of(i)] = q
        ys_q[0, f, pl.ds(i, 1), :] = q[0:1]
        ys_q[1, f, pl.ds(i, 1), :] = q[ny - 1 : ny]
        sums[f] += fold(rs[f, plane_of(i)] * q)
        sums[2 + f] += fold(q * q)
        return pack(zpack, q, f, i)

    def edge_plane(i, carry):
        zpack, sums = carry
        sums = list(sums)
        for f in range(2):
            zpack = finish(f, i, with_edges(f, i), zpack, sums)
        return zpack, tuple(sums)

    for side in range(2):
        for f in range(2):
            xq[side, f] = with_edges(f, 0 if side == 0 else nx - 1)
        start_face(QH, "gx", side)
    zpack, sums = lax.fori_loop(1, nx - 1, edge_plane, (zero, (none,) * 4), unroll=6)
    sums = list(sums)
    for side in range(2):
        wait_face(ST, "gx", side)
    for side in range(2):
        i = 0 if side == 0 else nx - 1
        xcon[side] = between(st[plane_of(i)], xr_st[side])
        for f in range(2):
            q = xq[side, f] + xcon[side] * (rs[f, plane_of(i)] - xr_r[side, f])
            zpack = finish(f, i, q, zpack, sums)
    sums12 = sums
    zs_q[...] = zpack
    for axis, side in faces[2:]:
        start_face(QH, axis, side)

    gprev[...] = jnp.zeros_like(gprev)
    forms = ((0, 1), (0, 3), (2, 1), (2, 3))

    def product_plane(i, carry):
        e_r, e_s = carry
        at = pl.multiple_of((i + 1) * ny, ny)
        here, after, up, down = pl.ds(at, ny), pl.ds(at + ny, ny), pl.ds(at + 1, ny), pl.ds(at - 1, ny)

        def get(where):
            return [rs[0, where], rs[1, where], qq[0, where], qq[1, where]]

        v = get(here)
        dg = diag[i]
        e_r += fold(dg * v[2] * v[2])
        e_s += fold(dg * v[3] * v[3])
        q_up = [pltpu.roll(v[f], nz - 1, 1) for f in (2, 3)]
        q_down = [pltpu.roll(v[f], 1, 1) for f in (2, 3)]

        def diffs(o):
            return [a - b for a, b in zip(v, o)]

        d = diffs(get(after))
        k = cx[i]
        t = [k * a for a in d]
        e_r += fold(t[2] * d[2])
        e_s += fold(t[3] * d[3])
        held = []
        for j, (a, b) in enumerate(forms):
            g = t[a] * t[b]
            held.append(g + gprev[j])
            gprev[j] = g
        sides = (
            (True, cy[here], lambda: diffs(get(up))),
            (False, cy[down], lambda: diffs(get(down))),
            (True, czu[i], lambda: [dzu[0, i], dzu[1, i], v[2] - q_up[0], v[3] - q_up[1]]),
            (False, czl[i], lambda: [dzl[0, i], dzl[1, i], v[2] - q_down[0], v[3] - q_down[1]]),
        )
        for own, k, make in sides:
            d = make()
            t = [k * a for a in d]
            if own:
                e_r += fold(t[2] * d[2])
                e_s += fold(t[3] * d[3])
            for j, (a, b) in enumerate(forms):
                held[j] += t[a] * t[b]
        for j in range(4):
            sarr[j, i] = held[j]
        return e_r, e_s

    e_r, e_s = lax.fori_loop(0, nx, product_plane, (none, none), unroll=2)

    row8 = lax.broadcasted_iota(I32, (8, nz), 0)
    lane8 = lax.broadcasted_iota(I32, (8, nz), 1)

    def to_lanes(first, values):
        tile = none
        for k, v in enumerate(values):
            tile = jnp.where(row8 == first + k, jnp.sum(v, axis=0, keepdims=True), tile)
        tile = jnp.where(row8 == lane8, jnp.sum(tile, axis=1, keepdims=True), 0.0)
        return jnp.sum(tile, axis=0, keepdims=True)

    early = to_lanes(0, (m0r, m0s) + tuple(sums12))

    for axis, side in faces:
        if side == 0:
            wait_face(QH, axis, side)
    for f in range(2):
        xr_q[1, f] += xcon[1] * (xr_r[1, f] - rs[f, plane_of(nx - 1)])

    dz = zs_q[...] - pltpu.roll(zr_q[1], nz - 1, 1)
    dz = zcon[...] * dz * dz
    parts = []
    for f in range(2):
        dx = qq[f, plane_of(nx - 1)] - xr_q[1, f]
        dy = ys_q[1, f] - yr_q[1, f]
        own = jnp.logical_and(jnp.logical_not(low_lane), field0 if f == 0 else jnp.logical_not(field0))
        parts.append(fold(xcon[1] * dx * dx + ycon[1] * dy * dy + jnp.where(own, dz, 0.0)))
    e_r += parts[0]
    e_s += parts[1]

    ar1[id1] = early + to_lanes(6, (e_r, e_s))

    def gather1(k):
        return pltpu.make_async_remote_copy(
            src_ref=ar1.at[id1], dst_ref=ar1.at[id1], send_sem=s_send.at[k], recv_sem=s_recv.at[k],
            device_id=peer1(k), device_id_type=MESH,
        )

    def gather1_in(k):
        src = lax.rem(id1 + 8 - k, 8)
        return pltpu.make_async_remote_copy(
            src_ref=ar1.at[src], dst_ref=ar1.at[src], send_sem=s_send.at[k], recv_sem=s_recv.at[k],
            device_id=peer1(8 - k), device_id_type=MESH,
        )

    def gather2(k):
        return pltpu.make_async_remote_copy(
            src_ref=ar2.at[id2], dst_ref=ar2.at[id2], send_sem=t_send.at[k], recv_sem=t_recv.at[k],
            device_id=peer2(k), device_id_type=MESH,
        )

    def gather2_in(k):
        src = lax.rem(id2 + 16 - k, 16)
        return pltpu.make_async_remote_copy(
            src_ref=ar2.at[src], dst_ref=ar2.at[src], send_sem=t_send.at[k], recv_sem=t_recv.at[k],
            device_id=peer2(16 - k), device_id_type=MESH,
        )

    for k in (4, 5, 3, 2, 6, 7, 1):
        gather1(k).start()

    col_k = lax.rem(row_i, 128)
    paired = col_i // 2 == col_k
    even = lax.rem(col_i, 2) == 0
    for ab in range(4):
        e = jnp.where(even, kid[2 * ab], kid[2 * ab + 1])
        wout[ab] = jnp.where(paired, e, 0.0).astype(BF16)

    for axis, side in faces:
        if side == 1:
            wait_face(QH, axis, side)
    for f in range(2):
        xr_q[0, f] += xcon[0] * (xr_r[0, f] - rs[f, plane_of(0)])
    zhal[1] = zs_q[...] - z_halo(zr_q)
    for side in range(2):
        edge = plane_of(0 if side == 0 else nx - 1)
        k = xcon[side]
        d = [k * (rs[f, edge] - xr_r[side, f]) for f in range(2)]
        d += [k * (qq[f, edge] - xr_q[side, f]) for f in range(2)]
        for j, (a, b) in enumerate(forms):
            sarr[j, 0 if side == 0 else nx - 1] += d[a] * d[b]
        k = ycon[side]
        d = [k * (ys_r[side, f] - yr_r[side, f]) for f in range(2)]
        d += [k * (ys_q[side, f] - yr_q[side, f]) for f in range(2)]
        for j, (a, b) in enumerate(forms):
            ysb[side, j] = d[a] * d[b]
    dr, dq = zcon[...] * zhal[0], zcon[...] * zhal[1]
    dr2, dq2 = pltpu.roll(dr, nz // 2, 1), pltpu.roll(dq, nz // 2, 1)
    zsb[0] = jnp.where(field0, dr * dr2, dq * dq2)
    zsb[1] = dr * dq2
    packed_at = ((0, 0), (1, 0), (1, 1), (0, 1))

    def scale_plane(i, carry):
        s = st[plane_of(i)]
        scale = 1.0 / (s * s)
        for j in range(4):
            buf, f = packed_at[j]
            g = sarr[j, i] + unpack(zsb[buf], f, i)
            g = add_rows(g, ysb[0, j, pl.ds(i, 1), :], ysb[1, j, pl.ds(i, 1), :])
            sarr[j, i] = scale * g
        return carry

    lax.fori_loop(0, nx // 2, scale_plane, 0, unroll=4)

    for k in range(1, 8):
        gather1_in(k).wait_recv()
    part = ar1[0]
    for k in range(1, 8):
        part = part + ar1[k]
    ar2[id2] = part
    for k in (12, 4, 13, 11, 5, 3, 8, 10, 14, 6, 2, 9, 7, 1, 15):
        gather2(k).start()

    lax.fori_loop(nx // 2, nx, scale_plane, 0, unroll=4)

    for ch in range(CHUNKS):
        for k in range(1, 4):
            a2a(ch, k).wait_send()
    for e in (ST, RH, QH):
        for axis, side in faces:
            end_face(e, axis, side)
    for k in range(1, 8):
        gather1(k).wait_send()

    for k in range(1, 16):
        gather2_in(k).wait_recv()
    whole = ar2[0]
    for k in range(1, 16):
        whole = whole + ar2[k]

    whole = jnp.where(row8 == lane8, whole, 0.0)
    coef[...] = jnp.broadcast_to(jnp.sum(whole, axis=1, keepdims=True), coef.shape)
    m0, m1, m2, m3 = (coef[pl.ds(2 * k, 2), :] for k in range(4))
    step0 = m0 / (m1 + TINY)
    rr1 = jnp.maximum(m0 - 2.0 * step0 * m1 + step0 * step0 * m2, 0.0)
    beta = rr1 / (m0 + TINY)
    r_a_r = m1 - 2.0 * step0 * m2 + step0 * step0 * m3
    r_a_d = m1 - step0 * m2
    d_a_d = r_a_r + 2.0 * beta * r_a_d + beta * beta * m1
    step1 = jnp.minimum(rr1 / (jnp.maximum(d_a_d, 0.0) + TINY), MAX_STEP)
    c0 = step0 + step1 * (1.0 + beta)
    c1 = -step0 * step1
    mix = [c0[0:1] * c0[1:2], c0[0:1] * c1[1:2], c1[0:1] * c0[1:2], c1[0:1] * c1[1:2]]

    def back(ch, k):
        dst = lax.rem(me + k, n_dev)
        part = pl.ds(ch * nx * 8 // BACKS, nx * 8 // BACKS)
        return pltpu.make_async_remote_copy(
            src_ref=bsend.at[dst, part],
            dst_ref=out.at[me, part],
            send_sem=b_send.at[ch, k - 1],
            recv_sem=b_recv.at[ch, k - 1],
            device_id={"gx": gx, "gy": gy, "dev": dst},
            device_id_type=MESH,
        )

    def back_in(ch, k):
        src = lax.rem(me + n_dev - k, n_dev)
        part = pl.ds(ch * nx * 8 // BACKS, nx * 8 // BACKS)
        return pltpu.make_async_remote_copy(
            src_ref=bsend.at[src, part],
            dst_ref=out.at[src, part],
            send_sem=b_send.at[ch, k - 1],
            recv_sem=b_recv.at[ch, k - 1],
            device_id={"gx": gx, "gy": gy, "dev": src},
            device_id_type=MESH,
        )

    def combine(into, slot, group):
        lines = pl.ds(pl.multiple_of(8 * group, 8), 8)

        def pair_planes(p, carry):
            v = None
            for j in range(4):
                add = mix[j] * sarr[j, pl.ds(2 * p, 2), lines]
                v = add if v is None else v + add
            into[slot, pl.ds(pl.multiple_of(p * 16, 16), 16)] = v.reshape(16, nz).astype(BF16)
            return carry

        lax.fori_loop(0, nx // 2, pair_planes, 0, unroll=8)

    for k in (2, 1, 3):
        dst = lax.rem(me + k, n_dev)
        combine(bsend, dst, dst)
        back(0, k).start()
    combine(out, me, me)
    for k in range(1, 16):
        gather2(k).wait_send()
    for ch in range(BACKS):
        for k in (2, 1, 3):
            back(ch, k).wait_send()
            back_in(ch, k).wait_recv()


def expand_kernel(s_ref, d_ref, w_ref, o_hbm, obuf, o_sem):
    n_dev, rows, nz = s_ref.shape
    nx = rows // 8
    per = nx // STEPS

    def store(c, l):
        return pltpu.make_async_copy(
            obuf.at[l, pl.ds(c * 2 * per, 2 * per)],
            o_hbm.at[pl.ds(c * 2 * per, 2 * per), :, pl.ds(128 * l, 128)],
            o_sem.at[c, l],
        )

    for c in range(STEPS):
        part = pl.ds(c * per * 8, per * 8)
        for d in range(n_dev):
            dens = d_ref[d, part]
            v = (-1.5 * (1.0 - FLOOR) * GAIN) * dens * dens * s_ref[d, part].astype(F32)
            high = v.astype(BF16)
            low = (v - high.astype(F32)).astype(BF16)
            lhs = jnp.concatenate([high, low], axis=1)
            for a in range(2):
                for b in range(2):
                    t = jnp.dot(lhs, w_ref[2 * a + b], preferred_element_type=F32)
                    for i in range(per):
                        for h in range(2):
                            obuf[2 * d + h, 2 * (c * per + i) + a, pl.ds(b, 8, stride=2), :] = t[
                                8 * i : 8 * i + 8, 128 * h : 128 * h + 128
                            ]
            for h in range(2):
                store(c, 2 * d + h).start()
    for c in range(STEPS):
        for l in range(2 * n_dev):
            store(c, l).wait()


def solution(mesh):
    n_gx, n_gy, n_dev = mesh.shape["gx"], mesh.shape["gy"], mesh.shape["dev"]

    def body(design, tap_offsets, tap_weights, input_load, input_mask, output_mask, fixed_mask):
        nx, ny, nz = input_load.shape
        cell = (nx, ny, nz)
        plane = (ny, nz)
        padded = ((nx + 2) * ny, nz)
        hbm = pl.BlockSpec(memory_space=pl.ANY)
        vmem = pl.BlockSpec(memory_space=pltpu.VMEM)
        vm = lambda *shape: pltpu.VMEM(shape, F32)
        dma = lambda *shape: pltpu.SemaphoreType.DMA(shape)
        taps = [pltpu.SMEM((3, 16), I32), pltpu.SMEM((16,), F32)]
        scratch = [
            pltpu.VMEM((nx, 2, 16, 1024), BF16),
            vm(*cell), pltpu.VMEM(cell, I32), pltpu.VMEM(cell, I32), pltpu.VMEM(cell, I32),
            pltpu.VMEM((2, 256, 256), BF16),
            vm(n_dev, 2, nx // CHUNKS * 16, 128),
            pltpu.VMEM((n_dev, nx * 8, nz), I16),
            pltpu.VMEM((n_dev, nx * 8, nz), I16),
            vm(*padded), vm(2, *padded), vm(2, *padded),
            vm(*cell), vm(2, *cell), vm(2, *cell),
            vm(*cell), vm(*padded), vm(*cell), vm(*cell),
            vm(4, *cell),
            vm(4, *plane),
            vm(2, *plane), vm(2, 2, *plane), vm(2, 2, *plane),
            vm(2, nx, nz), vm(2, 2, nx, nz), vm(2, 2, nx, nz),
            vm(2, nx, nz), vm(2, 2, nx, nz), vm(2, 2, nx, nz),
            vm(*plane), vm(*plane), vm(*plane),
            vm(2, *plane), vm(2, *plane), vm(2, *plane),
            vm(2, 2, nx, nz), vm(*plane), vm(*plane), vm(2, nx, nz), vm(2, *plane), vm(2, *plane),
            vm(2, 4, nx, nz), vm(2, *plane),
            vm(8, 1, 128), vm(16, 1, 128), vm(8, 128),
            pltpu.VMEM((n_dev, nx * 8, nz), BF16),
            vm(2, 2, *plane),
            *taps, dma(2),
            dma(CHUNKS + 4), dma(CHUNKS, 3), dma(CHUNKS, 3), dma(3, 6), dma(3, 6),
            dma(8), dma(8), dma(16), dma(16), dma(BACKS, 3), dma(BACKS, 3),
            pltpu.SemaphoreType.REGULAR,
        ]
        returned, local, fold = pl.pallas_call(
            functools.partial(step_kernel, n_gx, n_gy, n_dev),
            out_shape=(
                jax.ShapeDtypeStruct((n_dev, nx * 8, nz), BF16),
                jax.ShapeDtypeStruct((n_dev, nx * 8, nz), F32),
                jax.ShapeDtypeStruct((4, 256, 256), BF16),
            ),
            in_specs=[hbm] * 7,
            out_specs=(vmem, vmem, vmem),
            scratch_shapes=scratch,
            compiler_params=pltpu.CompilerParams(
                collective_id=0, has_side_effects=True, vmem_limit_bytes=40000 * 1024
            ),
            name="step",
        )(
            *(
                pltpu.with_memory_space_constraint(v, pltpu.HBM)
                for v in (
                    design.reshape(nx, 2, 16, 1024), input_load, input_mask, output_mask, fixed_mask,
                    tap_offsets.T, tap_weights,
                )
            )
        )
        return pl.pallas_call(
            expand_kernel,
            out_shape=jax.ShapeDtypeStruct(design.shape, F32),
            in_specs=[vmem] * 3,
            out_specs=hbm,
            scratch_shapes=[vm(2 * n_dev, 2 * nx, 16, 128), dma(STEPS, 2 * n_dev)],
            compiler_params=pltpu.CompilerParams(vmem_limit_bytes=32 * 1024 * 1024),
            name="expand",
        )(returned, local, fold)

    block = P("gx", "gy", "dev")
    owner = P("gx", ("gy", "dev"), None)
    return jax.shard_map(
        body, mesh=mesh,
        in_specs=(owner, P(), P(), block, block, block, block),
        out_specs=owner,
        check_vma=False,
    )
```
